32 devices in a mesh: groups: 2 (over y), wide: 4 (over z), heads: 4 (over x, core).
Axes of the slice: x: 2, y: 2, z: 4, core: 2. Of those that a mesh axis runs over, the one named last changes fastest.
Arguments:
- video_hidden: bfloat16 [2048, 4096], P(('groups', 'wide'), 'heads'), parts along dimension 0, may hold values from -6 to 6
- audio_hidden: bfloat16 [512, 2048], P(('groups', 'wide'), 'heads'), parts along dimension 0, may hold values from -6 to 6
- video_query: bfloat16 [2048, 2048], P(('groups', 'wide'), 'heads'), parts along dimension 0, may hold values from -8 to 8
- video_key: bfloat16 [2048, 2048], P(('groups', 'wide'), 'heads'), parts along dimension 0, may hold values from -8 to 8
- video_value: bfloat16 [2048, 2048], P(('groups', 'wide'), 'heads'), parts along dimension 0, may hold values from -6 to 6
- audio_query: bfloat16 [512, 1024], P(('groups', 'wide'), 'heads'), parts along dimension 0, may hold values from -8 to 8
- audio_key: bfloat16 [512, 1024], P(('groups', 'wide'), 'heads'), parts along dimension 0, may hold values from -8 to 8
- audio_value: bfloat16 [512, 1024], P(('groups', 'wide'), 'heads'), parts along dimension 0, may hold values from -6 to 6
- cross_video_query: bfloat16 [2048, 1024], P(('groups', 'wide'), 'heads'), parts along dimension 0, may hold values from -8 to 8
- cross_audio_key: bfloat16 [512, 1024], P(('groups', 'wide'), 'heads'), parts along dimension 0, may hold values from -8 to 8
- cross_audio_value: bfloat16 [512, 1024], P(('groups', 'wide'), 'heads'), parts along dimension 0, may hold values from -6 to 6
- cross_audio_query: bfloat16 [512, 1024], P(('groups', 'wide'), 'heads'), parts along dimension 0, may hold values from -8 to 8
- cross_video_key: bfloat16 [2048, 1024], P(('groups', 'wide'), 'heads'), parts along dimension 0, may hold values from -8 to 8
- cross_video_value: bfloat16 [2048, 1024], P(('groups', 'wide'), 'heads'), parts along dimension 0, may hold values from -6 to 6
- video_self_out: bfloat16 [2048, 4096], P('heads', 'wide'), may hold values from -0.125 to 0.125
- video_cross_out: bfloat16 [1024, 4096], P('heads', 'wide'), may hold values from -0.1875 to 0.1875
- audio_self_out: bfloat16 [1024, 2048], P('heads', 'wide'), may hold values from -0.1875 to 0.1875
- audio_cross_out: bfloat16 [1024, 2048], P('heads', 'wide'), may hold values from -0.1875 to 0.1875
- intersection: int32 [8, 5], P('groups'), parts along dimension 0, may hold values from 0 to 1, as said below
Outputs:
- video_out: bfloat16 [2048, 4096], P(('groups', 'wide'), 'heads'), parts along dimension 0
- audio_out: bfloat16 [512, 2048], P(('groups', 'wide'), 'heads'), parts along dimension 0
The draws below stay inside these ranges and needn't reach their ends.
There are 2 independent parts, one for each index of `groups`. The reference program is written for one: setup_inputs(seed, part) draws one part's arguments, and reference() takes and returns one part's arrays. A program takes and returns all parts, laid end to end along the dimension named above; an argument that names none is the same for every part. Nothing has to cross between parts.
Inputs may be any that keep to these rules, and one draw needn't show every extreme that they name: `intersection`: column 2 is 1 in every row; entries that would pair a block with one outside the clip are ignored.
All inputs are finite; a program needn't handle non-finite values.
Results may differ from the reference program's by a relative error of at most 0.012.
Values may be sent and summed in bfloat16 or wider, within the bound.
A program may use at most 64 MiB of HBM per device.

```python
import math
import jax
import jax.numpy as jnp
from jax import lax

DV = 4096
DA = 2048
HDV = 128
HDA = 64
HEADS = 16
REACH = 2
TV_DEV = 256
TA_DEV = 64
SPAN = 5
BLOCKS = 4
NV = 1024
NA = 256
N_HEADS = 4


def attention_pair(base_key, query_count, key_count, head_size):
    split_keys = jax.random.split(base_key, 2)
    queries = jnp.clip(3.0 * jax.random.normal(split_keys[0], (query_count, HEADS * head_size), jnp.float32), -8.0, 8.0)
    key_rows = jnp.clip(jax.random.normal(split_keys[1], (key_count, HEADS * head_size), jnp.float32), -4.0, 4.0)
    return (queries, key_rows)


def draw_video_query(key, part):
    return attention_pair(jax.random.fold_in(key, 11), NV, NV, HDV)[0].astype(jnp.bfloat16)


def draw_video_key(key, part):
    return attention_pair(jax.random.fold_in(key, 11), NV, NV, HDV)[1].astype(jnp.bfloat16)


def draw_audio_query(key, part):
    return attention_pair(jax.random.fold_in(key, 12), NA, NA, HDA)[0].astype(jnp.bfloat16)


def draw_audio_key(key, part):
    return attention_pair(jax.random.fold_in(key, 12), NA, NA, HDA)[1].astype(jnp.bfloat16)


def draw_cross_video_query(key, part):
    return attention_pair(jax.random.fold_in(key, 13), NV, NA, HDA)[0].astype(jnp.bfloat16)


def draw_cross_audio_key(key, part):
    return attention_pair(jax.random.fold_in(key, 13), NV, NA, HDA)[1].astype(jnp.bfloat16)


def draw_cross_audio_query(key, part):
    return attention_pair(jax.random.fold_in(key, 14), NA, NV, HDA)[0].astype(jnp.bfloat16)


def draw_cross_video_key(key, part):
    return attention_pair(jax.random.fold_in(key, 14), NA, NV, HDA)[1].astype(jnp.bfloat16)


def draw_intersection(key, part):
    level_key, rolled_key = jax.random.split(jax.random.fold_in(key, 15))
    levels = jax.random.randint(level_key, (BLOCKS, 1), 1, 5)
    rolled = jax.random.randint(rolled_key, (BLOCKS, SPAN), 0, 5)
    intersection_table = (rolled < levels).astype(jnp.int32)
    column = jnp.arange(SPAN, dtype=jnp.int32)
    return jnp.where(column[None, :] == REACH, 1, intersection_table).astype(jnp.int32)


def steps_of(stream_key, extent, cuts, least, top_value):
    gain = 1.0
    for dim, shards_of in cuts:
        draws = jax.random.uniform(jax.random.fold_in(jax.random.fold_in(stream_key, 6), dim), (shards_of,), jnp.float32, least / len(cuts), top_value / len(cuts))
        gain = gain * jnp.repeat(jnp.exp(draws), extent[dim] // shards_of).reshape((-1,) + (1,) * (len(extent) - 1 - dim))
    return gain


def noise(key, shape, spread, bound, cuts=(), held_as=jnp.bfloat16):
    values = spread * jax.random.normal(key, shape, jnp.float32)
    if cuts:
        values = values * steps_of(key, shape, cuts, -0.22, 0.18)
    return jnp.clip(values, -bound, bound).astype(held_as)


def setup_inputs(seed: int = 0, part: int = 0) -> dict:
    splits = jax.random.split(jax.random.key(seed), 20)
    part_keys = jax.random.split(jax.random.fold_in(splits[19], part), 20)
    return {
        "video_hidden": noise(part_keys[0], (NV, DV), 1.0, 6.0, ((0, 4), (1, 4))),
        "audio_hidden": noise(part_keys[1], (NA, DA), 1.0, 6.0, ((0, 4), (1, 4))),
        "video_query": draw_video_query(jax.random.fold_in(jax.random.fold_in(splits[19], part), 71), part),
        "video_key": draw_video_key(jax.random.fold_in(jax.random.fold_in(splits[19], part), 71), part),
        "video_value": noise(part_keys[4], (NV, HEADS * HDV), 1.0, 6.0, ((0, 4), (1, 4))),
        "audio_query": draw_audio_query(jax.random.fold_in(jax.random.fold_in(splits[19], part), 71), part),
        "audio_key": draw_audio_key(jax.random.fold_in(jax.random.fold_in(splits[19], part), 71), part),
        "audio_value": noise(part_keys[7], (NA, HEADS * HDA), 1.0, 6.0, ((0, 4), (1, 4))),
        "cross_video_query": draw_cross_video_query(jax.random.fold_in(jax.random.fold_in(splits[19], part), 71), part),
        "cross_audio_key": draw_cross_audio_key(jax.random.fold_in(jax.random.fold_in(splits[19], part), 71), part),
        "cross_audio_value": noise(part_keys[10], (NA, HEADS * HDA), 1.0, 6.0, ((0, 4), (1, 4))),
        "cross_audio_query": draw_cross_audio_query(jax.random.fold_in(jax.random.fold_in(splits[19], part), 71), part),
        "cross_video_key": draw_cross_video_key(jax.random.fold_in(jax.random.fold_in(splits[19], part), 71), part),
        "cross_video_value": noise(part_keys[13], (NV, HEADS * HDA), 1.0, 6.0, ((0, 4), (1, 4))),
        "video_self_out": noise(splits[14], (HEADS * HDV, DV), (HEADS * HDV) ** -0.5, 0.125, ((0, 4), (1, 4))),
        "video_cross_out": noise(splits[15], (HEADS * HDA, DV), (HEADS * HDA) ** -0.5, 0.1875, ((0, 4), (1, 4))),
        "audio_self_out": noise(splits[16], (HEADS * HDA, DA), (HEADS * HDA) ** -0.5, 0.1875, ((0, 4), (1, 4))),
        "audio_cross_out": noise(splits[17], (HEADS * HDA, DA), (HEADS * HDA) ** -0.5, 0.1875, ((0, 4), (1, 4))),
        "intersection": draw_intersection(jax.random.fold_in(jax.random.fold_in(splits[19], part), 71), part),
    }


def attend(queries, key_rows, value_rows, head_size, allowed):
    row_count = queries.shape[0]
    query_heads = queries.reshape(row_count, HEADS, head_size).transpose(1, 0, 2)
    key_heads = key_rows.reshape(key_rows.shape[0], HEADS, head_size).transpose(1, 0, 2)
    value_heads = value_rows.reshape(value_rows.shape[0], HEADS, head_size).transpose(1, 0, 2)

    def one_head(operands):
        query_one, key_one, value_one = operands
        scores = jnp.dot(query_one, key_one.T, preferred_element_type=jnp.float32) * (1.0 / math.sqrt(head_size))
        if allowed is not None:
            scores = jnp.where(allowed, scores, -1e+30)
        maximum = lax.optimization_barrier(jnp.max(scores, axis=1, keepdims=True))
        weights = jnp.exp(scores - maximum)
        if allowed is not None:
            weights = jnp.where(allowed, weights, 0.0)
        totals = lax.optimization_barrier(jnp.sum(weights, axis=1, keepdims=True))
        mixed = jnp.dot(weights.astype(jnp.bfloat16), value_one, preferred_element_type=jnp.float32)
        return (mixed / totals).astype(jnp.bfloat16)
    result = lax.map(one_head, (query_heads, key_heads, value_heads))
    return result.transpose(1, 0, 2).reshape(row_count, HEADS * head_size)

def cross_mask(intersection):
    video_blocks = jnp.arange(NV, dtype=jnp.int32) // TV_DEV
    audio_blocks = jnp.arange(NA, dtype=jnp.int32) // TA_DEV
    offsets = audio_blocks[None, :] - video_blocks[:, None] + REACH
    inside = (offsets >= 0) & (offsets < SPAN)
    picked = intersection[video_blocks[:, None], jnp.clip(offsets, 0, SPAN - 1)]
    return inside & (picked > 0)

def project(self_part, cross_part, self_weight, cross_weight, self_size, cross_size, hidden):
    per_group = HEADS // N_HEADS
    total = hidden.astype(jnp.float32)
    for head_group in range(N_HEADS):
        self_cols = self_part[:, head_group * per_group * self_size:(head_group + 1) * per_group * self_size]
        cross_cols = cross_part[:, head_group * per_group * cross_size:(head_group + 1) * per_group * cross_size]
        self_rows = self_weight[head_group * per_group * self_size:(head_group + 1) * per_group * self_size]
        cross_rows = cross_weight[head_group * per_group * cross_size:(head_group + 1) * per_group * cross_size]
        partial_value = jnp.dot(self_cols, self_rows, preferred_element_type=jnp.float32) + jnp.dot(cross_cols, cross_rows, preferred_element_type=jnp.float32)
        total = total + lax.optimization_barrier(partial_value.astype(jnp.bfloat16)).astype(jnp.float32)
    return total.astype(jnp.bfloat16)

def reference(video_hidden, audio_hidden, video_query, video_key, video_value, audio_query, audio_key, audio_value, cross_video_query, cross_audio_key, cross_audio_value, cross_audio_query, cross_video_key, cross_video_value, video_self_out, video_cross_out, audio_self_out, audio_cross_out, intersection):
    video_self = attend(video_query, video_key, video_value, HDV, None)
    audio_self = attend(audio_query, audio_key, audio_value, HDA, None)
    allowed = cross_mask(intersection)
    video_cross = attend(cross_video_query, cross_audio_key, cross_audio_value, HDA, allowed)
    audio_cross = attend(cross_audio_query, cross_video_key, cross_video_value, HDA, allowed.T)
    video_out = project(video_self, video_cross, video_self_out, video_cross_out, HDV, HDA, video_hidden)
    audio_out = project(audio_self, audio_cross, audio_self_out, audio_cross_out, HDA, HDA, audio_hidden)
    return (video_out, audio_out)
```

```python
import contextlib
import functools
import math

import jax
import jax.numpy as jnp
from jax import lax
from jax.experimental import pallas as pl
from jax.experimental.pallas import tpu as pltpu
from jax.sharding import PartitionSpec as P

HDV = 128
HDA = 64
REACH = 2


def passed_along(value, axis, by):
    length = lax.axis_size(axis)
    pairs = [(i, i + by) for i in range(length) if 0 <= i + by < length]
    return lax.ppermute(value, axis, pairs)


def empty_state(row_count, head_count, head_size):
    return (
        jnp.full((head_count, row_count), -1e30, jnp.float32),
        jnp.zeros((head_count, row_count), jnp.float32),
        jnp.zeros((head_count, row_count, head_size), jnp.float32),
    )


def absorb(state, queries, key_rows, value_rows, head_size, allowed):
    maxima, totals, running = state
    head_count = queries.shape[1] // head_size
    query_heads = queries.reshape(queries.shape[0], head_count, head_size)
    key_heads = key_rows.reshape(key_rows.shape[0], head_count, head_size)
    value_heads = value_rows.reshape(value_rows.shape[0], head_count, head_size)
    scores = jnp.einsum(
        "qhd,khd->hqk", query_heads, key_heads, preferred_element_type=jnp.float32
    ) * (1.0 / math.sqrt(head_size))
    if allowed is not None:
        scores = jnp.where(allowed[None, None, :], scores, -1e30)
    new_peak = jnp.maximum(maxima, jnp.max(scores, axis=2))
    weights = jnp.exp(scores - new_peak[:, :, None])
    if allowed is not None:
        weights = jnp.where(allowed[None, None, :], weights, 0.0)
    rescale = jnp.exp(maxima - new_peak)
    totals = totals * rescale + jnp.sum(weights, axis=2)
    running = running * rescale[:, :, None] + jnp.einsum(
        "hqk,khd->hqd",
        weights.astype(jnp.bfloat16),
        value_heads,
        preferred_element_type=jnp.float32,
    )
    return (new_peak, totals, running)


def finish(state, head_size):
    maxima, totals, running = state
    result = running / totals[:, :, None]
    return (
        result.transpose(1, 0, 2)
        .reshape(result.shape[1], result.shape[0] * head_size)
        .astype(jnp.bfloat16)
    )


def permitted(key_blocks, position, table_row, wide_count):
    offsets = key_blocks - position + REACH
    matches = (offsets[:, None] == jnp.arange(2 * REACH + 1, dtype=jnp.int32)[None, :]) & (
        table_row[None, :] > 0
    )
    inside = (key_blocks >= 0) & (key_blocks < wide_count)
    return jnp.any(matches, axis=1) & inside


def general_shards(
    video_hidden,
    audio_hidden,
    video_query,
    video_key,
    video_value,
    audio_query,
    audio_key,
    audio_value,
    cross_video_query,
    cross_audio_key,
    cross_audio_value,
    cross_audio_query,
    cross_video_key,
    cross_video_value,
    video_self_out,
    video_cross_out,
    audio_self_out,
    audio_cross_out,
    intersection,
):
    position = lax.axis_index("wide")
    wide_count = lax.axis_size("wide")
    video_count = video_query.shape[0]
    audio_count = audio_query.shape[0]
    head_count = video_query.shape[1] // HDV
    video_start = empty_state(video_count, head_count, HDV)
    audio_start = empty_state(audio_count, head_count, HDA)
    carried = (video_start, audio_start)
    portion = (
        lax.all_gather(video_key, "wide", axis=0, tiled=True),
        lax.all_gather(video_value, "wide", axis=0, tiled=True),
        lax.all_gather(audio_key, "wide", axis=0, tiled=True),
        lax.all_gather(audio_value, "wide", axis=0, tiled=True),
    )
    video_state = absorb(carried[0], video_query, portion[0], portion[1], HDV, None)
    audio_state = absorb(carried[1], audio_query, portion[2], portion[3], HDA, None)
    table_row = lax.dynamic_slice_in_dim(intersection, position, 1, 0)[0]
    padded_table = jnp.pad(intersection, ((REACH, REACH), (0, 0)))
    flag_row = jnp.diagonal(
        jnp.fliplr(lax.dynamic_slice_in_dim(padded_table, position, 2 * REACH + 1, 0))
    )
    stacked = jnp.concatenate(
        [cross_audio_key, cross_audio_value, cross_video_key, cross_video_value], 0
    )

    def take_cross(carried, portion, block):
        audio_keys = portion[:audio_count]
        audio_values = portion[audio_count : 2 * audio_count]
        video_keys = portion[2 * audio_count : 2 * audio_count + video_count]
        video_values = portion[2 * audio_count + video_count :]
        audio_blocks = jnp.full((audio_count,), block, jnp.int32)
        video_blocks = jnp.full((video_count,), block, jnp.int32)
        return (
            absorb(
                carried[0],
                cross_video_query,
                audio_keys,
                audio_values,
                HDA,
                permitted(audio_blocks, position, table_row, wide_count),
            ),
            absorb(
                carried[1],
                cross_audio_query,
                video_keys,
                video_values,
                HDA,
                permitted(video_blocks, position, flag_row, wide_count),
            ),
        )

    cross_start = (
        empty_state(video_count, head_count, HDA),
        empty_state(audio_count, head_count, HDA),
    )
    carried = take_cross(cross_start, stacked, position)
    for offset in range(-REACH, REACH + 1):
        if offset != 0:
            nearby = passed_along(stacked, "wide", -offset)
            carried = take_cross(carried, nearby, position + offset)
    to_video, to_audio = carried
    video_joined = jnp.concatenate([finish(video_state, HDV), finish(to_video, HDA)], 1)
    audio_joined = jnp.concatenate([finish(audio_state, HDA), finish(to_audio, HDA)], 1)
    video_weights = jnp.concatenate([video_self_out, video_cross_out], 0)
    audio_weights = jnp.concatenate([audio_self_out, audio_cross_out], 0)
    video_terms = jnp.dot(
        video_joined,
        lax.all_gather(video_weights, "wide", axis=1, tiled=True),
        preferred_element_type=jnp.float32,
    )
    audio_terms = jnp.dot(
        audio_joined,
        lax.all_gather(audio_weights, "wide", axis=1, tiled=True),
        preferred_element_type=jnp.float32,
    )
    video_sum, audio_sum = (
        lax.psum_scatter(
            video_terms.astype(jnp.bfloat16), "heads", scatter_dimension=1, tiled=True
        ).astype(jnp.float32),
        lax.psum_scatter(
            audio_terms.astype(jnp.bfloat16), "heads", scatter_dimension=1, tiled=True
        ).astype(jnp.float32),
    )
    video_out = (video_hidden.astype(jnp.float32) + video_sum).astype(jnp.bfloat16)
    audio_out = (audio_hidden.astype(jnp.float32) + audio_sum).astype(jnp.bfloat16)
    return (video_out, audio_out)


NT = (((1,), (1,)), ((), ()))
MESH = pl.DeviceIdType.MESH


def scope(name):
    return contextlib.nullcontext()


def softmax(scores, head_size):
    factor = math.log2(math.e) / math.sqrt(head_size)
    weights = jnp.exp2((scores - jnp.max(scores, axis=1, keepdims=True)) * factor)
    return weights.astype(jnp.bfloat16), jnp.sum(weights, axis=1, keepdims=True)


def scored(queries, keys):
    return lax.dot_general(queries, keys, NT, preferred_element_type=jnp.float32)


def mixed(weights, values):
    return jnp.dot(weights, values, preferred_element_type=jnp.float32)


def joint_kernel(
    n,
    vq, vk, vv, cvq, cvk, cvv, aq, ak, av, caq, cak, cav, ws, wc, aso, aco, table,
    out_v, out_a,
    q_all, k_all, v_all, wide_stage, few_stage, pack, p_all, ws_all, wc_all, wa_all,
    tall_bias, wide_bias, o_self, o_rest, r_self, r_rest, totals, sum_v, sum_a, mid_v, mid_a,
    a_send, a_recv, w_send, w_recv, f_send, f_recv, x_send, x_recv, z_send, z_recv, r_send,
    d_send, d_recv, e_send, e_recv, local,
):
    w = lax.axis_index("wide")
    h = lax.axis_index("heads")
    rows, few = vq.shape[0], aq.shape[0]
    half = rows // 2
    part_rows, part_few = rows // n, few // n
    depth = p_all.shape[1]
    bf16 = jnp.bfloat16

    def place(dw, dh):
        return {"wide": lax.rem(w + dw, n), "heads": lax.rem(h + dh, n)}

    def remote(source, target, send, recv, device):
        return pltpu.make_async_remote_copy(
            src_ref=source, dst_ref=target, send_sem=send, recv_sem=recv,
            device_id=device, device_id_type=MESH,
        )

    others = [(d, 0) for d in range(1, n)] + [(0, d) for d in range(1, n)]
    barrier = pltpu.get_barrier_semaphore()
    for dw, dh in others:
        pl.semaphore_signal(barrier, inc=1, device_id=place(dw, dh), device_id_type=MESH)

    def head_cols(ref, who):
        return ref.at[:, pl.ds(pl.multiple_of(who * HDV, HDV), HDV)]

    def start(copies):
        for copy in copies:
            copy.start()
        return copies

    staged = start(
        [
            pltpu.make_async_copy(source, wide_stage.at[i], local.at[i])
            for i, source in enumerate((cvq, cvk, cvv))
        ]
        + [
            pltpu.make_async_copy(source, few_stage.at[i], local.at[3 + i])
            for i, source in enumerate((cak, caq, av, aq, cav, ak))
        ]
    )
    own = start(
        [
            pltpu.make_async_copy(head_cols(source, w), target.at[w], local.at[9 + i])
            for i, (source, target) in enumerate(((vq, q_all), (vk, k_all), (vv, v_all)))
        ]
        + [
            pltpu.make_async_copy(source, target.at[h], local.at[12 + i])
            for i, (source, target) in enumerate(((ws, ws_all), (wc, wc_all)))
        ]
    )
    for j in range(n):
        for k, source in enumerate((aso, aco)):
            at = (2 * j + k) * HDA
            pltpu.make_async_copy(
                source.at[j * HDA : (j + 1) * HDA], wa_all.at[h, at : at + HDA], local.at[14]
            ).start()
    own.append(pltpu.make_async_copy(wa_all.at[h], wa_all.at[h], local.at[14]))
    with scope("T0barrier"):
        pl.semaphore_wait(barrier, len(others))

    a_copies, sent = {}, []

    def exchange(i, d, source, target):
        copy = remote(source, target, a_send.at[i, d], a_recv.at[i, d], place(d, 0))
        copy.start()
        a_copies[i, d] = copy

    for i, (source, target) in enumerate(((vq, q_all), (vk, k_all), (vv, v_all))):
        for d in range(1, n):
            exchange(i, d, head_cols(source, lax.rem(w + d, n)), target.at[w])

    targets = (ws_all, wc_all, wa_all)
    sources = (ws, wc, wa_all.at[h])
    partner = {"wide": w, "heads": h + 1 - 2 * lax.rem(h, 2)}
    w_copies, f_copies = {}, {i: [] for i in range(3)}

    def send_weights(i):
        for k in range(1, n // 2):
            copy = remote(
                sources[i], targets[i].at[h], w_send.at[i, k], w_recv.at[i, k], place(0, 2 * k)
            )
            copy.start()
            w_copies[i, k] = copy

    def share_weights(i):
        copy = remote(sources[i], targets[i].at[h], f_send.at[i, 0], f_recv.at[i, 0], partner)
        copy.start()
        f_copies[i].append(copy)

    def pass_weights(i):
        for k in range(1, n // 2):
            w_copies[i, k].wait_recv()
            slot = targets[i].at[lax.rem(h + n - 2 * k, n)]
            copy = remote(slot, slot, f_send.at[i, k], f_recv.at[i, k], partner)
            copy.start()
            f_copies[i].append(copy)

    def settle_weights(i):
        for copy in f_copies[i]:
            copy.wait_recv()

    send_weights(0)
    share_weights(0)
    share_weights(1)

    for copy in staged:
        copy.wait()
    for j in range(n):
        cols = slice(j * HDA, (j + 1) * HDA)
        pack[j, :rows, :] = jnp.concatenate([wide_stage[0, :, cols], wide_stage[1, :, cols]], 1)
        pack[j, rows : rows + half, :] = jnp.concatenate(
            [wide_stage[2, :half, cols], wide_stage[2, half:, cols]], 1
        )
        for k in range(3):
            at = rows + half + k * few
            pack[j, at : at + few, :] = jnp.concatenate(
                [few_stage[2 * k, :, cols], few_stage[2 * k + 1, :, cols]], 1
            )
    for d in range(1, n):
        exchange(3, d, pack.at[lax.rem(w + d, n)], p_all.at[w])
    own_pack = pltpu.make_async_copy(pack.at[w], p_all.at[w], local.at[0])
    own_pack.start()
    own.pop().wait()
    share_weights(2)

    for i in range(n):
        for j in range(n):
            column = j - i + REACH
            drop = jnp.float32(-1e30)
            if 0 <= column < table.shape[1]:
                drop = jnp.where(table[i, column] > 0, jnp.float32(0.0), drop)
            tall_bias[i * part_rows : (i + 1) * part_rows, j * few : (j + 1) * few] = jnp.full(
                (part_rows, few), drop
            )
            wide_bias[j * few : (j + 1) * few, i * rows : (i + 1) * rows] = jnp.full(
                (few, rows), drop
            )

    mine = h * n + w
    side = w // (n // 2)
    mate = w + 1 - 2 * lax.rem(w, 2)
    across_side = n // 2 - side
    far_start = (1 - side) * (n // 2)
    inner = (w > 0) & (w < n - 1)
    splits = (part_few * n + half // 2, half // 2)
    starts = (0, splits[0])
    x_copies = {}

    def chunk(ref, kind):
        if kind == 0:
            return ref
        return ref.at[pl.ds(starts[kind - 1], splits[kind - 1])]

    def buffers(kind):
        return (o_self, r_self) if kind == 0 else (o_rest, r_rest)

    def across(kind, d):
        source, landing = buffers(kind)
        copy = remote(
            source.at[lax.rem(h + d, n)], landing.at[mine],
            x_send.at[kind, d], x_recv.at[kind, d], place(0, d),
        )
        copy.start()
        x_copies[kind, d] = copy

    def along(kind, d):
        source, landing = buffers(kind)
        slot = lax.rem(h + n - d, n) * n + w
        piece = chunk(source.at[h] if d == 0 else landing.at[slot], kind)
        where = chunk(landing.at[slot], kind)
        for k, device, role in ((0, mate, 0), (1, across_side, 1 + lax.rem(w, 2))):
            copy = remote(
                piece, where, z_send.at[kind, d, k], z_recv.at[kind, d, role],
                {"wide": device, "heads": h},
            )
            copy.start()
            sent.append(copy)

    def arrival(kind, d, k):
        landing = buffers(kind)[1]
        slot = lax.rem(h + n - d, n) * n + far_start + k
        where = chunk(landing.at[slot], kind)
        return remote(
            where, where, r_send.at[kind, d, k], z_recv.at[kind, d, 1 + k],
            {"wide": mate, "heads": h},
        )

    def forward(kind, d):
        for k in range(2):
            copy = arrival(kind, d, k)
            copy.wait_recv()

            @pl.when(inner)
            def _():
                copy.start()

    def from_mate(kind, d):
        landing = buffers(kind)[1]
        slot = lax.rem(h + n - d, n) * n + mate
        where = chunk(landing.at[slot], kind)
        remote(
            where, where, z_send.at[kind, d, 0], z_recv.at[kind, d, 0],
            {"wide": mate, "heads": h},
        ).wait_recv()

    with scope("T1self"):
        for copy in own[:3]:
            copy.wait()
        for i in range(3):
            for d in range(1, n):
                a_copies[i, d].wait_recv()
    keys = k_all[...].reshape(n * rows, HDV)
    values = v_all[...].reshape(n * rows, HDV)

    def self_scores(d):
        at = pl.multiple_of(lax.rem(h + d, n) * part_rows, part_rows)
        return scored(q_all[:, pl.ds(at, part_rows), :].reshape(rows, HDV), keys)

    scores = self_scores(0)
    for d in range(n):
        following = self_scores(d + 1) if d + 1 < n else None
        weights, sums = softmax(scores, HDV)
        result = (mixed(weights, values) / sums).astype(bf16)
        scores = following
        o_self[pl.ds(lax.rem(h + d, n), 1)] = result[None]
        if d:
            across(0, d)
        else:
            r_self[pl.ds(mine, 1)] = result[None]
            along(0, 0)
        if d > 1:
            x_copies[0, d - 1].wait_recv()
            along(0, d - 1)
    send_weights(1)
    with scope("T2x"):
        x_copies[0, n - 1].wait_recv()
    along(0, n - 1)

    with scope("T3rest"):
        own_pack.wait()
        for d in range(1, n):
            a_copies[3, d].wait_recv()
    at = rows + half
    lane = lax.broadcasted_iota(jnp.int32, (n * few, 2 * HDA), 1)
    left = lane < HDA
    both = p_all[:, :rows, :].reshape(n * rows, 2 * HDA)
    vals = p_all[:, rows:at, :].reshape(n * half, 2 * HDA)
    keyed = p_all[:, at : at + few, :].reshape(n * few, 2 * HDA)
    asked = p_all[:, at + few : at + 2 * few, :].reshape(n * few, 2 * HDA)
    third = p_all[:, at + 2 * few : depth, :].reshape(n * few, 2 * HDA)
    zero = jnp.zeros_like(keyed)
    key_left = jnp.where(left, keyed, zero)
    query_right = jnp.where(left, zero, keyed)
    key_right = jnp.where(left, zero, third)
    twice = jnp.concatenate([third[:, :HDA], third[:, :HDA]], 1)

    scores_a = scored(asked, key_right)
    scores_c = scored(query_right, both) + wide_bias[...]
    weights, sums = softmax(scores_a, HDA)
    audio_own = mixed(weights, asked) / sums
    weights, sums = softmax(scores_c, HDA)
    upper = jnp.concatenate([weights[:, j * rows : j * rows + half] for j in range(n)], 1)
    lower = jnp.concatenate([weights[:, j * rows + half : (j + 1) * rows] for j in range(n)], 1)
    audio_other = (pltpu.roll(mixed(upper, vals), HDA, 1) + mixed(lower, vals)) / sums
    audio = jnp.where(left, audio_own, audio_other).astype(bf16)
    for t in range(n):
        o_rest[t, : n * part_few, :] = jnp.concatenate(
            [audio[j * few + t * part_few : j * few + (t + 1) * part_few, :] for j in range(n)], 0
        )
    forward(0, 0)

    def cross_scores(d):
        begin = pl.multiple_of(lax.rem(h + d, n) * part_rows, part_rows)
        queries = p_all[:, pl.ds(begin, part_rows), :].reshape(rows, 2 * HDA)
        return scored(queries, key_left) + tall_bias[...]

    low = lax.broadcasted_iota(jnp.int32, (half, 2 * HDA), 1) < HDA
    scores = cross_scores(0)
    for d in range(n):
        following = cross_scores(d + 1) if d + 1 < n else None
        weights, sums = softmax(scores, HDA)
        result = mixed(weights, twice) / sums
        scores = following
        block = lax.rem(h + d, n)
        packed = jnp.where(low, result[:half], result[half:]).astype(bf16)
        o_rest[pl.ds(block, 1), n * part_few :, :] = packed[None]
        if d:
            across(1, d)
            forward(0, d)
        else:
            r_rest[pl.ds(mine, 1)] = o_rest[pl.ds(h, 1)]
            along(1, 0)
            along(2, 0)
        if d > 1:
            x_copies[1, d - 1].wait_recv()
            along(1, d - 1)
            along(2, d - 1)
    send_weights(2)
    with scope("T4x"):
        x_copies[1, n - 1].wait_recv()
    along(1, n - 1)
    along(2, n - 1)

    with scope("T5w"):
        own[3].wait()
        own[4].wait()
        pass_weights(0)
        settle_weights(0)
    with scope("T6self"):
        for d in range(n):
            from_mate(0, d)
    heads = n * n
    joined = jnp.concatenate([r_self[s] for s in range(heads)], 1)
    totals[...] = jnp.dot(
        joined, ws_all[...].reshape(-1, ws.shape[1]), preferred_element_type=jnp.float32
    )
    with scope("T7w"):
        pass_weights(1)
        settle_weights(1)
        pass_weights(2)
        settle_weights(2)

    chunks = d_send.shape[0] - 1
    width = ws.shape[1] // chunks
    d_copies, last = {}, []

    def cut(ref, c):
        return ref if c == 0 else ref.at[:, (c - 1) * width : c * width]

    def rows_of(ref, c, block):
        size = part_few if c == 0 else part_rows
        return cut(ref.at[pl.ds(pl.multiple_of(block * size, size), size)], c)

    def first_hop(c, b):
        source, middle = (sum_a, mid_a) if c == 0 else (sum_v, mid_v)

        @pl.when(w != b)
        def _():
            remote(
                rows_of(source, c, b), cut(middle.at[w], c),
                d_send.at[c, b], d_recv.at[c, w], {"wide": b, "heads": h},
            ).start()

    def second_hop(c, origin):
        source, middle, out = (sum_a, mid_a, out_a) if c == 0 else (sum_v, mid_v, out_v)

        def go(ready):
            target = rows_of(out, c, h)

            @pl.when(origin != h)
            def _():
                remote(
                    ready, target, e_send.at[c, origin], e_recv.at[c, h],
                    {"wide": w, "heads": origin},
                ).start()

            @pl.when(origin == h)
            def _():
                pltpu.make_async_copy(ready, target, e_send.at[c, origin]).start()

        @pl.when(w == origin)
        def _():
            go(rows_of(source, c, w))

        @pl.when(w != origin)
        def _():
            piece = cut(middle.at[origin], c)
            remote(
                piece, piece, d_send.at[c, origin], d_recv.at[c, origin],
                {"wide": origin, "heads": h},
            ).wait_recv()
            go(piece)

    flat_c = wc_all[...].reshape(-1, wc.shape[1])
    for u in range(2):
        with scope("T8gather%d" % u):
            for d in range(n):
                forward(1 + u, d)
            for d in range(n):
                from_mate(1 + u, d)
        begin = n * part_few + u * (half // 2)
        piece = slice(begin, begin + half // 2)
        crossed = jnp.concatenate(
            [
                jnp.concatenate([r_rest[s, piece, :HDA] for s in range(heads)], 1),
                jnp.concatenate([r_rest[s, piece, HDA:] for s in range(heads)], 1),
            ],
            0,
        )
        products = jnp.dot(crossed, flat_c, preferred_element_type=jnp.float32)
        size = half // 2
        for k in range(2):
            where = slice((u + 2 * k) * size, (u + 2 * k + 1) * size)
            sum_v[where, :] = (
                totals[where, :] + products[k * size : (k + 1) * size, :]
            ).astype(bf16)
        for c in range(1, chunks + 1):
            for k in (1 - u, u):
                first_hop(c, u + 2 * k)
        if u == 0:
            audio_joined = jnp.concatenate([r_rest[s, : n * part_few, :] for s in range(heads)], 1)
            sum_a[...] = jnp.dot(
                audio_joined, wa_all[...].reshape(-1, aso.shape[1]),
                preferred_element_type=jnp.float32,
            ).astype(bf16)
            for b in range(n):
                first_hop(0, b)
    order = list(range(1, chunks + 1)) + [0]
    with scope("T9results"):
        for c in order:
            for origin in range(n):
                second_hop(c, origin)

    with scope("TAout"):
        for c in order:
            out = out_a if c == 0 else out_v
            for who in range(n):
                @pl.when(who != h)
                def _():
                    target = rows_of(out, c, who)
                    remote(
                        target, target, e_send.at[c, who], e_recv.at[c, who],
                        {"wide": w, "heads": who},
                    ).wait()

                @pl.when(who == h)
                def _():
                    target = rows_of(out, c, h)
                    pltpu.make_async_copy(target, target, e_send.at[c, who]).wait()

    with scope("TBsends"):
        for copy in (
            list(a_copies.values()) + list(w_copies.values()) + sum(f_copies.values(), [])
            + list(x_copies.values()) + sent
        ):
            copy.wait_send()
        for c in order:
            source = sum_a if c == 0 else sum_v
            for b in range(n):
                @pl.when(w != b)
                def _():
                    piece = rows_of(source, c, b)
                    remote(
                        piece, piece, d_send.at[c, b], d_recv.at[c, b], {"wide": b, "heads": h}
                    ).wait_send()

        @pl.when(inner)
        def _():
            for kind in range(3):
                for d in range(n):
                    for k in range(2):
                        arrival(kind, d, k).wait_send()


def shards(*args):
    n = lax.axis_size("wide")
    count = lax.axis_size("heads")
    head_count = args[2].shape[1] // HDV
    if not (n == count == head_count == 2 * REACH and args[5].shape[0] % (16 * n) == 0):
        return general_shards(*args)
    (video_hidden, audio_hidden, vq, vk, vv, aq, ak, av, cvq, cak, cav, caq, cvk, cvv,
     vso, vco, aso, aco, table) = args
    rows, few = vq.shape[0], aq.shape[0]
    depth = rows + rows // 2 + 3 * few
    anywhere = pl.BlockSpec(memory_space=pl.ANY)
    bf16, f32 = jnp.bfloat16, jnp.float32
    chunks = max(1, vso.shape[1] // 512)
    rest = rows // 2 + few
    dma = pltpu.SemaphoreType.DMA
    video_sum, audio_sum = pl.pallas_call(
        functools.partial(joint_kernel, n),
        out_shape=(
            jax.ShapeDtypeStruct(video_hidden.shape, bf16),
            jax.ShapeDtypeStruct(audio_hidden.shape, bf16),
        ),
        in_specs=[anywhere] * 16 + [pl.BlockSpec(memory_space=pltpu.SMEM)],
        out_specs=(anywhere, anywhere),
        scratch_shapes=[
            pltpu.VMEM((n, rows, HDV), bf16),
            pltpu.VMEM((n, rows, HDV), bf16),
            pltpu.VMEM((n, rows, HDV), bf16),
            pltpu.VMEM((3,) + cvq.shape, bf16),
            pltpu.VMEM((6,) + aq.shape, bf16),
            pltpu.VMEM((n, depth, 2 * HDA), bf16),
            pltpu.VMEM((n, depth, 2 * HDA), bf16),
            pltpu.VMEM((n,) + vso.shape, bf16),
            pltpu.VMEM((n,) + vco.shape, bf16),
            pltpu.VMEM((n, 2 * aso.shape[0], aso.shape[1]), bf16),
            pltpu.VMEM((rows, n * few), f32),
            pltpu.VMEM((n * few, n * rows), f32),
            pltpu.VMEM((n, rows, HDV), bf16),
            pltpu.VMEM((n, rest, 2 * HDA), bf16),
            pltpu.VMEM((n * n, rows, HDV), bf16),
            pltpu.VMEM((n * n, rest, 2 * HDA), bf16),
            pltpu.VMEM(video_hidden.shape, f32),
            pltpu.VMEM(video_hidden.shape, bf16),
            pltpu.VMEM(audio_hidden.shape, bf16),
            pltpu.VMEM((n, rows // n, video_hidden.shape[1]), bf16),
            pltpu.VMEM((n, few // n, audio_hidden.shape[1]), bf16),
            dma((4, n)), dma((4, n)),
            dma((3, n)), dma((3, n)),
            dma((3, n)), dma((3, n)),
            dma((2, n)), dma((2, n)),
            dma((3, n, 2)), dma((3, n, 3)), dma((3, n, 2)),
            dma((1 + chunks, n)), dma((1 + chunks, n)),
            dma((1 + chunks, n)), dma((1 + chunks, n)),
            dma((15,)),
        ],
        compiler_params=pltpu.CompilerParams(collective_id=0, has_side_effects=True),
        name="joint",
    )(vq, vk, vv, cvq, cvk, cvv, aq, ak, av, caq, cak, cav, vso, vco, aso, aco, table)
    video_out = video_hidden.astype(f32) + video_sum.astype(f32)
    audio_out = audio_hidden.astype(f32) + audio_sum.astype(f32)
    return (video_out.astype(bf16), audio_out.astype(bf16))


def solution(mesh):
    placed = (
        P(("groups", "wide"), "heads"),
        P(("groups", "wide"), "heads"),
        P(("groups", "wide"), "heads"),
        P(("groups", "wide"), "heads"),
        P(("groups", "wide"), "heads"),
        P(("groups", "wide"), "heads"),
        P(("groups", "wide"), "heads"),
        P(("groups", "wide"), "heads"),
        P(("groups", "wide"), "heads"),
        P(("groups", "wide"), "heads"),
        P(("groups", "wide"), "heads"),
        P(("groups", "wide"), "heads"),
        P(("groups", "wide"), "heads"),
        P(("groups", "wide"), "heads"),
        P("heads", "wide"),
        P("heads", "wide"),
        P("heads", "wide"),
        P("heads", "wide"),
        P("groups", None),
    )
    return jax.shard_map(
        shards,
        mesh=mesh,
        in_specs=placed,
        out_specs=(P(("groups", "wide"), "heads"), P(("groups", "wide"), "heads")),
        check_vma=False,
    )
```

```python
import contextlib
import functools
import math

import jax
import jax.numpy as jnp
from jax import lax
from jax.experimental import pallas as pl
from jax.experimental.pallas import tpu as pltpu
from jax.sharding import PartitionSpec as P

HDV = 128
HDA = 64
REACH = 2


def passed_along(value, axis, by):
    length = lax.axis_size(axis)
    pairs = [(i, i + by) for i in range(length) if 0 <= i + by < length]
    return lax.ppermute(value, axis, pairs)


def empty_state(row_count, head_count, head_size):
    return (
        jnp.full((head_count, row_count), -1e30, jnp.float32),
        jnp.zeros((head_count, row_count), jnp.float32),
        jnp.zeros((head_count, row_count, head_size), jnp.float32),
    )


def absorb(state, queries, key_rows, value_rows, head_size, allowed):
    maxima, totals, running = state
    head_count = queries.shape[1] // head_size
    query_heads = queries.reshape(queries.shape[0], head_count, head_size)
    key_heads = key_rows.reshape(key_rows.shape[0], head_count, head_size)
    value_heads = value_rows.reshape(value_rows.shape[0], head_count, head_size)
    scores = jnp.einsum(
        "qhd,khd->hqk", query_heads, key_heads, preferred_element_type=jnp.float32
    ) * (1.0 / math.sqrt(head_size))
    if allowed is not None:
        scores = jnp.where(allowed[None, None, :], scores, -1e30)
    new_peak = jnp.maximum(maxima, jnp.max(scores, axis=2))
    weights = jnp.exp(scores - new_peak[:, :, None])
    if allowed is not None:
        weights = jnp.where(allowed[None, None, :], weights, 0.0)
    rescale = jnp.exp(maxima - new_peak)
    totals = totals * rescale + jnp.sum(weights, axis=2)
    running = running * rescale[:, :, None] + jnp.einsum(
        "hqk,khd->hqd",
        weights.astype(jnp.bfloat16),
        value_heads,
        preferred_element_type=jnp.float32,
    )
    return (new_peak, totals, running)


def finish(state, head_size):
    maxima, totals, running = state
    result = running / totals[:, :, None]
    return (
        result.transpose(1, 0, 2)
        .reshape(result.shape[1], result.shape[0] * head_size)
        .astype(jnp.bfloat16)
    )


def permitted(key_blocks, position, table_row, wide_count):
    offsets = key_blocks - position + REACH
    matches = (offsets[:, None] == jnp.arange(2 * REACH + 1, dtype=jnp.int32)[None, :]) & (
        table_row[None, :] > 0
    )
    inside = (key_blocks >= 0) & (key_blocks < wide_count)
    return jnp.any(matches, axis=1) & inside


def general_shards(
    video_hidden,
    audio_hidden,
    video_query,
    video_key,
    video_value,
    audio_query,
    audio_key,
    audio_value,
    cross_video_query,
    cross_audio_key,
    cross_audio_value,
    cross_audio_query,
    cross_video_key,
    cross_video_value,
    video_self_out,
    video_cross_out,
    audio_self_out,
    audio_cross_out,
    intersection,
):
    position = lax.axis_index("wide")
    wide_count = lax.axis_size("wide")
    video_count = video_query.shape[0]
    audio_count = audio_query.shape[0]
    head_count = video_query.shape[1] // HDV
    video_start = empty_state(video_count, head_count, HDV)
    audio_start = empty_state(audio_count, head_count, HDA)
    carried = (video_start, audio_start)
    portion = (
        lax.all_gather(video_key, "wide", axis=0, tiled=True),
        lax.all_gather(video_value, "wide", axis=0, tiled=True),
        lax.all_gather(audio_key, "wide", axis=0, tiled=True),
        lax.all_gather(audio_value, "wide", axis=0, tiled=True),
    )
    video_state = absorb(carried[0], video_query, portion[0], portion[1], HDV, None)
    audio_state = absorb(carried[1], audio_query, portion[2], portion[3], HDA, None)
    table_row = lax.dynamic_slice_in_dim(intersection, position, 1, 0)[0]
    padded_table = jnp.pad(intersection, ((REACH, REACH), (0, 0)))
    flag_row = jnp.diagonal(
        jnp.fliplr(lax.dynamic_slice_in_dim(padded_table, position, 2 * REACH + 1, 0))
    )
    stacked = jnp.concatenate(
        [cross_audio_key, cross_audio_value, cross_video_key, cross_video_value], 0
    )

    def take_cross(carried, portion, block):
        audio_keys = portion[:audio_count]
        audio_values = portion[audio_count : 2 * audio_count]
        video_keys = portion[2 * audio_count : 2 * audio_count + video_count]
        video_values = portion[2 * audio_count + video_count :]
        audio_blocks = jnp.full((audio_count,), block, jnp.int32)
        video_blocks = jnp.full((video_count,), block, jnp.int32)
        return (
            absorb(
                carried[0],
                cross_video_query,
                audio_keys,
                audio_values,
                HDA,
                permitted(audio_blocks, position, table_row, wide_count),
            ),
            absorb(
                carried[1],
                cross_audio_query,
                video_keys,
                video_values,
                HDA,
                permitted(video_blocks, position, flag_row, wide_count),
            ),
        )

    cross_start = (
        empty_state(video_count, head_count, HDA),
        empty_state(audio_count, head_count, HDA),
    )
    carried = take_cross(cross_start, stacked, position)
    for offset in range(-REACH, REACH + 1):
        if offset != 0:
            nearby = passed_along(stacked, "wide", -offset)
            carried = take_cross(carried, nearby, position + offset)
    to_video, to_audio = carried
    video_joined = jnp.concatenate([finish(video_state, HDV), finish(to_video, HDA)], 1)
    audio_joined = jnp.concatenate([finish(audio_state, HDA), finish(to_audio, HDA)], 1)
    video_weights = jnp.concatenate([video_self_out, video_cross_out], 0)
    audio_weights = jnp.concatenate([audio_self_out, audio_cross_out], 0)
    video_terms = jnp.dot(
        video_joined,
        lax.all_gather(video_weights, "wide", axis=1, tiled=True),
        preferred_element_type=jnp.float32,
    )
    audio_terms = jnp.dot(
        audio_joined,
        lax.all_gather(audio_weights, "wide", axis=1, tiled=True),
        preferred_element_type=jnp.float32,
    )
    video_sum, audio_sum = (
        lax.psum_scatter(
            video_terms.astype(jnp.bfloat16), "heads", scatter_dimension=1, tiled=True
        ).astype(jnp.float32),
        lax.psum_scatter(
            audio_terms.astype(jnp.bfloat16), "heads", scatter_dimension=1, tiled=True
        ).astype(jnp.float32),
    )
    video_out = (video_hidden.astype(jnp.float32) + video_sum).astype(jnp.bfloat16)
    audio_out = (audio_hidden.astype(jnp.float32) + audio_sum).astype(jnp.bfloat16)
    return (video_out, audio_out)


NT = (((1,), (1,)), ((), ()))
MESH = pl.DeviceIdType.MESH


def scope(name):
    return contextlib.nullcontext()


def softmax(scores, head_size):
    factor = math.log2(math.e) / math.sqrt(head_size)
    weights = jnp.exp2((scores - jnp.max(scores, axis=1, keepdims=True)) * factor)
    return weights.astype(jnp.bfloat16), jnp.sum(weights, axis=1, keepdims=True)


def scored(queries, keys):
    return lax.dot_general(queries, keys, NT, preferred_element_type=jnp.float32)


def mixed(weights, values):
    return jnp.dot(weights, values, preferred_element_type=jnp.float32)


def joint_kernel(
    n,
    vq, vk, vv, cvq, cvk, cvv, aq, ak, av, caq, cak, cav, ws, wc, aso, aco, table,
    out_v, out_a,
    q_all, k_all, v_all, wide_stage, few_stage, pack, p_all, ws_all, wc_all, wa_all,
    tall_bias, wide_bias, o_self, o_rest, r_self, r_rest, totals, sum_v, sum_a,
    a_send, a_recv, w_send, w_recv, x_send, x_recv, z_send, z_recv, m_recv, r_send,
    e_send, e_recv, local,
):
    g = lax.axis_index("groups")
    w = lax.axis_index("wide")
    h = lax.axis_index("heads")
    rows, few = vq.shape[0], aq.shape[0]
    half = rows // 2
    part_rows, part_few = rows // n, few // n
    depth = p_all.shape[1]
    bf16 = jnp.bfloat16

    mine = h * n + w
    side = w // (n // 2)
    mate = w + 1 - 2 * lax.rem(w, 2)
    across_side = n // 2 - side
    far_start = (1 - side) * (n // 2)
    inner = (w > 0) & (w < n - 1)

    def place(dw, dh):
        return {"wide": lax.rem(w + dw, n), "heads": lax.rem(h + dh, n)}

    def remote(source, target, send, recv, device):
        return pltpu.make_async_remote_copy(
            src_ref=source, dst_ref=target, send_sem=send, recv_sem=recv,
            device_id=device, device_id_type=MESH,
        )

    others = [(d, 0) for d in range(1, n)] + [(0, d) for d in range(1, n)]
    barrier = pltpu.get_barrier_semaphore()
    for dw, dh in others:
        pl.semaphore_signal(barrier, inc=1, device_id=place(dw, dh), device_id_type=MESH)
    twin = {"groups": 1 - g}
    pl.semaphore_signal(barrier, inc=1, device_id=twin, device_id_type=MESH)

    def settle(piece, sem):
        pltpu.make_async_copy(piece, piece, sem).wait()

    def head_cols(ref, who):
        return ref.at[:, pl.ds(pl.multiple_of(who * HDV, HDV), HDV)]

    def start(copies):
        for copy in copies:
            copy.start()
        return copies

    staged = start(
        [
            pltpu.make_async_copy(source, wide_stage.at[i], local.at[i])
            for i, source in enumerate((cvq, cvk, cvv))
        ]
        + [
            pltpu.make_async_copy(source, few_stage.at[i], local.at[3 + i])
            for i, source in enumerate((cak, caq, av, aq, cav, ak))
        ]
    )
    own = start(
        [
            pltpu.make_async_copy(head_cols(source, w), target.at[w], local.at[9 + i])
            for i, (source, target) in enumerate(((vq, q_all), (vk, k_all), (vv, v_all)))
        ]
        + [
            pltpu.make_async_copy(source, target.at[h], local.at[12 + i])
            for i, (source, target) in enumerate(((ws, ws_all), (wc, wc_all)))
        ]
    )
    for j in range(n):
        for k, source in enumerate((aso, aco)):
            at = (2 * j + k) * HDA
            pltpu.make_async_copy(
                source.at[j * HDA : (j + 1) * HDA], wa_all.at[h, at : at + HDA], local.at[14]
            ).start()
    own.append(pltpu.make_async_copy(wa_all.at[h], wa_all.at[h], local.at[14]))
    with scope("T0barrier"):
        pl.semaphore_wait(barrier, len(others) + 1)

    far_end = (1 - side) * (n - 1)

    def exchange(target):
        for i, (source, landing) in enumerate(((vq, q_all), (vk, k_all), (vv, v_all))):
            remote(
                head_cols(source, target), landing.at[w], a_send.at[i], a_recv.at[i],
                {"wide": target, "heads": h},
            ).start()

    near = jnp.where(inner, across_side, mate)
    last = jnp.where(inner, mate, across_side)
    for target in (far_end, near, last):
        exchange(target)

    targets = (ws_all, wc_all, wa_all)
    sources = (ws, wc, wa_all.at[h])
    partner = {"wide": w, "heads": h + 1 - 2 * lax.rem(h, 2)}
    opposite = lax.rem(h + n // 2, n)

    def part_of(ref, which):
        size = ref.shape[0] // 2
        return ref.at[pl.ds(pl.multiple_of(which * size, size), size)]

    def send_weights(i):
        remote(
            part_of(sources[i], g), part_of(targets[i].at[h], g),
            w_send.at[i, 0], w_recv.at[i, 0], {"wide": w, "heads": opposite},
        ).start()

    def share_weights(i):
        remote(sources[i], targets[i].at[h], w_send.at[i, 1], w_recv.at[i, 1], partner).start()

    def swap_weights(i):
        piece = part_of(targets[i].at[opposite], g)
        settle(piece, w_recv.at[i, 0])
        remote(piece, piece, w_send.at[i, 2], w_recv.at[i, 2], twin).start()

    def pass_weights(i):
        slot = targets[i].at[opposite]
        settle(part_of(slot, 1 - g), w_recv.at[i, 2])
        remote(slot, slot, w_send.at[i, 3], w_recv.at[i, 3], partner).start()

    def settle_weights(i):
        settle(targets[i].at[h], w_recv.at[i, 1])
        settle(targets[i].at[h], w_recv.at[i, 3])

    for i in range(2):
        send_weights(i)
        share_weights(i)

    for copy in staged:
        copy.wait()
    for j in range(n):
        cols = slice(j * HDA, (j + 1) * HDA)
        pack[j, :rows, :] = jnp.concatenate([wide_stage[0, :, cols], wide_stage[1, :, cols]], 1)
        pack[j, rows : rows + half, :] = jnp.concatenate(
            [wide_stage[2, :half, cols], wide_stage[2, half:, cols]], 1
        )
        for k in range(3):
            at = rows + half + k * few
            pack[j, at : at + few, :] = jnp.concatenate(
                [few_stage[2 * k, :, cols], few_stage[2 * k + 1, :, cols]], 1
            )

    def exchange_rest(target):
        remote(
            pack.at[target], p_all.at[w], a_send.at[3], a_recv.at[3], {"wide": target, "heads": h}
        ).start()

    exchange_rest(mate)

    @pl.when(jnp.logical_not(inner))
    def _():
        exchange_rest(far_end)

    own_pack = pltpu.make_async_copy(pack.at[w], p_all.at[w], local.at[0])
    own_pack.start()
    own.pop().wait()
    share_weights(2)

    for i in range(n):
        for j in range(n):
            column = j - i + REACH
            drop = jnp.float32(-1e30)
            if 0 <= column < table.shape[1]:
                drop = jnp.where(table[i, column] > 0, jnp.float32(0.0), drop)
            tall_bias[i * part_rows : (i + 1) * part_rows, j * few : (j + 1) * few] = jnp.full(
                (part_rows, few), drop
            )
            wide_bias[j * few : (j + 1) * few, i * rows : (i + 1) * rows] = jnp.full(
                (few, rows), drop
            )

    splits = (part_few * n + half // 2, half // 2)
    starts = (0, splits[0])

    def chunk(ref, kind):
        if kind == 0:
            return ref
        return ref.at[pl.ds(starts[kind - 1], splits[kind - 1])]

    def buffers(kind):
        return (o_self, r_self) if kind == 0 else (o_rest, r_rest)

    def spread(kind, d):
        source, landing = buffers(kind)
        part = lax.rem(h + d, n)
        piece, where = chunk(source.at[part], kind), chunk(landing.at[mine], kind)
        if d:
            remote(
                piece, where, x_send.at[kind], x_recv.at[kind], {"wide": w, "heads": part}
            ).start()
        remote(
            piece, where, z_send.at[kind], z_recv.at[kind, d, lax.rem(w, 2)],
            {"wide": across_side, "heads": part},
        ).start()
        remote(
            piece, where, z_send.at[kind], m_recv.at[kind], {"wide": mate, "heads": part}
        ).start()

    def far_piece(kind, d, k):
        slot = lax.rem(h + n - d, n) * n + far_start + k
        return chunk(buffers(kind)[1].at[slot], kind)

    def forward(kind, d, ks):
        for k in ks:
            piece = far_piece(kind, d, k)
            settle(piece, z_recv.at[kind, d, k])
            remote(
                piece, piece, r_send.at[kind], z_recv.at[kind, d, k],
                {"wide": mate, "heads": h},
            ).start()

    def many(kind, count):
        landing = buffers(kind)[1]
        if kind == 0:
            return landing.at[:count]
        return landing.at[:count, pl.ds(starts[kind - 1], splits[kind - 1])]

    def gathered(kind):
        settle(many(kind, n - 1), x_recv.at[kind])
        settle(many(kind, n), m_recv.at[kind])

        @pl.when(jnp.logical_not(inner))
        def _():
            for d in range(n):
                for k in range(2):
                    settle(far_piece(kind, d, k), z_recv.at[kind, d, k])

    with scope("T1self"):
        for i, target in enumerate((q_all, k_all, v_all)):
            own[i].wait()
            settle(target.at[: n - 1], a_recv.at[i])

    @pl.when(inner)
    def _():
        exchange_rest(far_end)

    keys = k_all[...].reshape(n * rows, HDV)
    values = v_all[...].reshape(n * rows, HDV)

    def self_scores(d):
        at = pl.multiple_of(lax.rem(h + d, n) * part_rows, part_rows)
        return scored(q_all[:, pl.ds(at, part_rows), :].reshape(rows, HDV), keys)

    turns = list(range(1, n)) + [0]
    scores = self_scores(turns[0])
    for turn, d in enumerate(turns):
        following = self_scores(turns[turn + 1]) if turn + 1 < n else None
        weights, sums = softmax(scores, HDV)
        result = (mixed(weights, values) / sums).astype(bf16)
        scores = following
        o_self[pl.ds(lax.rem(h + d, n), 1)] = result[None]
        if not d:
            r_self[pl.ds(mine, 1)] = result[None]
        spread(0, d)
    exchange_rest(across_side)
    with scope("T2weights"):
        swap_weights(0)
        swap_weights(1)
    send_weights(2)
    with scope("T2forward"):
        @pl.when(inner)
        def _():
            for d in turns:
                forward(0, d, range(2))
    with scope("T3rest"):
        own_pack.wait()
        settle(p_all.at[: n - 1], a_recv.at[3])
    at = rows + half
    lane = lax.broadcasted_iota(jnp.int32, (n * few, 2 * HDA), 1)
    left = lane < HDA
    both = p_all[:, :rows, :].reshape(n * rows, 2 * HDA)
    vals = p_all[:, rows:at, :].reshape(n * half, 2 * HDA)
    keyed = p_all[:, at : at + few, :].reshape(n * few, 2 * HDA)
    asked = p_all[:, at + few : at + 2 * few, :].reshape(n * few, 2 * HDA)
    third = p_all[:, at + 2 * few : depth, :].reshape(n * few, 2 * HDA)
    zero = jnp.zeros_like(keyed)
    key_left = jnp.where(left, keyed, zero)
    query_right = jnp.where(left, zero, keyed)
    key_right = jnp.where(left, zero, third)
    twice = jnp.concatenate([third[:, :HDA], third[:, :HDA]], 1)

    scores_a = scored(asked, key_right)
    scores_c = scored(query_right, both) + wide_bias[...]
    weights, sums = softmax(scores_a, HDA)
    audio_own = mixed(weights, asked) / sums
    weights, sums = softmax(scores_c, HDA)
    upper = jnp.concatenate([weights[:, j * rows : j * rows + half] for j in range(n)], 1)
    lower = jnp.concatenate([weights[:, j * rows + half : (j + 1) * rows] for j in range(n)], 1)
    audio_other = (pltpu.roll(mixed(upper, vals), HDA, 1) + mixed(lower, vals)) / sums
    audio = jnp.where(left, audio_own, audio_other).astype(bf16)
    for t in range(n):
        o_rest[t, : n * part_few, :] = jnp.concatenate(
            [audio[j * few + t * part_few : j * few + (t + 1) * part_few, :] for j in range(n)], 0
        )
    def cross_scores(d):
        begin = pl.multiple_of(lax.rem(h + d, n) * part_rows, part_rows)
        queries = p_all[:, pl.ds(begin, part_rows), :].reshape(rows, 2 * HDA)
        return scored(queries, key_left) + tall_bias[...]

    low = lax.broadcasted_iota(jnp.int32, (half, 2 * HDA), 1) < HDA
    scores = cross_scores(turns[0])
    for turn, d in enumerate(turns):
        following = cross_scores(turns[turn + 1]) if turn + 1 < n else None
        weights, sums = softmax(scores, HDA)
        result = mixed(weights, twice) / sums
        scores = following
        block = lax.rem(h + d, n)
        upper = [result[j * part_rows : (j + 1) * part_rows] for j in reversed(range(n // 2))]
        packed = jnp.where(low, jnp.concatenate(upper, 0), result[half:]).astype(bf16)
        o_rest[pl.ds(block, 1), n * part_few :, :] = packed[None]
        if not d:
            r_rest[pl.ds(mine, 1)] = o_rest[pl.ds(h, 1)]
        spread(1, d)
        spread(2, d)
    with scope("T4weights"):
        swap_weights(2)
        pass_weights(0)
        pass_weights(1)
    with scope("T4forward"):
        @pl.when(inner)
        def _():
            for which in range(2):
                for kind in (1, 2):
                    for d in turns:
                        forward(kind, d, [lax.rem(w + which, 2)])
    with scope("T5w"):
        own[3].wait()
        own[4].wait()
        settle_weights(0)
    with scope("T6self"):
        gathered(0)
    heads = n * n
    joined = jnp.concatenate([r_self[s] for s in range(heads)], 1)
    totals[...] = jnp.dot(
        joined, ws_all[...].reshape(-1, ws.shape[1]), preferred_element_type=jnp.float32
    )
    with scope("T7w"):
        settle_weights(1)

    def rows_of(ref, block, size):
        return ref.at[pl.ds(pl.multiple_of(block * size, size), size)]

    def deliver(c, b):
        source, out, size = ((sum_v, out_v, part_rows), (sum_a, out_a, part_few))[c]
        piece, target = rows_of(source, b, size), rows_of(out, h, size)
        away = (w != b) | (w != h)

        @pl.when(away)
        def _():
            remote(
                piece, target, e_send.at[c], e_recv.at[c], {"wide": b, "heads": w}
            ).start()

        @pl.when(jnp.logical_not(away))
        def _():
            pltpu.make_async_copy(piece, target, e_recv.at[c]).start()

    flat_c = wc_all[...].reshape(-1, wc.shape[1])
    for u in range(2):
        with scope("T8gather%d" % u):
            gathered(1 + u)
        begin = n * part_few + u * (half // 2)
        piece = slice(begin, begin + half // 2)
        crossed = jnp.concatenate(
            [
                jnp.concatenate([r_rest[s, piece, :HDA] for s in range(heads)], 1),
                jnp.concatenate([r_rest[s, piece, HDA:] for s in range(heads)], 1),
            ],
            0,
        )
        products = jnp.dot(crossed, flat_c, preferred_element_type=jnp.float32)
        size = half // 2
        for k in range(2):
            b = (n // 2 - 1 - u, n // 2 + u)[k]
            where = slice(b * size, (b + 1) * size)
            sum_v[where, :] = (
                totals[where, :] + products[k * size : (k + 1) * size, :]
            ).astype(bf16)
        if u == 1:
            with scope("T8sent"):
                @pl.when(inner)
                def _():
                    for kind in range(3):
                        settle(many(kind, 2 * n), r_send.at[kind])

        for b in (n // 2 - 1 - u, n // 2 + u):
            deliver(0, b)
        if u == 0:
            with scope("T8weights"):
                pass_weights(2)
                settle_weights(2)
            audio_joined = jnp.concatenate([r_rest[s, : n * part_few, :] for s in range(heads)], 1)
            sum_a[...] = jnp.dot(
                audio_joined, wa_all[...].reshape(-1, aso.shape[1]),
                preferred_element_type=jnp.float32,
            ).astype(bf16)
            for b in range(n):
                deliver(1, b)

    with scope("T9results"):
        settle(out_v, e_recv.at[0])
        settle(out_a, e_recv.at[1])

    with scope("TBsends"):
        for i, target in enumerate((q_all, k_all, v_all, p_all)):
            settle(target.at[: n - 1], a_send.at[i])
        for i in range(3):
            settle(part_of(targets[i].at[h], g), w_send.at[i, 0])
            settle(targets[i].at[h], w_send.at[i, 1])
            settle(part_of(targets[i].at[h], g), w_send.at[i, 2])
            settle(targets[i].at[h], w_send.at[i, 3])
        for kind in range(3):
            settle(many(kind, n - 1), x_send.at[kind])
            settle(many(kind, 2 * n), z_send.at[kind])
        for c, (ref, size) in enumerate(((sum_v, part_rows), (sum_a, part_few))):
            settle(ref.at[: (n - 1) * size], e_send.at[c])

            @pl.when(w != h)
            def _():
                settle(ref.at[:size], e_send.at[c])


def shards(*args):
    n = lax.axis_size("wide")
    count = lax.axis_size("heads")
    head_count = args[2].shape[1] // HDV
    paired = lax.axis_size("groups") == 2
    if not (paired and n == count == head_count == 2 * REACH and args[5].shape[0] % (16 * n) == 0):
        return general_shards(*args)
    (video_hidden, audio_hidden, vq, vk, vv, aq, ak, av, cvq, cak, cav, caq, cvk, cvv,
     vso, vco, aso, aco, table) = args
    rows, few = vq.shape[0], aq.shape[0]
    depth = rows + rows // 2 + 3 * few
    anywhere = pl.BlockSpec(memory_space=pl.ANY)
    bf16, f32 = jnp.bfloat16, jnp.float32
    rest = rows // 2 + few
    dma = pltpu.SemaphoreType.DMA
    video_sum, audio_sum = pl.pallas_call(
        functools.partial(joint_kernel, n),
        out_shape=(
            jax.ShapeDtypeStruct(video_hidden.shape, bf16),
            jax.ShapeDtypeStruct(audio_hidden.shape, bf16),
        ),
        in_specs=[anywhere] * 16 + [pl.BlockSpec(memory_space=pltpu.SMEM)],
        out_specs=(anywhere, anywhere),
        scratch_shapes=[
            pltpu.VMEM((n, rows, HDV), bf16),
            pltpu.VMEM((n, rows, HDV), bf16),
            pltpu.VMEM((n, rows, HDV), bf16),
            pltpu.VMEM((3,) + cvq.shape, bf16),
            pltpu.VMEM((6,) + aq.shape, bf16),
            pltpu.VMEM((n, depth, 2 * HDA), bf16),
            pltpu.VMEM((n, depth, 2 * HDA), bf16),
            pltpu.VMEM((n,) + vso.shape, bf16),
            pltpu.VMEM((n,) + vco.shape, bf16),
            pltpu.VMEM((n, 2 * aso.shape[0], aso.shape[1]), bf16),
            pltpu.VMEM((rows, n * few), f32),
            pltpu.VMEM((n * few, n * rows), f32),
            pltpu.VMEM((n, rows, HDV), bf16),
            pltpu.VMEM((n, rest, 2 * HDA), bf16),
            pltpu.VMEM((n * n, rows, HDV), bf16),
            pltpu.VMEM((n * n, rest, 2 * HDA), bf16),
            pltpu.VMEM(video_hidden.shape, f32),
            pltpu.VMEM(video_hidden.shape, bf16),
            pltpu.VMEM(audio_hidden.shape, bf16),
            dma((4,)), dma((4,)),
            dma((3, 4)), dma((3, 4)),
            dma((3,)), dma((3,)),
            dma((3,)), dma((3, n, 2)), dma((3,)), dma((3,)),
            dma((2,)), dma((2,)),
            dma((15,)),
        ],
        compiler_params=pltpu.CompilerParams(collective_id=0, has_side_effects=True),
        name="joint",
    )(vq, vk, vv, cvq, cvk, cvv, aq, ak, av, caq, cak, cav, vso, vco, aso, aco, table)
    video_out = video_hidden.astype(f32) + video_sum.astype(f32)
    audio_out = audio_hidden.astype(f32) + audio_sum.astype(f32)
    return (video_out.astype(bf16), audio_out.astype(bf16))


def solution(mesh):
    placed = (
        P(("groups", "wide"), "heads"),
        P(("groups", "wide"), "heads"),
        P(("groups", "wide"), "heads"),
        P(("groups", "wide"), "heads"),
        P(("groups", "wide"), "heads"),
        P(("groups", "wide"), "heads"),
        P(("groups", "wide"), "heads"),
        P(("groups", "wide"), "heads"),
        P(("groups", "wide"), "heads"),
        P(("groups", "wide"), "heads"),
        P(("groups", "wide"), "heads"),
        P(("groups", "wide"), "heads"),
        P(("groups", "wide"), "heads"),
        P(("groups", "wide"), "heads"),
        P("heads", "wide"),
        P("heads", "wide"),
        P("heads", "wide"),
        P("heads", "wide"),
        P("groups", None),
    )
    return jax.shard_map(
        shards,
        mesh=mesh,
        in_specs=placed,
        out_specs=(P(("groups", "wide"), "heads"), P(("groups", "wide"), "heads")),
        check_vma=False,
    )
```

```python
import contextlib
import functools
import math

import jax
import jax.numpy as jnp
from jax import lax
from jax.experimental import pallas as pl
from jax.experimental.pallas import tpu as pltpu
from jax.sharding import PartitionSpec as P

HDV = 128
HDA = 64
REACH = 2


def passed_along(value, axis, by):
    length = lax.axis_size(axis)
    pairs = [(i, i + by) for i in range(length) if 0 <= i + by < length]
    return lax.ppermute(value, axis, pairs)


def empty_state(row_count, head_count, head_size):
    return (
        jnp.full((head_count, row_count), -1e30, jnp.float32),
        jnp.zeros((head_count, row_count), jnp.float32),
        jnp.zeros((head_count, row_count, head_size), jnp.float32),
    )


def absorb(state, queries, key_rows, value_rows, head_size, allowed):
    maxima, totals, running = state
    head_count = queries.shape[1] // head_size
    query_heads = queries.reshape(queries.shape[0], head_count, head_size)
    key_heads = key_rows.reshape(key_rows.shape[0], head_count, head_size)
    value_heads = value_rows.reshape(value_rows.shape[0], head_count, head_size)
    scores = jnp.einsum(
        "qhd,khd->hqk", query_heads, key_heads, preferred_element_type=jnp.float32
    ) * (1.0 / math.sqrt(head_size))
    if allowed is not None:
        scores = jnp.where(allowed[None, None, :], scores, -1e30)
    new_peak = jnp.maximum(maxima, jnp.max(scores, axis=2))
    weights = jnp.exp(scores - new_peak[:, :, None])
    if allowed is not None:
        weights = jnp.where(allowed[None, None, :], weights, 0.0)
    rescale = jnp.exp(maxima - new_peak)
    totals = totals * rescale + jnp.sum(weights, axis=2)
    running = running * rescale[:, :, None] + jnp.einsum(
        "hqk,khd->hqd",
        weights.astype(jnp.bfloat16),
        value_heads,
        preferred_element_type=jnp.float32,
    )
    return (new_peak, totals, running)


def finish(state, head_size):
    maxima, totals, running = state
    result = running / totals[:, :, None]
    return (
        result.transpose(1, 0, 2)
        .reshape(result.shape[1], result.shape[0] * head_size)
        .astype(jnp.bfloat16)
    )


def permitted(key_blocks, position, table_row, wide_count):
    offsets = key_blocks - position + REACH
    matches = (offsets[:, None] == jnp.arange(2 * REACH + 1, dtype=jnp.int32)[None, :]) & (
        table_row[None, :] > 0
    )
    inside = (key_blocks >= 0) & (key_blocks < wide_count)
    return jnp.any(matches, axis=1) & inside


def general_shards(
    video_hidden,
    audio_hidden,
    video_query,
    video_key,
    video_value,
    audio_query,
    audio_key,
    audio_value,
    cross_video_query,
    cross_audio_key,
    cross_audio_value,
    cross_audio_query,
    cross_video_key,
    cross_video_value,
    video_self_out,
    video_cross_out,
    audio_self_out,
    audio_cross_out,
    intersection,
):
    position = lax.axis_index("wide")
    wide_count = lax.axis_size("wide")
    video_count = video_query.shape[0]
    audio_count = audio_query.shape[0]
    head_count = video_query.shape[1] // HDV
    video_start = empty_state(video_count, head_count, HDV)
    audio_start = empty_state(audio_count, head_count, HDA)
    carried = (video_start, audio_start)
    portion = (
        lax.all_gather(video_key, "wide", axis=0, tiled=True),
        lax.all_gather(video_value, "wide", axis=0, tiled=True),
        lax.all_gather(audio_key, "wide", axis=0, tiled=True),
        lax.all_gather(audio_value, "wide", axis=0, tiled=True),
    )
    video_state = absorb(carried[0], video_query, portion[0], portion[1], HDV, None)
    audio_state = absorb(carried[1], audio_query, portion[2], portion[3], HDA, None)
    table_row = lax.dynamic_slice_in_dim(intersection, position, 1, 0)[0]
    padded_table = jnp.pad(intersection, ((REACH, REACH), (0, 0)))
    flag_row = jnp.diagonal(
        jnp.fliplr(lax.dynamic_slice_in_dim(padded_table, position, 2 * REACH + 1, 0))
    )
    stacked = jnp.concatenate(
        [cross_audio_key, cross_audio_value, cross_video_key, cross_video_value], 0
    )

    def take_cross(carried, portion, block):
        audio_keys = portion[:audio_count]
        audio_values = portion[audio_count : 2 * audio_count]
        video_keys = portion[2 * audio_count : 2 * audio_count + video_count]
        video_values = portion[2 * audio_count + video_count :]
        audio_blocks = jnp.full((audio_count,), block, jnp.int32)
        video_blocks = jnp.full((video_count,), block, jnp.int32)
        return (
            absorb(
                carried[0],
                cross_video_query,
                audio_keys,
                audio_values,
                HDA,
                permitted(audio_blocks, position, table_row, wide_count),
            ),
            absorb(
                carried[1],
                cross_audio_query,
                video_keys,
                video_values,
                HDA,
                permitted(video_blocks, position, flag_row, wide_count),
            ),
        )

    cross_start = (
        empty_state(video_count, head_count, HDA),
        empty_state(audio_count, head_count, HDA),
    )
    carried = take_cross(cross_start, stacked, position)
    for offset in range(-REACH, REACH + 1):
        if offset != 0:
            nearby = passed_along(stacked, "wide", -offset)
            carried = take_cross(carried, nearby, position + offset)
    to_video, to_audio = carried
    video_joined = jnp.concatenate([finish(video_state, HDV), finish(to_video, HDA)], 1)
    audio_joined = jnp.concatenate([finish(audio_state, HDA), finish(to_audio, HDA)], 1)
    video_weights = jnp.concatenate([video_self_out, video_cross_out], 0)
    audio_weights = jnp.concatenate([audio_self_out, audio_cross_out], 0)
    video_terms = jnp.dot(
        video_joined,
        lax.all_gather(video_weights, "wide", axis=1, tiled=True),
        preferred_element_type=jnp.float32,
    )
    audio_terms = jnp.dot(
        audio_joined,
        lax.all_gather(audio_weights, "wide", axis=1, tiled=True),
        preferred_element_type=jnp.float32,
    )
    video_sum, audio_sum = (
        lax.psum_scatter(
            video_terms.astype(jnp.bfloat16), "heads", scatter_dimension=1, tiled=True
        ).astype(jnp.float32),
        lax.psum_scatter(
            audio_terms.astype(jnp.bfloat16), "heads", scatter_dimension=1, tiled=True
        ).astype(jnp.float32),
    )
    video_out = (video_hidden.astype(jnp.float32) + video_sum).astype(jnp.bfloat16)
    audio_out = (audio_hidden.astype(jnp.float32) + audio_sum).astype(jnp.bfloat16)
    return (video_out, audio_out)


NT = (((1,), (1,)), ((), ()))
MESH = pl.DeviceIdType.MESH


def scope(name):
    return contextlib.nullcontext()


def softmax(scores, head_size):
    factor = math.log2(math.e) / math.sqrt(head_size)
    weights = jnp.exp2((scores - jnp.max(scores, axis=1, keepdims=True)) * factor)
    return weights.astype(jnp.bfloat16), jnp.sum(weights, axis=1, keepdims=True)


def scored(queries, keys):
    return lax.dot_general(queries, keys, NT, preferred_element_type=jnp.float32)


def mixed(weights, values):
    return jnp.dot(weights, values, preferred_element_type=jnp.float32)


def joint_kernel(
    n,
    vq, vk, vv, cvq, cvk, cvv, aq, ak, av, caq, cak, cav, ws, wc, aso, aco, table,
    out_v, out_a,
    q_all, k_all, v_all, self_stage, wide_stage, few_stage, pack, p_all, ws_all, wc_all, wa_all,
    tall_bias, wide_bias, o_self, o_rest, r_self, r_rest, totals, sum_v, sum_a,
    a_send, a_recv, w_send, w_recv, x_send, x_recv, z_send, z_recv, m_recv, r_send,
    e_send, e_recv, local,
):
    g = lax.axis_index("groups")
    w = lax.axis_index("wide")
    h = lax.axis_index("heads")
    rows, few = vq.shape[0], aq.shape[0]
    half = rows // 2
    part_rows, part_few = rows // n, few // n
    depth = p_all.shape[1]
    bf16 = jnp.bfloat16

    mine = h * n + w
    side = w // (n // 2)
    mate = w + 1 - 2 * lax.rem(w, 2)
    across_side = n // 2 - side
    far_start = (1 - side) * (n // 2)
    inner = (w > 0) & (w < n - 1)

    def place(dw, dh):
        return {"wide": lax.rem(w + dw, n), "heads": lax.rem(h + dh, n)}

    def remote(source, target, send, recv, device):
        return pltpu.make_async_remote_copy(
            src_ref=source, dst_ref=target, send_sem=send, recv_sem=recv,
            device_id=device, device_id_type=MESH,
        )

    others = [(d, 0) for d in range(1, n)] + [(0, d) for d in range(1, n)]
    barrier = pltpu.get_barrier_semaphore()
    for dw, dh in others:
        pl.semaphore_signal(barrier, inc=1, device_id=place(dw, dh), device_id_type=MESH)
    twin = {"groups": 1 - g}
    pl.semaphore_signal(barrier, inc=1, device_id=twin, device_id_type=MESH)

    def settle(piece, sem):
        pltpu.make_async_copy(piece, piece, sem).wait()

    def head_cols(ref, who):
        return ref.at[:, pl.ds(pl.multiple_of(who * HDV, HDV), HDV)]

    def start(copies):
        for copy in copies:
            copy.start()
        return copies

    streams = ((vq, q_all), (vk, k_all), (vv, v_all))
    self_staged = start(
        [
            pltpu.make_async_copy(source, self_stage.at[i], local.at[15 + i])
            for i, (source, _) in enumerate(streams)
        ]
    )
    staged = start(
        [
            pltpu.make_async_copy(source, wide_stage.at[i], local.at[i])
            for i, source in enumerate((cvq, cvk, cvv))
        ]
        + [
            pltpu.make_async_copy(source, few_stage.at[i], local.at[3 + i])
            for i, source in enumerate((cak, caq, av, aq, cav, ak))
        ]
    )
    own = start(
        [
            pltpu.make_async_copy(head_cols(source, w), target.at[w], local.at[9 + i])
            for i, (source, target) in enumerate(streams)
        ]
        + [
            pltpu.make_async_copy(source, target.at[h], local.at[12 + i])
            for i, (source, target) in enumerate(((ws, ws_all), (wc, wc_all)))
        ]
    )
    for j in range(n):
        for k, source in enumerate((aso, aco)):
            at = (2 * j + k) * HDA
            pltpu.make_async_copy(
                source.at[j * HDA : (j + 1) * HDA], wa_all.at[h, at : at + HDA], local.at[14]
            ).start()
    own.append(pltpu.make_async_copy(wa_all.at[h], wa_all.at[h], local.at[14]))
    for copy in self_staged:
        copy.wait()
    with scope("T0barrier"):
        pl.semaphore_wait(barrier, len(others) + 1)

    far_end = (1 - side) * (n - 1)

    def exchange(target):
        for i, (_, landing) in enumerate(streams):
            remote(
                head_cols(self_stage.at[i], target), landing.at[w], a_send.at[i], a_recv.at[i],
                {"wide": target, "heads": h},
            ).start()

    near = jnp.where(inner, across_side, mate)
    last = jnp.where(inner, mate, across_side)
    for target in (far_end, near, last):
        exchange(target)

    targets = (ws_all, wc_all, wa_all)
    sources = (ws, wc, wa_all.at[h])
    partner = {"wide": w, "heads": h + 1 - 2 * lax.rem(h, 2)}
    opposite = lax.rem(h + n // 2, n)

    def part_of(ref, which):
        size = ref.shape[0] // 2
        return ref.at[pl.ds(pl.multiple_of(which * size, size), size)]

    def send_weights(i):
        remote(
            part_of(sources[i], g), part_of(targets[i].at[h], g),
            w_send.at[i, 0], w_recv.at[i, 0], {"wide": w, "heads": opposite},
        ).start()

    def share_weights(i):
        remote(sources[i], targets[i].at[h], w_send.at[i, 1], w_recv.at[i, 1], partner).start()

    def swap_weights(i):
        piece = part_of(targets[i].at[opposite], g)
        settle(piece, w_recv.at[i, 0])
        remote(piece, piece, w_send.at[i, 2], w_recv.at[i, 2], twin).start()

    def pass_weights(i):
        slot = targets[i].at[opposite]
        settle(part_of(slot, 1 - g), w_recv.at[i, 2])
        remote(slot, slot, w_send.at[i, 3], w_recv.at[i, 3], partner).start()

    def settle_weights(i):
        settle(targets[i].at[h], w_recv.at[i, 1])
        settle(targets[i].at[h], w_recv.at[i, 3])

    for i in range(2):
        send_weights(i)
        share_weights(i)

    for copy in staged:
        copy.wait()
    for j in range(n):
        cols = slice(j * HDA, (j + 1) * HDA)
        pack[j, :rows, :] = jnp.concatenate([wide_stage[0, :, cols], wide_stage[1, :, cols]], 1)
        pack[j, rows : rows + half, :] = jnp.concatenate(
            [wide_stage[2, :half, cols], wide_stage[2, half:, cols]], 1
        )
        for k in range(3):
            at = rows + half + k * few
            pack[j, at : at + few, :] = jnp.concatenate(
                [few_stage[2 * k, :, cols], few_stage[2 * k + 1, :, cols]], 1
            )

    def exchange_rest(target):
        remote(
            pack.at[target], p_all.at[w], a_send.at[3], a_recv.at[3], {"wide": target, "heads": h}
        ).start()

    outer = jnp.logical_not(inner)
    exchange_rest(mate)

    @pl.when(outer)
    def _():
        exchange_rest(far_end)


    own_pack = pltpu.make_async_copy(pack.at[w], p_all.at[w], local.at[0])
    own_pack.start()
    own.pop().wait()
    send_weights(2)
    share_weights(2)

    for i in range(n):
        for j in range(n):
            column = j - i + REACH
            drop = jnp.float32(-1e30)
            if 0 <= column < table.shape[1]:
                drop = jnp.where(table[i, column] > 0, jnp.float32(0.0), drop)
            tall_bias[i * part_rows : (i + 1) * part_rows, j * few : (j + 1) * few] = jnp.full(
                (part_rows, few), drop
            )
            wide_bias[j * few : (j + 1) * few, i * rows : (i + 1) * rows] = jnp.full(
                (few, rows), drop
            )

    splits = (part_few * n + half // 2, half // 2)
    starts = (0, splits[0])

    def chunk(ref, kind):
        if kind == 0:
            return ref
        return ref.at[pl.ds(starts[kind - 1], splits[kind - 1])]

    def buffers(kind):
        return (o_self, r_self) if kind == 0 else (o_rest, r_rest)

    orders = ((1, 0, 2, 3), (2, 3, 1, 0))

    def moved(e):
        return lax.rem(h // 2 + e // 2, 2) * 2 + lax.rem(h + e, 2)

    def turn_of(i):
        return orders[0][i] + lax.rem(w, 2) * (orders[1][i] - orders[0][i])

    def outgoing(kind, i):
        source, landing = buffers(kind)
        d = turn_of(i)
        part = moved(d)
        return d, part, chunk(source.at[part], kind), chunk(landing.at[mine], kind)

    def to_plane(kind, i):
        _, part, piece, where = outgoing(kind, i)

        @pl.when(part != h)
        def _():
            remote(
                piece, where, x_send.at[kind], x_recv.at[kind], {"wide": w, "heads": part}
            ).start()

    def to_across(kind, i):
        d, part, piece, where = outgoing(kind, i)
        remote(
            piece, where, z_send.at[kind], z_recv.at[kind, d, lax.rem(w, 2)],
            {"wide": across_side, "heads": part},
        ).start()

    def to_mate(kind, i):
        _, part, piece, where = outgoing(kind, i)
        remote(
            piece, where, z_send.at[kind], m_recv.at[kind], {"wide": mate, "heads": part}
        ).start()

    def far_piece(kind, d, k):
        return chunk(buffers(kind)[1].at[moved(d) * n + far_start + k], kind)

    def forward(kind, i, ks):
        for k in ks:
            d = orders[0][i] + k * (orders[1][i] - orders[0][i])
            piece = far_piece(kind, d, k)
            settle(piece, z_recv.at[kind, d, k])
            remote(
                piece, piece, r_send.at[kind], z_recv.at[kind, d, k],
                {"wide": mate, "heads": h},
            ).start()

    def many(kind, count):
        landing = buffers(kind)[1]
        if kind == 0:
            return landing.at[:count]
        return landing.at[:count, pl.ds(starts[kind - 1], splits[kind - 1])]

    def gathered(kind):
        settle(many(kind, n - 1), x_recv.at[kind])
        settle(many(kind, n), m_recv.at[kind])

        @pl.when(outer)
        def _():
            for d in range(n):
                for k in range(2):
                    settle(far_piece(kind, d, k), z_recv.at[kind, d, k])

    with scope("T1self"):
        for i, target in enumerate((q_all, k_all, v_all)):
            own[i].wait()
            settle(target.at[: n - 1], a_recv.at[i])

    @pl.when(inner)
    def _():
        exchange_rest(far_end)

    keys = k_all[...].reshape(n * rows, HDV)
    values = v_all[...].reshape(n * rows, HDV)

    def self_scores(i):
        at = pl.multiple_of(moved(turn_of(i)) * part_rows, part_rows)
        return scored(q_all[:, pl.ds(at, part_rows), :].reshape(rows, HDV), keys)

    scores = self_scores(0)
    for i in range(n):
        following = self_scores(i + 1) if i + 1 < n else None
        weights, sums = softmax(scores, HDV)
        result = (mixed(weights, values) / sums).astype(bf16)
        scores = following
        o_self[pl.ds(moved(turn_of(i)), 1)] = result[None]
        to_plane(0, i)
        to_across(0, i)
        to_mate(0, i)
    r_self[pl.ds(mine, 1)] = o_self[pl.ds(h, 1)]

    @pl.when(inner)
    def _():
        exchange_rest(across_side)

    with scope("T2weights"):
        swap_weights(0)
        swap_weights(1)
    with scope("T2forward"):
        @pl.when(inner)
        def _():
            for k in (lax.rem(w, 2), lax.rem(w + 1, 2)):
                for i in range(n):
                    forward(0, i, [k])

    swap_weights(2)
    with scope("T3rest"):
        own_pack.wait()
        settle(p_all.at[: n - 1], a_recv.at[3])

    at = rows + half
    lane = lax.broadcasted_iota(jnp.int32, (n * few, 2 * HDA), 1)
    left = lane < HDA
    both = p_all[:, :rows, :].reshape(n * rows, 2 * HDA)
    vals = p_all[:, rows:at, :].reshape(n * half, 2 * HDA)
    keyed = p_all[:, at : at + few, :].reshape(n * few, 2 * HDA)
    asked = p_all[:, at + few : at + 2 * few, :].reshape(n * few, 2 * HDA)
    third = p_all[:, at + 2 * few : depth, :].reshape(n * few, 2 * HDA)
    zero = jnp.zeros_like(keyed)
    key_left = jnp.where(left, keyed, zero)
    query_right = jnp.where(left, zero, keyed)
    key_right = jnp.where(left, zero, third)
    twice = jnp.concatenate([third[:, :HDA], third[:, :HDA]], 1)

    scores_a = scored(asked, key_right)
    scores_c = scored(query_right, both) + wide_bias[...]
    weights, sums = softmax(scores_a, HDA)
    audio_own = mixed(weights, asked) / sums
    weights, sums = softmax(scores_c, HDA)
    upper = jnp.concatenate([weights[:, j * rows : j * rows + half] for j in range(n)], 1)
    lower = jnp.concatenate([weights[:, j * rows + half : (j + 1) * rows] for j in range(n)], 1)
    audio_other = (pltpu.roll(mixed(upper, vals), HDA, 1) + mixed(lower, vals)) / sums
    audio = jnp.where(left, audio_own, audio_other).astype(bf16)
    for t in range(n):
        o_rest[t, : n * part_few, :] = jnp.concatenate(
            [audio[j * few + t * part_few : j * few + (t + 1) * part_few, :] for j in range(n)], 0
        )
    def cross_scores(i):
        begin = pl.multiple_of(moved(turn_of(i)) * part_rows, part_rows)
        queries = p_all[:, pl.ds(begin, part_rows), :].reshape(rows, 2 * HDA)
        return scored(queries, key_left) + tall_bias[...]

    low = lax.broadcasted_iota(jnp.int32, (half, 2 * HDA), 1) < HDA
    scores = cross_scores(0)
    for i in range(n):
        following = cross_scores(i + 1) if i + 1 < n else None
        weights, sums = softmax(scores, HDA)
        result = mixed(weights, twice) / sums
        scores = following
        block = moved(turn_of(i))
        upper = [result[j * part_rows : (j + 1) * part_rows] for j in reversed(range(n // 2))]
        packed = jnp.where(low, jnp.concatenate(upper, 0), result[half:]).astype(bf16)
        o_rest[pl.ds(block, 1), n * part_few :, :] = packed[None]
        to_plane(1, i)

        @pl.when(inner)
        def _():
            to_across(1, i)
            to_mate(1, i)

    r_rest[pl.ds(mine, 1)] = o_rest[pl.ds(h, 1)]
    with scope("T4weights"):
        @pl.when(inner)
        def _():
            for i in range(3):
                pass_weights(i)

    ends, peers = [lax.rem(w, 2)], [lax.rem(w + 1, 2)]
    with scope("T4forward"):
        for i in range(n):
            to_plane(2, i)

        @pl.when(outer)
        def _():
            for kind in (1, 2):
                for i in range(n):
                    to_mate(kind, i)
            exchange_rest(across_side)

        @pl.when(inner)
        def _():
            for i in range(n):
                forward(1, i, ends)
            for i in range(n):
                to_across(2, i)
                to_mate(2, i)
            for kind, ks in ((1, peers), (2, ends), (2, peers)):
                for i in range(n):
                    forward(kind, i, ks)

    with scope("T5pass"):
        @pl.when(outer)
        def _():
            for i in range(3):
                pass_weights(i)

    with scope("T5w"):
        own[3].wait()
        own[4].wait()
        settle_weights(0)
    with scope("T6self"):
        gathered(0)
    heads = n * n
    joined = jnp.concatenate([r_self[s] for s in range(heads)], 1)
    totals[...] = jnp.dot(
        joined, ws_all[...].reshape(-1, ws.shape[1]), preferred_element_type=jnp.float32
    )

    @pl.when(outer)
    def _():
        for kind in (1, 2):
            for i in range(n):
                to_across(kind, i)

    with scope("T7w"):
        settle_weights(1)

    def rows_of(ref, block, size):
        return ref.at[pl.ds(pl.multiple_of(block * size, size), size)]

    def deliver(c, b):
        source, out, size = ((sum_v, out_v, part_rows), (sum_a, out_a, part_few))[c]
        piece, target = rows_of(source, b, size), rows_of(out, h, size)
        away = (w != b) | (w != h)

        @pl.when(away)
        def _():
            remote(
                piece, target, e_send.at[c], e_recv.at[c], {"wide": b, "heads": w}
            ).start()

        @pl.when(jnp.logical_not(away))
        def _():
            pltpu.make_async_copy(piece, target, e_recv.at[c]).start()

    flat_c = wc_all[...].reshape(-1, wc.shape[1])
    for u in range(2):
        with scope("T8gather%d" % u):
            gathered(1 + u)
        begin = n * part_few + u * (half // 2)
        piece = slice(begin, begin + half // 2)
        crossed = jnp.concatenate(
            [
                jnp.concatenate([r_rest[s, piece, :HDA] for s in range(heads)], 1),
                jnp.concatenate([r_rest[s, piece, HDA:] for s in range(heads)], 1),
            ],
            0,
        )
        products = jnp.dot(crossed, flat_c, preferred_element_type=jnp.float32)
        size = half // 2
        for k in range(2):
            b = (n // 2 - 1 - u, n // 2 + u)[k]
            where = slice(b * size, (b + 1) * size)
            sum_v[where, :] = (
                totals[where, :] + products[k * size : (k + 1) * size, :]
            ).astype(bf16)
        if u == 1:
            with scope("T8sent"):
                @pl.when(inner)
                def _():
                    for kind in range(3):
                        settle(many(kind, 2 * n), r_send.at[kind])

        for b in (n // 2 - 1 - u, n // 2 + u):
            deliver(0, b)
        if u == 0:
            with scope("T8weights"):
                settle_weights(2)
            audio_joined = jnp.concatenate([r_rest[s, : n * part_few, :] for s in range(heads)], 1)
            sum_a[...] = jnp.dot(
                audio_joined, wa_all[...].reshape(-1, aso.shape[1]),
                preferred_element_type=jnp.float32,
            ).astype(bf16)
            for b in range(n):
                deliver(1, b)

    with scope("T9results"):
        settle(out_v, e_recv.at[0])
        settle(out_a, e_recv.at[1])

    with scope("TBsends"):
        for i, target in enumerate((q_all, k_all, v_all, p_all)):
            settle(target.at[: n - 1], a_send.at[i])
        for i in range(3):
            settle(part_of(targets[i].at[h], g), w_send.at[i, 0])
            settle(targets[i].at[h], w_send.at[i, 1])
            settle(part_of(targets[i].at[h], g), w_send.at[i, 2])
            settle(targets[i].at[h], w_send.at[i, 3])
        for kind in range(3):
            settle(many(kind, n - 1), x_send.at[kind])
            settle(many(kind, 2 * n), z_send.at[kind])
        for c, (ref, size) in enumerate(((sum_v, part_rows), (sum_a, part_few))):
            settle(ref.at[: (n - 1) * size], e_send.at[c])

            @pl.when(w != h)
            def _():
                settle(ref.at[:size], e_send.at[c])


def shards(*args):
    n = lax.axis_size("wide")
    count = lax.axis_size("heads")
    head_count = args[2].shape[1] // HDV
    paired = lax.axis_size("groups") == 2
    if not (paired and n == count == head_count == 2 * REACH and args[5].shape[0] % (16 * n) == 0):
        return general_shards(*args)
    (video_hidden, audio_hidden, vq, vk, vv, aq, ak, av, cvq, cak, cav, caq, cvk, cvv,
     vso, vco, aso, aco, table) = args
    rows, few = vq.shape[0], aq.shape[0]
    depth = rows + rows // 2 + 3 * few
    anywhere = pl.BlockSpec(memory_space=pl.ANY)
    bf16, f32 = jnp.bfloat16, jnp.float32
    rest = rows // 2 + few
    dma = pltpu.SemaphoreType.DMA
    video_sum, audio_sum = pl.pallas_call(
        functools.partial(joint_kernel, n),
        out_shape=(
            jax.ShapeDtypeStruct(video_hidden.shape, bf16),
            jax.ShapeDtypeStruct(audio_hidden.shape, bf16),
        ),
        in_specs=[pl.BlockSpec(memory_space=pltpu.HBM)] * 16 + [pl.BlockSpec(memory_space=pltpu.SMEM)],
        out_specs=(anywhere, anywhere),
        scratch_shapes=[
            pltpu.VMEM((n, rows, HDV), bf16),
            pltpu.VMEM((n, rows, HDV), bf16),
            pltpu.VMEM((n, rows, HDV), bf16),
            pltpu.VMEM((3,) + vq.shape, bf16),
            pltpu.VMEM((3,) + cvq.shape, bf16),
            pltpu.VMEM((6,) + aq.shape, bf16),
            pltpu.VMEM((n, depth, 2 * HDA), bf16),
            pltpu.VMEM((n, depth, 2 * HDA), bf16),
            pltpu.VMEM((n,) + vso.shape, bf16),
            pltpu.VMEM((n,) + vco.shape, bf16),
            pltpu.VMEM((n, 2 * aso.shape[0], aso.shape[1]), bf16),
            pltpu.VMEM((rows, n * few), f32),
            pltpu.VMEM((n * few, n * rows), f32),
            pltpu.VMEM((n, rows, HDV), bf16),
            pltpu.VMEM((n, rest, 2 * HDA), bf16),
            pltpu.VMEM((n * n, rows, HDV), bf16),
            pltpu.VMEM((n * n, rest, 2 * HDA), bf16),
            pltpu.VMEM(video_hidden.shape, f32),
            pltpu.VMEM(video_hidden.shape, bf16),
            pltpu.VMEM(audio_hidden.shape, bf16),
            dma((4,)), dma((4,)),
            dma((3, 4)), dma((3, 4)),
            dma((3,)), dma((3,)),
            dma((3,)), dma((3, n, 2)), dma((3,)), dma((3,)),
            dma((2,)), dma((2,)),
            dma((18,)),
        ],
        compiler_params=pltpu.CompilerParams(
            collective_id=0, has_side_effects=True, vmem_limit_bytes=48 * 1024 * 1024
        ),
        name="joint",
    )(
        *(
            pltpu.with_memory_space_constraint(operand, pltpu.HBM)
            for operand in (
                vq, vk, vv, cvq, cvk, cvv, aq, ak, av, caq, cak, cav, vso, vco, aso, aco, table
            )
        )
    )
    video_out = video_hidden.astype(f32) + video_sum.astype(f32)
    audio_out = audio_hidden.astype(f32) + audio_sum.astype(f32)
    return (video_out.astype(bf16), audio_out.astype(bf16))


def solution(mesh):
    placed = (
        P(("groups", "wide"), "heads"),
        P(("groups", "wide"), "heads"),
        P(("groups", "wide"), "heads"),
        P(("groups", "wide"), "heads"),
        P(("groups", "wide"), "heads"),
        P(("groups", "wide"), "heads"),
        P(("groups", "wide"), "heads"),
        P(("groups", "wide"), "heads"),
        P(("groups", "wide"), "heads"),
        P(("groups", "wide"), "heads"),
        P(("groups", "wide"), "heads"),
        P(("groups", "wide"), "heads"),
        P(("groups", "wide"), "heads"),
        P(("groups", "wide"), "heads"),
        P("heads", "wide"),
        P("heads", "wide"),
        P("heads", "wide"),
        P("heads", "wide"),
        P("groups", None),
    )
    return jax.shard_map(
        shards,
        mesh=mesh,
        in_specs=placed,
        out_specs=(P(("groups", "wide"), "heads"), P(("groups", "wide"), "heads")),
        check_vma=False,
    )
```

```python
import contextlib
import functools
import math

import jax
import jax.numpy as jnp
from jax import lax
from jax.experimental import pallas as pl
from jax.experimental.pallas import tpu as pltpu
from jax.sharding import PartitionSpec as P

HDV = 128
HDA = 64
REACH = 2


def passed_along(value, axis, by):
    length = lax.axis_size(axis)
    pairs = [(i, i + by) for i in range(length) if 0 <= i + by < length]
    return lax.ppermute(value, axis, pairs)


def empty_state(row_count, head_count, head_size):
    return (
        jnp.full((head_count, row_count), -1e30, jnp.float32),
        jnp.zeros((head_count, row_count), jnp.float32),
        jnp.zeros((head_count, row_count, head_size), jnp.float32),
    )


def absorb(state, queries, key_rows, value_rows, head_size, allowed):
    maxima, totals, running = state
    head_count = queries.shape[1] // head_size
    query_heads = queries.reshape(queries.shape[0], head_count, head_size)
    key_heads = key_rows.reshape(key_rows.shape[0], head_count, head_size)
    value_heads = value_rows.reshape(value_rows.shape[0], head_count, head_size)
    scores = jnp.einsum(
        "qhd,khd->hqk", query_heads, key_heads, preferred_element_type=jnp.float32
    ) * (1.0 / math.sqrt(head_size))
    if allowed is not None:
        scores = jnp.where(allowed[None, None, :], scores, -1e30)
    new_peak = jnp.maximum(maxima, jnp.max(scores, axis=2))
    weights = jnp.exp(scores - new_peak[:, :, None])
    if allowed is not None:
        weights = jnp.where(allowed[None, None, :], weights, 0.0)
    rescale = jnp.exp(maxima - new_peak)
    totals = totals * rescale + jnp.sum(weights, axis=2)
    running = running * rescale[:, :, None] + jnp.einsum(
        "hqk,khd->hqd",
        weights.astype(jnp.bfloat16),
        value_heads,
        preferred_element_type=jnp.float32,
    )
    return (new_peak, totals, running)


def finish(state, head_size):
    maxima, totals, running = state
    result = running / totals[:, :, None]
    return (
        result.transpose(1, 0, 2)
        .reshape(result.shape[1], result.shape[0] * head_size)
        .astype(jnp.bfloat16)
    )


def permitted(key_blocks, position, table_row, wide_count):
    offsets = key_blocks - position + REACH
    matches = (offsets[:, None] == jnp.arange(2 * REACH + 1, dtype=jnp.int32)[None, :]) & (
        table_row[None, :] > 0
    )
    inside = (key_blocks >= 0) & (key_blocks < wide_count)
    return jnp.any(matches, axis=1) & inside


def general_shards(
    video_hidden,
    audio_hidden,
    video_query,
    video_key,
    video_value,
    audio_query,
    audio_key,
    audio_value,
    cross_video_query,
    cross_audio_key,
    cross_audio_value,
    cross_audio_query,
    cross_video_key,
    cross_video_value,
    video_self_out,
    video_cross_out,
    audio_self_out,
    audio_cross_out,
    intersection,
):
    position = lax.axis_index("wide")
    wide_count = lax.axis_size("wide")
    video_count = video_query.shape[0]
    audio_count = audio_query.shape[0]
    head_count = video_query.shape[1] // HDV
    video_start = empty_state(video_count, head_count, HDV)
    audio_start = empty_state(audio_count, head_count, HDA)
    carried = (video_start, audio_start)
    portion = (
        lax.all_gather(video_key, "wide", axis=0, tiled=True),
        lax.all_gather(video_value, "wide", axis=0, tiled=True),
        lax.all_gather(audio_key, "wide", axis=0, tiled=True),
        lax.all_gather(audio_value, "wide", axis=0, tiled=True),
    )
    video_state = absorb(carried[0], video_query, portion[0], portion[1], HDV, None)
    audio_state = absorb(carried[1], audio_query, portion[2], portion[3], HDA, None)
    table_row = lax.dynamic_slice_in_dim(intersection, position, 1, 0)[0]
    padded_table = jnp.pad(intersection, ((REACH, REACH), (0, 0)))
    flag_row = jnp.diagonal(
        jnp.fliplr(lax.dynamic_slice_in_dim(padded_table, position, 2 * REACH + 1, 0))
    )
    stacked = jnp.concatenate(
        [cross_audio_key, cross_audio_value, cross_video_key, cross_video_value], 0
    )

    def take_cross(carried, portion, block):
        audio_keys = portion[:audio_count]
        audio_values = portion[audio_count : 2 * audio_count]
        video_keys = portion[2 * audio_count : 2 * audio_count + video_count]
        video_values = portion[2 * audio_count + video_count :]
        audio_blocks = jnp.full((audio_count,), block, jnp.int32)
        video_blocks = jnp.full((video_count,), block, jnp.int32)
        return (
            absorb(
                carried[0],
                cross_video_query,
                audio_keys,
                audio_values,
                HDA,
                permitted(audio_blocks, position, table_row, wide_count),
            ),
            absorb(
                carried[1],
                cross_audio_query,
                video_keys,
                video_values,
                HDA,
                permitted(video_blocks, position, flag_row, wide_count),
            ),
        )

    cross_start = (
        empty_state(video_count, head_count, HDA),
        empty_state(audio_count, head_count, HDA),
    )
    carried = take_cross(cross_start, stacked, position)
    for offset in range(-REACH, REACH + 1):
        if offset != 0:
            nearby = passed_along(stacked, "wide", -offset)
            carried = take_cross(carried, nearby, position + offset)
    to_video, to_audio = carried
    video_joined = jnp.concatenate([finish(video_state, HDV), finish(to_video, HDA)], 1)
    audio_joined = jnp.concatenate([finish(audio_state, HDA), finish(to_audio, HDA)], 1)
    video_weights = jnp.concatenate([video_self_out, video_cross_out], 0)
    audio_weights = jnp.concatenate([audio_self_out, audio_cross_out], 0)
    video_terms = jnp.dot(
        video_joined,
        lax.all_gather(video_weights, "wide", axis=1, tiled=True),
        preferred_element_type=jnp.float32,
    )
    audio_terms = jnp.dot(
        audio_joined,
        lax.all_gather(audio_weights, "wide", axis=1, tiled=True),
        preferred_element_type=jnp.float32,
    )
    video_sum, audio_sum = (
        lax.psum_scatter(
            video_terms.astype(jnp.bfloat16), "heads", scatter_dimension=1, tiled=True
        ).astype(jnp.float32),
        lax.psum_scatter(
            audio_terms.astype(jnp.bfloat16), "heads", scatter_dimension=1, tiled=True
        ).astype(jnp.float32),
    )
    video_out = (video_hidden.astype(jnp.float32) + video_sum).astype(jnp.bfloat16)
    audio_out = (audio_hidden.astype(jnp.float32) + audio_sum).astype(jnp.bfloat16)
    return (video_out, audio_out)


NT = (((1,), (1,)), ((), ()))
MESH = pl.DeviceIdType.MESH


def scope(name):
    return contextlib.nullcontext()


def softmax(scores, head_size):
    factor = math.log2(math.e) / math.sqrt(head_size)
    weights = jnp.exp2((scores - jnp.max(scores, axis=1, keepdims=True)) * factor)
    return weights.astype(jnp.bfloat16), jnp.sum(weights, axis=1, keepdims=True)


def scored(queries, keys):
    return lax.dot_general(queries, keys, NT, preferred_element_type=jnp.float32)


def mixed(weights, values):
    return jnp.dot(weights, values, preferred_element_type=jnp.float32)


def joint_kernel(
    n,
    vq, vk, vv, cvq, cvk, cvv, aq, ak, av, caq, cak, cav, ws, wc, aso, aco, table,
    out_v, out_a,
    q_all, k_all, v_all, self_stage, wide_stage, few_stage, pack, p_all, ws_all, wc_all, wa_all,
    tall_bias, wide_bias, o_self, o_rest, r_self, r_rest, totals, sum_v, sum_a,
    a_send, a_recv, w_send, w_recv, x_send, x_recv, z_send, z_recv, m_recv, r_send,
    e_send, e_recv, local,
):
    g = lax.axis_index("groups")
    w = lax.axis_index("wide")
    h = lax.axis_index("heads")
    rows, few = vq.shape[0], aq.shape[0]
    half = rows // 2
    part_rows, part_few = rows // n, few // n
    depth = p_all.shape[1]
    bf16 = jnp.bfloat16

    mine = h * n + w
    side = w // (n // 2)
    mate = w + 1 - 2 * lax.rem(w, 2)
    across_side = n // 2 - side
    far_start = (1 - side) * (n // 2)
    inner = (w > 0) & (w < n - 1)

    def place(dw, dh):
        return {"wide": lax.rem(w + dw, n), "heads": lax.rem(h + dh, n)}

    def remote(source, target, send, recv, device):
        return pltpu.make_async_remote_copy(
            src_ref=source, dst_ref=target, send_sem=send, recv_sem=recv,
            device_id=device, device_id_type=MESH,
        )

    others = [(d, 0) for d in range(1, n)] + [(0, d) for d in range(1, n)]
    barrier = pltpu.get_barrier_semaphore()
    for dw, dh in others:
        pl.semaphore_signal(barrier, inc=1, device_id=place(dw, dh), device_id_type=MESH)
    twin = {"groups": 1 - g}
    pl.semaphore_signal(barrier, inc=1, device_id=twin, device_id_type=MESH)

    def settle(piece, sem):
        pltpu.make_async_copy(piece, piece, sem).wait()

    def head_cols(ref, who):
        return ref.at[:, pl.ds(pl.multiple_of(who * HDV, HDV), HDV)]

    def start(copies):
        for copy in copies:
            copy.start()
        return copies

    streams = ((vq, q_all), (vk, k_all), (vv, v_all))
    self_staged = start(
        [
            pltpu.make_async_copy(source, self_stage.at[i], local.at[15 + i])
            for i, (source, _) in enumerate(streams)
        ]
    )
    staged = start(
        [
            pltpu.make_async_copy(source, wide_stage.at[i], local.at[i])
            for i, source in enumerate((cvq, cvk, cvv))
        ]
        + [
            pltpu.make_async_copy(source, few_stage.at[i], local.at[3 + i])
            for i, source in enumerate((cak, caq, av, aq, cav, ak))
        ]
    )
    own = start(
        [
            pltpu.make_async_copy(head_cols(source, w), target.at[w], local.at[9 + i])
            for i, (source, target) in enumerate(streams)
        ]
        + [
            pltpu.make_async_copy(source, target.at[h], local.at[12 + i])
            for i, (source, target) in enumerate(((ws, ws_all), (wc, wc_all)))
        ]
    )
    for j in range(n):
        for k, source in enumerate((aso, aco)):
            at = (2 * j + k) * HDA
            pltpu.make_async_copy(
                source.at[j * HDA : (j + 1) * HDA], wa_all.at[h, at : at + HDA], local.at[14]
            ).start()
    own.append(pltpu.make_async_copy(wa_all.at[h], wa_all.at[h], local.at[14]))
    for copy in self_staged:
        copy.wait()
    with scope("T0barrier"):
        pl.semaphore_wait(barrier, len(others) + 1)

    far_end = (1 - side) * (n - 1)

    def exchange(target):
        for i, (_, landing) in enumerate(streams):
            remote(
                head_cols(self_stage.at[i], target), landing.at[w], a_send.at[i], a_recv.at[i],
                {"wide": target, "heads": h},
            ).start()

    near = jnp.where(inner, across_side, mate)
    last = jnp.where(inner, mate, across_side)
    for target in (far_end, near, last):
        exchange(target)

    targets = (ws_all, wc_all, wa_all)
    sources = (ws, wc, wa_all.at[h])
    partner = {"wide": w, "heads": h + 1 - 2 * lax.rem(h, 2)}
    opposite = lax.rem(h + n // 2, n)

    def part_of(ref, which):
        size = ref.shape[0] // 2
        return ref.at[pl.ds(pl.multiple_of(which * size, size), size)]

    def send_weights(i):
        remote(
            part_of(sources[i], g), part_of(targets[i].at[h], g),
            w_send.at[i, 0], w_recv.at[i, 0], {"wide": w, "heads": opposite},
        ).start()

    def share_weights(i):
        remote(sources[i], targets[i].at[h], w_send.at[i, 1], w_recv.at[i, 1], partner).start()

    def swap_weights(i):
        piece = part_of(targets[i].at[opposite], g)
        settle(piece, w_recv.at[i, 0])
        remote(piece, piece, w_send.at[i, 2], w_recv.at[i, 2], twin).start()

    def pass_weights(i):
        slot = targets[i].at[opposite]
        settle(part_of(slot, 1 - g), w_recv.at[i, 2])
        remote(slot, slot, w_send.at[i, 3], w_recv.at[i, 3], partner).start()

    def settle_weights(i):
        settle(targets[i].at[h], w_recv.at[i, 1])
        settle(targets[i].at[h], w_recv.at[i, 3])

    for i in range(2):
        send_weights(i)
        share_weights(i)

    for copy in staged:
        copy.wait()
    for j in range(n):
        cols = slice(j * HDA, (j + 1) * HDA)
        pack[j, :rows, :] = jnp.concatenate([wide_stage[0, :, cols], wide_stage[1, :, cols]], 1)
        pack[j, rows : rows + half, :] = jnp.concatenate(
            [wide_stage[2, :half, cols], wide_stage[2, half:, cols]], 1
        )
        for k in range(3):
            at = rows + half + k * few
            pack[j, at : at + few, :] = jnp.concatenate(
                [few_stage[2 * k, :, cols], few_stage[2 * k + 1, :, cols]], 1
            )

    def exchange_rest(target):
        remote(
            pack.at[target], p_all.at[w], a_send.at[3], a_recv.at[3], {"wide": target, "heads": h}
        ).start()

    outer = jnp.logical_not(inner)
    exchange_rest(mate)

    @pl.when(outer)
    def _():
        exchange_rest(far_end)


    own_pack = pltpu.make_async_copy(pack.at[w], p_all.at[w], local.at[0])
    own_pack.start()
    own.pop().wait()
    send_weights(2)
    share_weights(2)

    for i in range(n):
        for j in range(n):
            column = j - i + REACH
            drop = jnp.float32(-1e30)
            if 0 <= column < table.shape[1]:
                drop = jnp.where(table[i, column] > 0, jnp.float32(0.0), drop)
            tall_bias[i * part_rows : (i + 1) * part_rows, j * few : (j + 1) * few] = jnp.full(
                (part_rows, few), drop
            )
            wide_bias[j * few : (j + 1) * few, i * rows : (i + 1) * rows] = jnp.full(
                (few, rows), drop
            )

    splits = (part_few * n + half // 2, half // 2)
    starts = (0, splits[0])

    def chunk(ref, kind):
        if kind == 0:
            return ref
        return ref.at[pl.ds(starts[kind - 1], splits[kind - 1])]

    def buffers(kind):
        return (o_self, r_self) if kind == 0 else (o_rest, r_rest)

    orders = ((1, 0, 2, 3), (2, 3, 1, 0))

    def moved(e):
        return lax.rem(h // 2 + e // 2, 2) * 2 + lax.rem(h + e, 2)

    def turn_of(i):
        return orders[0][i] + lax.rem(w, 2) * (orders[1][i] - orders[0][i])

    def outgoing(kind, i):
        source, landing = buffers(kind)
        d = turn_of(i)
        part = moved(d)
        return d, part, chunk(source.at[part], kind), chunk(landing.at[mine], kind)

    def to_plane(kind, i):
        _, part, piece, where = outgoing(kind, i)

        @pl.when(part != h)
        def _():
            remote(
                piece, where, x_send.at[kind], x_recv.at[kind], {"wide": w, "heads": part}
            ).start()

    def to_across(kind, i):
        d, part, piece, where = outgoing(kind, i)
        remote(
            piece, where, z_send.at[kind], z_recv.at[kind, d, lax.rem(w, 2)],
            {"wide": across_side, "heads": part},
        ).start()

    def to_mate(kind, i):
        _, part, piece, where = outgoing(kind, i)
        remote(
            piece, where, z_send.at[kind], m_recv.at[kind], {"wide": mate, "heads": part}
        ).start()

    def far_piece(kind, d, k):
        return chunk(buffers(kind)[1].at[moved(d) * n + far_start + k], kind)

    def forward(kind, i, ks):
        for k in ks:
            d = orders[0][i] + k * (orders[1][i] - orders[0][i])
            piece = far_piece(kind, d, k)
            settle(piece, z_recv.at[kind, d, k])
            remote(
                piece, piece, r_send.at[kind], z_recv.at[kind, d, k],
                {"wide": mate, "heads": h},
            ).start()

    def many(kind, count):
        landing = buffers(kind)[1]
        if kind == 0:
            return landing.at[:count]
        return landing.at[:count, pl.ds(starts[kind - 1], splits[kind - 1])]

    def gathered(kind):
        settle(many(kind, n - 1), x_recv.at[kind])
        if kind != 1:
            settle(many(kind, n), m_recv.at[kind])
        else:
            @pl.when(inner)
            def _():
                settle(many(kind, n), m_recv.at[kind])


        @pl.when(outer)
        def _():
            for d in range(n):
                for k in range(2):
                    settle(far_piece(kind, d, k), z_recv.at[kind, d, k])

    with scope("T1self"):
        for i, target in enumerate((q_all, k_all, v_all)):
            own[i].wait()
            settle(target.at[: n - 1], a_recv.at[i])

    @pl.when(inner)
    def _():
        exchange_rest(far_end)

    keys = k_all[...].reshape(n * rows, HDV)
    values = v_all[...].reshape(n * rows, HDV)

    def self_scores(i):
        at = pl.multiple_of(moved(turn_of(i)) * part_rows, part_rows)
        return scored(q_all[:, pl.ds(at, part_rows), :].reshape(rows, HDV), keys)

    scores = self_scores(0)
    for i in range(n):
        following = self_scores(i + 1) if i + 1 < n else None
        weights, sums = softmax(scores, HDV)
        result = (mixed(weights, values) / sums).astype(bf16)
        scores = following
        o_self[pl.ds(moved(turn_of(i)), 1)] = result[None]
        to_plane(0, i)
        to_across(0, i)
        to_mate(0, i)
    r_self[pl.ds(mine, 1)] = o_self[pl.ds(h, 1)]

    @pl.when(inner)
    def _():
        exchange_rest(across_side)

    with scope("T2weights"):
        swap_weights(0)
        swap_weights(1)
    with scope("T2forward"):
        @pl.when(inner)
        def _():
            for k in (lax.rem(w, 2), lax.rem(w + 1, 2)):
                for i in range(n):
                    forward(0, i, [k])
            with scope("T2pass"):
                pass_weights(0)
                pass_weights(1)

    swap_weights(2)
    with scope("T3rest"):
        own_pack.wait()
        settle(p_all.at[: n - 1], a_recv.at[3])

    at = rows + half
    lane = lax.broadcasted_iota(jnp.int32, (n * few, 2 * HDA), 1)
    left = lane < HDA
    both = p_all[:, :rows, :].reshape(n * rows, 2 * HDA)
    vals = p_all[:, rows:at, :].reshape(n * half, 2 * HDA)
    keyed = p_all[:, at : at + few, :].reshape(n * few, 2 * HDA)
    asked = p_all[:, at + few : at + 2 * few, :].reshape(n * few, 2 * HDA)
    third = p_all[:, at + 2 * few : depth, :].reshape(n * few, 2 * HDA)
    zero = jnp.zeros_like(keyed)
    key_left = jnp.where(left, keyed, zero)
    query_right = jnp.where(left, zero, keyed)
    key_right = jnp.where(left, zero, third)
    twice = jnp.concatenate([third[:, :HDA], third[:, :HDA]], 1)

    scores_a = scored(asked, key_right)
    scores_c = scored(query_right, both) + wide_bias[...]
    weights, sums = softmax(scores_a, HDA)
    audio_own = mixed(weights, asked) / sums
    weights, sums = softmax(scores_c, HDA)
    upper = jnp.concatenate([weights[:, j * rows : j * rows + half] for j in range(n)], 1)
    lower = jnp.concatenate([weights[:, j * rows + half : (j + 1) * rows] for j in range(n)], 1)
    audio_other = (pltpu.roll(mixed(upper, vals), HDA, 1) + mixed(lower, vals)) / sums
    audio = jnp.where(left, audio_own, audio_other).astype(bf16)
    for t in range(n):
        o_rest[t, : n * part_few, :] = jnp.concatenate(
            [audio[j * few + t * part_few : j * few + (t + 1) * part_few, :] for j in range(n)], 0
        )
    def cross_scores(i):
        begin = pl.multiple_of(moved(turn_of(i)) * part_rows, part_rows)
        queries = p_all[:, pl.ds(begin, part_rows), :].reshape(rows, 2 * HDA)
        return scored(queries, key_left) + tall_bias[...]

    ends, peers = [lax.rem(w, 2)], [lax.rem(w + 1, 2)]
    low = lax.broadcasted_iota(jnp.int32, (half, 2 * HDA), 1) < HDA
    scores = cross_scores(0)
    for i in range(n):
        following = cross_scores(i + 1) if i + 1 < n else None
        weights, sums = softmax(scores, HDA)
        result = mixed(weights, twice) / sums
        scores = following
        block = moved(turn_of(i))
        upper = [result[j * part_rows : (j + 1) * part_rows] for j in reversed(range(n // 2))]
        packed = jnp.where(low, jnp.concatenate(upper, 0), result[half:]).astype(bf16)
        o_rest[pl.ds(block, 1), n * part_few :, :] = packed[None]
        to_plane(1, i)

        @pl.when(inner)
        def _():
            to_across(1, i)
            to_mate(1, i)

    r_rest[pl.ds(mine, 1)] = o_rest[pl.ds(h, 1)]
    ends, peers = [lax.rem(w, 2)], [lax.rem(w + 1, 2)]
    with scope("T4outer"):
        for i in range(n):
            to_plane(2, i)

        @pl.when(outer)
        def _():
            for kind in (1, 2):
                for i in range(n):
                    to_mate(kind, i)
            exchange_rest(across_side)
            for i in range(3):
                pass_weights(i)

        @pl.when(inner)
        def _():
            for i in range(n):
                to_across(2, i)

    with scope("T5w"):
        own[3].wait()
        own[4].wait()
        settle_weights(0)
    with scope("T6self"):
        gathered(0)

    @pl.when(outer)
    def _():
        for i in range(n):
            to_across(1, i)

    heads = n * n
    joined = jnp.concatenate([r_self[s] for s in range(heads)], 1)
    totals[...] = jnp.dot(
        joined, ws_all[...].reshape(-1, ws.shape[1]), preferred_element_type=jnp.float32
    )

    @pl.when(outer)
    def _():
        with scope("T7m"):
            settle(many(1, n), m_recv.at[1])
        for i in range(n):
            to_across(2, i)

    with scope("T7forward"):
        @pl.when(inner)
        def _():
            for i in range(n):
                forward(1, i, ends)
            for i in range(n):
                to_mate(2, i)
            pass_weights(2)
            for i in range(n):
                forward(1, i, peers)

    with scope("T7w"):
        settle_weights(1)

    def rows_of(ref, block, size):
        return ref.at[pl.ds(pl.multiple_of(block * size, size), size)]

    def deliver(c, b):
        source, out, size = ((sum_v, out_v, part_rows), (sum_a, out_a, part_few))[c]
        piece, target = rows_of(source, b, size), rows_of(out, h, size)
        away = (w != b) | (w != h)

        @pl.when(away)
        def _():
            remote(
                piece, target, e_send.at[c], e_recv.at[c], {"wide": b, "heads": w}
            ).start()

        @pl.when(jnp.logical_not(away))
        def _():
            pltpu.make_async_copy(piece, target, e_recv.at[c]).start()

    flat_c = wc_all[...].reshape(-1, wc.shape[1])
    for u in range(2):
        with scope("T8gather%d" % u):
            gathered(1 + u)
        begin = n * part_few + u * (half // 2)
        piece = slice(begin, begin + half // 2)
        crossed = jnp.concatenate(
            [
                jnp.concatenate([r_rest[s, piece, :HDA] for s in range(heads)], 1),
                jnp.concatenate([r_rest[s, piece, HDA:] for s in range(heads)], 1),
            ],
            0,
        )
        products = jnp.dot(crossed, flat_c, preferred_element_type=jnp.float32)
        size = half // 2
        for k in range(2):
            b = (n // 2 - 1 - u, n // 2 + u)[k]
            where = slice(b * size, (b + 1) * size)
            sum_v[where, :] = (
                totals[where, :] + products[k * size : (k + 1) * size, :]
            ).astype(bf16)
        if u == 1:
            with scope("T8sent"):
                @pl.when(inner)
                def _():
                    for kind in range(3):
                        settle(many(kind, 2 * n), r_send.at[kind])

        for b in (n // 2 - 1 - u, n // 2 + u):
            deliver(0, b)
        if u == 0:
            with scope("T8forward"):
                @pl.when(inner)
                def _():
                    for ks in (ends, peers):
                        for i in range(n):
                            forward(2, i, ks)

            with scope("T8weights"):
                settle_weights(2)
            audio_joined = jnp.concatenate([r_rest[s, : n * part_few, :] for s in range(heads)], 1)
            sum_a[...] = jnp.dot(
                audio_joined, wa_all[...].reshape(-1, aso.shape[1]),
                preferred_element_type=jnp.float32,
            ).astype(bf16)
            for b in range(n):
                deliver(1, b)

    with scope("T9results"):
        settle(out_v, e_recv.at[0])
        settle(out_a, e_recv.at[1])

    with scope("TBsends"):
        for i, target in enumerate((q_all, k_all, v_all, p_all)):
            settle(target.at[: n - 1], a_send.at[i])
        for i in range(3):
            settle(part_of(targets[i].at[h], g), w_send.at[i, 0])
            settle(targets[i].at[h], w_send.at[i, 1])
            settle(part_of(targets[i].at[h], g), w_send.at[i, 2])
            settle(targets[i].at[h], w_send.at[i, 3])
        for kind in range(3):
            settle(many(kind, n - 1), x_send.at[kind])
            settle(many(kind, 2 * n), z_send.at[kind])
        for c, (ref, size) in enumerate(((sum_v, part_rows), (sum_a, part_few))):
            settle(ref.at[: (n - 1) * size], e_send.at[c])

            @pl.when(w != h)
            def _():
                settle(ref.at[:size], e_send.at[c])


def shards(*args):
    n = lax.axis_size("wide")
    count = lax.axis_size("heads")
    head_count = args[2].shape[1] // HDV
    paired = lax.axis_size("groups") == 2
    if not (paired and n == count == head_count == 2 * REACH and args[5].shape[0] % (16 * n) == 0):
        return general_shards(*args)
    (video_hidden, audio_hidden, vq, vk, vv, aq, ak, av, cvq, cak, cav, caq, cvk, cvv,
     vso, vco, aso, aco, table) = args
    rows, few = vq.shape[0], aq.shape[0]
    depth = rows + rows // 2 + 3 * few
    anywhere = pl.BlockSpec(memory_space=pl.ANY)
    bf16, f32 = jnp.bfloat16, jnp.float32
    rest = rows // 2 + few
    dma = pltpu.SemaphoreType.DMA
    video_sum, audio_sum = pl.pallas_call(
        functools.partial(joint_kernel, n),
        out_shape=(
            jax.ShapeDtypeStruct(video_hidden.shape, bf16),
            jax.ShapeDtypeStruct(audio_hidden.shape, bf16),
        ),
        in_specs=[pl.BlockSpec(memory_space=pltpu.HBM)] * 16 + [pl.BlockSpec(memory_space=pltpu.SMEM)],
        out_specs=(anywhere, anywhere),
        scratch_shapes=[
            pltpu.VMEM((n, rows, HDV), bf16),
            pltpu.VMEM((n, rows, HDV), bf16),
            pltpu.VMEM((n, rows, HDV), bf16),
            pltpu.VMEM((3,) + vq.shape, bf16),
            pltpu.VMEM((3,) + cvq.shape, bf16),
            pltpu.VMEM((6,) + aq.shape, bf16),
            pltpu.VMEM((n, depth, 2 * HDA), bf16),
            pltpu.VMEM((n, depth, 2 * HDA), bf16),
            pltpu.VMEM((n,) + vso.shape, bf16),
            pltpu.VMEM((n,) + vco.shape, bf16),
            pltpu.VMEM((n, 2 * aso.shape[0], aso.shape[1]), bf16),
            pltpu.VMEM((rows, n * few), f32),
            pltpu.VMEM((n * few, n * rows), f32),
            pltpu.VMEM((n, rows, HDV), bf16),
            pltpu.VMEM((n, rest, 2 * HDA), bf16),
            pltpu.VMEM((n * n, rows, HDV), bf16),
            pltpu.VMEM((n * n, rest, 2 * HDA), bf16),
            pltpu.VMEM(video_hidden.shape, f32),
            pltpu.VMEM(video_hidden.shape, bf16),
            pltpu.VMEM(audio_hidden.shape, bf16),
            dma((4,)), dma((4,)),
            dma((3, 4)), dma((3, 4)),
            dma((3,)), dma((3,)),
            dma((3,)), dma((3, n, 2)), dma((3,)), dma((3,)),
            dma((2,)), dma((2,)),
            dma((18,)),
        ],
        compiler_params=pltpu.CompilerParams(
            collective_id=0, has_side_effects=True, vmem_limit_bytes=48 * 1024 * 1024
        ),
        name="joint",
    )(
        *(
            pltpu.with_memory_space_constraint(operand, pltpu.HBM)
            for operand in (
                vq, vk, vv, cvq, cvk, cvv, aq, ak, av, caq, cak, cav, vso, vco, aso, aco, table
            )
        )
    )
    video_out = video_hidden.astype(f32) + video_sum.astype(f32)
    audio_out = audio_hidden.astype(f32) + audio_sum.astype(f32)
    return (video_out.astype(bf16), audio_out.astype(bf16))


def solution(mesh):
    placed = (
        P(("groups", "wide"), "heads"),
        P(("groups", "wide"), "heads"),
        P(("groups", "wide"), "heads"),
        P(("groups", "wide"), "heads"),
        P(("groups", "wide"), "heads"),
        P(("groups", "wide"), "heads"),
        P(("groups", "wide"), "heads"),
        P(("groups", "wide"), "heads"),
        P(("groups", "wide"), "heads"),
        P(("groups", "wide"), "heads"),
        P(("groups", "wide"), "heads"),
        P(("groups", "wide"), "heads"),
        P(("groups", "wide"), "heads"),
        P(("groups", "wide"), "heads"),
        P("heads", "wide"),
        P("heads", "wide"),
        P("heads", "wide"),
        P("heads", "wide"),
        P("groups", None),
    )
    return jax.shard_map(
        shards,
        mesh=mesh,
        in_specs=placed,
        out_specs=(P(("groups", "wide"), "heads"), P(("groups", "wide"), "heads")),
        check_vma=False,
    )
```

```python
import contextlib
import functools
import math

import jax
import jax.numpy as jnp
from jax import lax
from jax.experimental import pallas as pl
from jax.experimental.pallas import tpu as pltpu
from jax.sharding import PartitionSpec as P

HDV = 128
HDA = 64
REACH = 2


def passed_along(value, axis, by):
    length = lax.axis_size(axis)
    pairs = [(i, i + by) for i in range(length) if 0 <= i + by < length]
    return lax.ppermute(value, axis, pairs)


def empty_state(row_count, head_count, head_size):
    return (
        jnp.full((head_count, row_count), -1e30, jnp.float32),
        jnp.zeros((head_count, row_count), jnp.float32),
        jnp.zeros((head_count, row_count, head_size), jnp.float32),
    )


def absorb(state, queries, key_rows, value_rows, head_size, allowed):
    maxima, totals, running = state
    head_count = queries.shape[1] // head_size
    query_heads = queries.reshape(queries.shape[0], head_count, head_size)
    key_heads = key_rows.reshape(key_rows.shape[0], head_count, head_size)
    value_heads = value_rows.reshape(value_rows.shape[0], head_count, head_size)
    scores = jnp.einsum(
        "qhd,khd->hqk", query_heads, key_heads, preferred_element_type=jnp.float32
    ) * (1.0 / math.sqrt(head_size))
    if allowed is not None:
        scores = jnp.where(allowed[None, None, :], scores, -1e30)
    new_peak = jnp.maximum(maxima, jnp.max(scores, axis=2))
    weights = jnp.exp(scores - new_peak[:, :, None])
    if allowed is not None:
        weights = jnp.where(allowed[None, None, :], weights, 0.0)
    rescale = jnp.exp(maxima - new_peak)
    totals = totals * rescale + jnp.sum(weights, axis=2)
    running = running * rescale[:, :, None] + jnp.einsum(
        "hqk,khd->hqd",
        weights.astype(jnp.bfloat16),
        value_heads,
        preferred_element_type=jnp.float32,
    )
    return (new_peak, totals, running)


def finish(state, head_size):
    maxima, totals, running = state
    result = running / totals[:, :, None]
    return (
        result.transpose(1, 0, 2)
        .reshape(result.shape[1], result.shape[0] * head_size)
        .astype(jnp.bfloat16)
    )


def permitted(key_blocks, position, table_row, wide_count):
    offsets = key_blocks - position + REACH
    matches = (offsets[:, None] == jnp.arange(2 * REACH + 1, dtype=jnp.int32)[None, :]) & (
        table_row[None, :] > 0
    )
    inside = (key_blocks >= 0) & (key_blocks < wide_count)
    return jnp.any(matches, axis=1) & inside


def general_shards(
    video_hidden,
    audio_hidden,
    video_query,
    video_key,
    video_value,
    audio_query,
    audio_key,
    audio_value,
    cross_video_query,
    cross_audio_key,
    cross_audio_value,
    cross_audio_query,
    cross_video_key,
    cross_video_value,
    video_self_out,
    video_cross_out,
    audio_self_out,
    audio_cross_out,
    intersection,
):
    position = lax.axis_index("wide")
    wide_count = lax.axis_size("wide")
    video_count = video_query.shape[0]
    audio_count = audio_query.shape[0]
    head_count = video_query.shape[1] // HDV
    video_start = empty_state(video_count, head_count, HDV)
    audio_start = empty_state(audio_count, head_count, HDA)
    carried = (video_start, audio_start)
    portion = (
        lax.all_gather(video_key, "wide", axis=0, tiled=True),
        lax.all_gather(video_value, "wide", axis=0, tiled=True),
        lax.all_gather(audio_key, "wide", axis=0, tiled=True),
        lax.all_gather(audio_value, "wide", axis=0, tiled=True),
    )
    video_state = absorb(carried[0], video_query, portion[0], portion[1], HDV, None)
    audio_state = absorb(carried[1], audio_query, portion[2], portion[3], HDA, None)
    table_row = lax.dynamic_slice_in_dim(intersection, position, 1, 0)[0]
    padded_table = jnp.pad(intersection, ((REACH, REACH), (0, 0)))
    flag_row = jnp.diagonal(
        jnp.fliplr(lax.dynamic_slice_in_dim(padded_table, position, 2 * REACH + 1, 0))
    )
    stacked = jnp.concatenate(
        [cross_audio_key, cross_audio_value, cross_video_key, cross_video_value], 0
    )

    def take_cross(carried, portion, block):
        audio_keys = portion[:audio_count]
        audio_values = portion[audio_count : 2 * audio_count]
        video_keys = portion[2 * audio_count : 2 * audio_count + video_count]
        video_values = portion[2 * audio_count + video_count :]
        audio_blocks = jnp.full((audio_count,), block, jnp.int32)
        video_blocks = jnp.full((video_count,), block, jnp.int32)
        return (
            absorb(
                carried[0],
                cross_video_query,
                audio_keys,
                audio_values,
                HDA,
                permitted(audio_blocks, position, table_row, wide_count),
            ),
            absorb(
                carried[1],
                cross_audio_query,
                video_keys,
                video_values,
                HDA,
                permitted(video_blocks, position, flag_row, wide_count),
            ),
        )

    cross_start = (
        empty_state(video_count, head_count, HDA),
        empty_state(audio_count, head_count, HDA),
    )
    carried = take_cross(cross_start, stacked, position)
    for offset in range(-REACH, REACH + 1):
        if offset != 0:
            nearby = passed_along(stacked, "wide", -offset)
            carried = take_cross(carried, nearby, position + offset)
    to_video, to_audio = carried
    video_joined = jnp.concatenate([finish(video_state, HDV), finish(to_video, HDA)], 1)
    audio_joined = jnp.concatenate([finish(audio_state, HDA), finish(to_audio, HDA)], 1)
    video_weights = jnp.concatenate([video_self_out, video_cross_out], 0)
    audio_weights = jnp.concatenate([audio_self_out, audio_cross_out], 0)
    video_terms = jnp.dot(
        video_joined,
        lax.all_gather(video_weights, "wide", axis=1, tiled=True),
        preferred_element_type=jnp.float32,
    )
    audio_terms = jnp.dot(
        audio_joined,
        lax.all_gather(audio_weights, "wide", axis=1, tiled=True),
        preferred_element_type=jnp.float32,
    )
    video_sum, audio_sum = (
        lax.psum_scatter(
            video_terms.astype(jnp.bfloat16), "heads", scatter_dimension=1, tiled=True
        ).astype(jnp.float32),
        lax.psum_scatter(
            audio_terms.astype(jnp.bfloat16), "heads", scatter_dimension=1, tiled=True
        ).astype(jnp.float32),
    )
    video_out = (video_hidden.astype(jnp.float32) + video_sum).astype(jnp.bfloat16)
    audio_out = (audio_hidden.astype(jnp.float32) + audio_sum).astype(jnp.bfloat16)
    return (video_out, audio_out)


NT = (((1,), (1,)), ((), ()))
MESH = pl.DeviceIdType.MESH


def scope(name):
    return contextlib.nullcontext()


def softmax(scores, head_size):
    factor = math.log2(math.e) / math.sqrt(head_size)
    weights = jnp.exp2((scores - jnp.max(scores, axis=1, keepdims=True)) * factor)
    return weights.astype(jnp.bfloat16), jnp.sum(weights, axis=1, keepdims=True)


def scored(queries, keys):
    return lax.dot_general(queries, keys, NT, preferred_element_type=jnp.float32)


def mixed(weights, values):
    return jnp.dot(weights, values, preferred_element_type=jnp.float32)


def joint_kernel(
    n,
    vq, vk, vv, cvq, cvk, cvv, aq, ak, av, caq, cak, cav, ws, wc, aso, aco, table,
    out_v, out_a,
    q_all, k_all, v_all, self_stage, wide_stage, few_stage, pack, p_all, ws_all, wc_all, wa_all,
    tall_bias, wide_bias, o_self, o_rest, r_self, r_rest, totals, sum_v, sum_a,
    a_send, a_recv, w_send, w_recv, x_send, x_recv, z_send, z_recv, m_recv, r_send,
    e_send, e_recv, local,
):
    g = lax.axis_index("groups")
    w = lax.axis_index("wide")
    h = lax.axis_index("heads")
    rows, few = vq.shape[0], aq.shape[0]
    half = rows // 2
    part_rows, part_few = rows // n, few // n
    depth = p_all.shape[1]
    bf16 = jnp.bfloat16

    mine = h * n + w
    side = w // (n // 2)
    mate = w + 1 - 2 * lax.rem(w, 2)
    across_side = n // 2 - side
    far_start = (1 - side) * (n // 2)
    inner = (w > 0) & (w < n - 1)

    def place(dw, dh):
        return {"wide": lax.rem(w + dw, n), "heads": lax.rem(h + dh, n)}

    def remote(source, target, send, recv, device):
        return pltpu.make_async_remote_copy(
            src_ref=source, dst_ref=target, send_sem=send, recv_sem=recv,
            device_id=device, device_id_type=MESH,
        )

    others = [(d, 0) for d in range(1, n)] + [(0, d) for d in range(1, n)]
    barrier = pltpu.get_barrier_semaphore()
    for dw, dh in others:
        pl.semaphore_signal(barrier, inc=1, device_id=place(dw, dh), device_id_type=MESH)
    twin = {"groups": 1 - g}
    pl.semaphore_signal(barrier, inc=1, device_id=twin, device_id_type=MESH)

    def settle(piece, sem):
        pltpu.make_async_copy(piece, piece, sem).wait()

    def head_cols(ref, who):
        return ref.at[:, pl.ds(pl.multiple_of(who * HDV, HDV), HDV)]

    def start(copies):
        for copy in copies:
            copy.start()
        return copies

    streams = ((vq, q_all), (vk, k_all), (vv, v_all))
    self_staged = start(
        [
            pltpu.make_async_copy(source, self_stage.at[i], local.at[15 + i])
            for i, (source, _) in enumerate(streams)
        ]
    )
    staged = start(
        [
            pltpu.make_async_copy(source, wide_stage.at[i], local.at[i])
            for i, source in enumerate((cvq, cvk, cvv))
        ]
        + [
            pltpu.make_async_copy(source, few_stage.at[i], local.at[3 + i])
            for i, source in enumerate((cak, cav, caq, aq, av, ak))
        ]
    )
    own = start(
        [
            pltpu.make_async_copy(head_cols(source, w), target.at[w], local.at[9 + i])
            for i, (source, target) in enumerate(streams)
        ]
        + [
            pltpu.make_async_copy(source, target.at[h], local.at[12 + i])
            for i, (source, target) in enumerate(((ws, ws_all), (wc, wc_all)))
        ]
    )
    for j in range(n):
        for k, source in enumerate((aso, aco)):
            at = (2 * j + k) * HDA
            pltpu.make_async_copy(
                source.at[j * HDA : (j + 1) * HDA], wa_all.at[h, at : at + HDA], local.at[14]
            ).start()
    own.append(pltpu.make_async_copy(wa_all.at[h], wa_all.at[h], local.at[14]))
    for copy in self_staged:
        copy.wait()
    with scope("T0barrier"):
        pl.semaphore_wait(barrier, len(others) + 1)

    far_end = (1 - side) * (n - 1)

    def exchange(target):
        for i, (_, landing) in enumerate(streams):
            remote(
                head_cols(self_stage.at[i], target), landing.at[w], a_send.at[i], a_recv.at[i],
                {"wide": target, "heads": h},
            ).start()

    near = jnp.where(inner, across_side, mate)
    last = jnp.where(inner, mate, across_side)
    for target in (far_end, near, last):
        exchange(target)

    targets = (ws_all, wc_all, wa_all)
    sources = (ws, wc, wa_all.at[h])
    partner = {"wide": w, "heads": h + 1 - 2 * lax.rem(h, 2)}
    opposite = lax.rem(h + n // 2, n)

    def part_of(ref, which):
        size = ref.shape[0] // 2
        return ref.at[pl.ds(pl.multiple_of(which * size, size), size)]

    def send_weights(i):
        remote(
            part_of(sources[i], g), part_of(targets[i].at[h], g),
            w_send.at[i, 0], w_recv.at[i, 0], {"wide": w, "heads": opposite},
        ).start()

    def share_weights(i):
        remote(sources[i], targets[i].at[h], w_send.at[i, 1], w_recv.at[i, 1], partner).start()

    def swap_weights(i):
        piece = part_of(targets[i].at[opposite], g)
        settle(piece, w_recv.at[i, 0])
        remote(piece, piece, w_send.at[i, 2], w_recv.at[i, 2], twin).start()

    def pass_weights(i):
        slot = targets[i].at[opposite]
        settle(part_of(slot, 1 - g), w_recv.at[i, 2])
        remote(slot, slot, w_send.at[i, 3], w_recv.at[i, 3], partner).start()

    def settle_weights(i):
        settle(targets[i].at[h], w_recv.at[i, 1])
        settle(targets[i].at[h], w_recv.at[i, 3])

    for i in range(2):
        send_weights(i)
        share_weights(i)

    for copy in staged:
        copy.wait()
    later = half + few
    for j in range(n):
        cols = slice(j * HDA, (j + 1) * HDA)
        for begin, k in ((0, 0), (later, 1), (later + half, 2)):
            pack[j, begin : begin + half, :] = jnp.concatenate(
                [wide_stage[k, :half, cols], wide_stage[k, half:, cols]], 1
            )
        for begin, k in ((half, 0), (later + 2 * half, 2), (later + 2 * half + few, 4)):
            pack[j, begin : begin + few, :] = jnp.concatenate(
                [few_stage[k, :, cols], few_stage[k + 1, :, cols]], 1
            )

    portions = (slice(0, later), slice(later, depth))

    def exchange_rest(target, k):
        remote(
            pack.at[target, portions[k]], p_all.at[w, portions[k]], a_send.at[3 + k],
            a_recv.at[3 + k], {"wide": target, "heads": h},
        ).start()

    outer = jnp.logical_not(inner)
    exchange_rest(mate, 0)
    exchange_rest(mate, 1)

    @pl.when(outer)
    def _():
        exchange_rest(far_end, 0)
        exchange_rest(far_end, 1)
        exchange_rest(across_side, 0)

    own_pack = pltpu.make_async_copy(pack.at[w], p_all.at[w], local.at[0])
    own_pack.start()
    own.pop().wait()
    send_weights(2)
    share_weights(2)

    for i in range(n):
        for j in range(n):
            column = j - i + REACH
            drop = jnp.float32(-1e30)
            if 0 <= column < table.shape[1]:
                drop = jnp.where(table[i, column] > 0, jnp.float32(0.0), drop)
            tall_bias[i * part_rows : (i + 1) * part_rows, j * few : (j + 1) * few] = jnp.full(
                (part_rows, few), drop
            )
            for k in range(2):
                begin = (k * n + i) * half
                wide_bias[j * few : (j + 1) * few, begin : begin + half] = jnp.full(
                    (few, half), drop
                )

    splits = (half // 2, half // 2, n * part_few)
    starts = (n * part_few, n * part_few + half // 2, 0)

    def chunk(ref, kind):
        if kind == 0:
            return ref
        return ref.at[pl.ds(starts[kind - 1], splits[kind - 1])]

    def buffers(kind):
        return (o_self, r_self) if kind == 0 else (o_rest, r_rest)

    orders = ((1, 0, 2, 3), (2, 3, 1, 0))

    def moved(e):
        return lax.rem(h // 2 + e // 2, 2) * 2 + lax.rem(h + e, 2)

    def turn_of(i):
        return orders[0][i] + lax.rem(w, 2) * (orders[1][i] - orders[0][i])

    def outgoing(kind, i):
        source, landing = buffers(kind)
        d = turn_of(i)
        part = moved(d)
        return d, part, chunk(source.at[part], kind), chunk(landing.at[mine], kind)

    def to_plane(kind, i):
        _, part, piece, where = outgoing(kind, i)

        @pl.when(part != h)
        def _():
            remote(
                piece, where, x_send.at[kind], x_recv.at[kind], {"wide": w, "heads": part}
            ).start()

    def to_across(kind, i):
        d, part, piece, where = outgoing(kind, i)
        remote(
            piece, where, z_send.at[kind], z_recv.at[kind, d, lax.rem(w, 2)],
            {"wide": across_side, "heads": part},
        ).start()

    def to_mate(kind, i):
        _, part, piece, where = outgoing(kind, i)
        remote(
            piece, where, z_send.at[kind], m_recv.at[kind], {"wide": mate, "heads": part}
        ).start()

    def far_piece(kind, d, k):
        return chunk(buffers(kind)[1].at[moved(d) * n + far_start + k], kind)

    def forward(kind, i, ks):
        for k in ks:
            d = orders[0][i] + k * (orders[1][i] - orders[0][i])
            piece = far_piece(kind, d, k)
            settle(piece, z_recv.at[kind, d, k])
            remote(
                piece, piece, r_send.at[kind], z_recv.at[kind, d, k],
                {"wide": mate, "heads": h},
            ).start()

    def many(kind, count):
        landing = buffers(kind)[1]
        if kind == 0:
            return landing.at[:count]
        return landing.at[:count, pl.ds(starts[kind - 1], splits[kind - 1])]

    def gathered(kind):
        settle(many(kind, n - 1), x_recv.at[kind])
        settle(many(kind, n), m_recv.at[kind])

        @pl.when(outer)
        def _():
            for d in range(n):
                for k in range(2):
                    settle(far_piece(kind, d, k), z_recv.at[kind, d, k])

    with scope("T1self"):
        for i, target in enumerate((q_all, k_all, v_all)):
            own[i].wait()
            settle(target.at[: n - 1], a_recv.at[i])

    @pl.when(inner)
    def _():
        exchange_rest(far_end, 0)
        exchange_rest(far_end, 1)
        exchange_rest(across_side, 0)

    keys = k_all[...].reshape(n * rows, HDV)
    values = v_all[...].reshape(n * rows, HDV)

    def self_scores(i):
        at = pl.multiple_of(moved(turn_of(i)) * part_rows, part_rows)
        return scored(q_all[:, pl.ds(at, part_rows), :].reshape(rows, HDV), keys)

    scores = self_scores(0)
    for i in range(n):
        following = self_scores(i + 1) if i + 1 < n else None
        weights, sums = softmax(scores, HDV)
        result = (mixed(weights, values) / sums).astype(bf16)
        scores = following
        o_self[pl.ds(moved(turn_of(i)), 1)] = result[None]
        to_plane(0, i)
        to_across(0, i)
        to_mate(0, i)
    r_self[pl.ds(mine, 1)] = o_self[pl.ds(h, 1)]
    ends, peers = [lax.rem(w, 2)], [lax.rem(w + 1, 2)]

    with scope("T2weights"):
        swap_weights(0)
        swap_weights(1)
    with scope("T2ends"):
        @pl.when(inner)
        def _():
            for i in range(n):
                forward(0, i, ends)

    with scope("T2video"):
        own_pack.wait()
        settle(p_all.at[: n - 1, portions[0]], a_recv.at[3])
    lane = lax.broadcasted_iota(jnp.int32, (n * few, 2 * HDA), 1)
    left = lane < HDA

    def swapped(block):
        return jnp.concatenate([block[:, HDA:], block[:, :HDA]], 1)

    def only(block, keep_left):
        zero = jnp.zeros_like(block)
        return jnp.where(left, block, zero) if keep_left else jnp.where(left, zero, block)

    keyed = p_all[:, half:later, :].reshape(n * few, 2 * HDA)
    key_left, key_right = only(keyed, True), only(swapped(keyed), False)
    twice = jnp.concatenate([keyed[:, HDA:], keyed[:, HDA:]], 1)

    def cross_scores(i):
        part = moved(turn_of(i))
        begin = pl.multiple_of(lax.rem(part, n // 2) * part_rows, part_rows)
        queries = p_all[:, pl.ds(begin, part_rows), :].reshape(rows, 2 * HDA)
        chosen = jnp.where(part < n // 2, key_left, key_right)
        return scored(queries, chosen) + tall_bias[...]

    low = lax.broadcasted_iota(jnp.int32, (half, 2 * HDA), 1) < HDA
    tail = n * part_few
    scores = cross_scores(0)
    for i in range(n):
        following = cross_scores(i + 1) if i + 1 < n else None
        weights, sums = softmax(scores, HDA)
        result = mixed(weights, twice) / sums
        scores = following
        block = moved(turn_of(i))
        upper = [result[j * part_rows : (j + 1) * part_rows] for j in reversed(range(n // 2))]
        packed = jnp.where(low, jnp.concatenate(upper, 0), result[half:]).astype(bf16)
        o_rest[pl.ds(block, 1), tail:, :] = packed[None]
        for kind in (1, 2):
            to_plane(kind, i)

        @pl.when(inner)
        def _():
            for kind in (1, 2):
                to_across(kind, i)
                to_mate(kind, i)

    r_rest[pl.ds(mine, 1), tail:, :] = o_rest[pl.ds(h, 1), tail:, :]

    @pl.when(outer)
    def _():
        for kind in (1, 2):
            for i in range(n):
                to_mate(kind, i)

    exchange_rest(across_side, 1)
    with scope("T2peers"):
        @pl.when(inner)
        def _():
            for i in range(n):
                forward(0, i, peers)
            for i in range(2):
                pass_weights(i)

    swap_weights(2)
    with scope("T3peers"):
        @pl.when(inner)
        def _():
            for kind in (1, 2):
                for i in range(n):
                    forward(kind, i, peers)

    with scope("T3rest"):
        settle(p_all.at[: n - 1, portions[1]], a_recv.at[4])
    begin = later
    both = p_all[:, begin : begin + half, :].reshape(n * half, 2 * HDA)
    vals = p_all[:, begin + half : begin + 2 * half, :].reshape(n * half, 2 * HDA)
    begin += 2 * half
    asked = p_all[:, begin : begin + few, :].reshape(n * few, 2 * HDA)
    third = p_all[:, begin + few : depth, :].reshape(n * few, 2 * HDA)
    scores_a = scored(asked, only(third, False))
    scores_c = jnp.concatenate(
        [scored(only(asked, True), both), scored(only(swapped(asked), False), both)], 1
    ) + wide_bias[...]
    weights, sums = softmax(scores_a, HDA)
    audio_own = mixed(weights, third) / sums
    weights, sums = softmax(scores_c, HDA)
    upper, lower = weights[:, : n * half], weights[:, n * half :]
    audio_other = (pltpu.roll(mixed(upper, vals), HDA, 1) + mixed(lower, vals)) / sums
    audio = jnp.where(left, audio_own, audio_other).astype(bf16)
    for t in range(n):
        o_rest[t, :tail, :] = jnp.concatenate(
            [audio[j * few + t * part_few : j * few + (t + 1) * part_few, :] for j in range(n)], 0
        )
    r_rest[pl.ds(mine, 1), :tail, :] = o_rest[pl.ds(h, 1), :tail, :]
    for i in range(n):
        to_plane(3, i)
        to_mate(3, i)

    @pl.when(inner)
    def _():
        for i in range(n):
            to_across(3, i)

    with scope("T4pass"):
        @pl.when(outer)
        def _():
            for i in range(3):
                pass_weights(i)

    with scope("T5w"):
        own[3].wait()
        own[4].wait()
        settle_weights(0)
    with scope("T6self"):
        gathered(0)

    @pl.when(outer)
    def _():
        for kind in (1, 2, 3):
            for i in range(n):
                to_across(kind, i)

    heads = n * n
    joined = jnp.concatenate([r_self[s] for s in range(heads)], 1)
    totals[...] = jnp.dot(
        joined, ws_all[...].reshape(-1, ws.shape[1]), preferred_element_type=jnp.float32
    )

    with scope("T7forward"):
        @pl.when(inner)
        def _():
            for kind in (1, 2):
                for i in range(n):
                    forward(kind, i, ends)
            pass_weights(2)

    with scope("T7w"):
        settle_weights(1)

    def rows_of(ref, block, size):
        return ref.at[pl.ds(pl.multiple_of(block * size, size), size)]

    def deliver(c, b):
        source, out, size = ((sum_v, out_v, part_rows), (sum_a, out_a, part_few))[c]
        piece, target = rows_of(source, b, size), rows_of(out, h, size)
        away = (w != b) | (w != h)

        @pl.when(away)
        def _():
            remote(
                piece, target, e_send.at[c], e_recv.at[c], {"wide": b, "heads": w}
            ).start()

        @pl.when(jnp.logical_not(away))
        def _():
            pltpu.make_async_copy(piece, target, e_recv.at[c]).start()

    flat_c = wc_all[...].reshape(-1, wc.shape[1])
    for u in range(2):
        with scope("T8gather%d" % u):
            gathered(1 + u)
        begin = tail + u * (half // 2)
        piece = slice(begin, begin + half // 2)
        crossed = jnp.concatenate(
            [
                jnp.concatenate([r_rest[s, piece, :HDA] for s in range(heads)], 1),
                jnp.concatenate([r_rest[s, piece, HDA:] for s in range(heads)], 1),
            ],
            0,
        )
        products = jnp.dot(crossed, flat_c, preferred_element_type=jnp.float32)
        size = half // 2
        for k in range(2):
            b = (n // 2 - 1 - u, n // 2 + u)[k]
            where = slice(b * size, (b + 1) * size)
            sum_v[where, :] = (
                totals[where, :] + products[k * size : (k + 1) * size, :]
            ).astype(bf16)
        for b in (n // 2 - 1 - u, n // 2 + u):
            deliver(0, b)
        if u == 0:
            with scope("T7audio"):
                @pl.when(inner)
                def _():
                    for ks in (ends, peers):
                        for i in range(n):
                            forward(3, i, ks)

    with scope("T8audio"):
        settle_weights(2)
        gathered(3)
    audio_joined = jnp.concatenate([r_rest[s, :tail, :] for s in range(heads)], 1)
    sum_a[...] = jnp.dot(
        audio_joined, wa_all[...].reshape(-1, aso.shape[1]), preferred_element_type=jnp.float32
    ).astype(bf16)
    for b in range(n):
        deliver(1, b)

    with scope("T9results"):
        settle(out_v, e_recv.at[0])
        settle(out_a, e_recv.at[1])

    with scope("TBsends"):
        for i, target in enumerate((q_all, k_all, v_all)):
            settle(target.at[: n - 1], a_send.at[i])
        for k, portion in enumerate(portions):
            settle(p_all.at[: n - 1, portion], a_send.at[3 + k])
        for i in range(3):
            settle(part_of(targets[i].at[h], g), w_send.at[i, 0])
            settle(targets[i].at[h], w_send.at[i, 1])
            settle(part_of(targets[i].at[h], g), w_send.at[i, 2])
            settle(targets[i].at[h], w_send.at[i, 3])
        for kind in range(4):
            settle(many(kind, n - 1), x_send.at[kind])
            settle(many(kind, 2 * n), z_send.at[kind])
        @pl.when(inner)
        def _():
            for kind in range(4):
                settle(many(kind, 2 * n), r_send.at[kind])

        for c, (ref, size) in enumerate(((sum_v, part_rows), (sum_a, part_few))):
            settle(ref.at[: (n - 1) * size], e_send.at[c])

            @pl.when(w != h)
            def _():
                settle(ref.at[:size], e_send.at[c])


def shards(*args):
    n = lax.axis_size("wide")
    count = lax.axis_size("heads")
    head_count = args[2].shape[1] // HDV
    paired = lax.axis_size("groups") == 2
    if not (paired and n == count == head_count == 2 * REACH and args[5].shape[0] % (16 * n) == 0):
        return general_shards(*args)
    (video_hidden, audio_hidden, vq, vk, vv, aq, ak, av, cvq, cak, cav, caq, cvk, cvv,
     vso, vco, aso, aco, table) = args
    rows, few = vq.shape[0], aq.shape[0]
    depth = rows + rows // 2 + 3 * few
    anywhere = pl.BlockSpec(memory_space=pl.ANY)
    bf16, f32 = jnp.bfloat16, jnp.float32
    rest = rows // 2 + few
    dma = pltpu.SemaphoreType.DMA
    video_sum, audio_sum = pl.pallas_call(
        functools.partial(joint_kernel, n),
        out_shape=(
            jax.ShapeDtypeStruct(video_hidden.shape, bf16),
            jax.ShapeDtypeStruct(audio_hidden.shape, bf16),
        ),
        in_specs=[pl.BlockSpec(memory_space=pltpu.HBM)] * 16 + [pl.BlockSpec(memory_space=pltpu.SMEM)],
        out_specs=(anywhere, anywhere),
        scratch_shapes=[
            pltpu.VMEM((n, rows, HDV), bf16),
            pltpu.VMEM((n, rows, HDV), bf16),
            pltpu.VMEM((n, rows, HDV), bf16),
            pltpu.VMEM((3,) + vq.shape, bf16),
            pltpu.VMEM((3,) + cvq.shape, bf16),
            pltpu.VMEM((6,) + aq.shape, bf16),
            pltpu.VMEM((n, depth, 2 * HDA), bf16),
            pltpu.VMEM((n, depth, 2 * HDA), bf16),
            pltpu.VMEM((n,) + vso.shape, bf16),
            pltpu.VMEM((n,) + vco.shape, bf16),
            pltpu.VMEM((n, 2 * aso.shape[0], aso.shape[1]), bf16),
            pltpu.VMEM((rows, n * few), f32),
            pltpu.VMEM((n * few, n * rows), f32),
            pltpu.VMEM((n, rows, HDV), bf16),
            pltpu.VMEM((n, rest, 2 * HDA), bf16),
            pltpu.VMEM((n * n, rows, HDV), bf16),
            pltpu.VMEM((n * n, rest, 2 * HDA), bf16),
            pltpu.VMEM(video_hidden.shape, f32),
            pltpu.VMEM(video_hidden.shape, bf16),
            pltpu.VMEM(audio_hidden.shape, bf16),
            dma((5,)), dma((5,)),
            dma((3, 4)), dma((3, 4)),
            dma((4,)), dma((4,)),
            dma((4,)), dma((4, n, 2)), dma((4,)), dma((4,)),
            dma((2,)), dma((2,)),
            dma((18,)),
        ],
        compiler_params=pltpu.CompilerParams(
            collective_id=0, has_side_effects=True, vmem_limit_bytes=48 * 1024 * 1024
        ),
        name="joint",
    )(
        *(
            pltpu.with_memory_space_constraint(operand, pltpu.HBM)
            for operand in (
                vq, vk, vv, cvq, cvk, cvv, aq, ak, av, caq, cak, cav, vso, vco, aso, aco, table
            )
        )
    )
    video_out = video_hidden.astype(f32) + video_sum.astype(f32)
    audio_out = audio_hidden.astype(f32) + audio_sum.astype(f32)
    return (video_out.astype(bf16), audio_out.astype(bf16))


def solution(mesh):
    placed = (
        P(("groups", "wide"), "heads"),
        P(("groups", "wide"), "heads"),
        P(("groups", "wide"), "heads"),
        P(("groups", "wide"), "heads"),
        P(("groups", "wide"), "heads"),
        P(("groups", "wide"), "heads"),
        P(("groups", "wide"), "heads"),
        P(("groups", "wide"), "heads"),
        P(("groups", "wide"), "heads"),
        P(("groups", "wide"), "heads"),
        P(("groups", "wide"), "heads"),
        P(("groups", "wide"), "heads"),
        P(("groups", "wide"), "heads"),
        P(("groups", "wide"), "heads"),
        P("heads", "wide"),
        P("heads", "wide"),
        P("heads", "wide"),
        P("heads", "wide"),
        P("groups", None),
    )
    return jax.shard_map(
        shards,
        mesh=mesh,
        in_specs=placed,
        out_specs=(P(("groups", "wide"), "heads"), P(("groups", "wide"), "heads")),
        check_vma=False,
    )
```

```python
import contextlib
import functools
import math

import jax
import jax.numpy as jnp
from jax import lax
from jax.experimental import pallas as pl
from jax.experimental.pallas import tpu as pltpu
from jax.sharding import PartitionSpec as P

HDV = 128
HDA = 64
REACH = 2


def passed_along(value, axis, by):
    length = lax.axis_size(axis)
    pairs = [(i, i + by) for i in range(length) if 0 <= i + by < length]
    return lax.ppermute(value, axis, pairs)


def empty_state(row_count, head_count, head_size):
    return (
        jnp.full((head_count, row_count), -1e30, jnp.float32),
        jnp.zeros((head_count, row_count), jnp.float32),
        jnp.zeros((head_count, row_count, head_size), jnp.float32),
    )


def absorb(state, queries, key_rows, value_rows, head_size, allowed):
    maxima, totals, running = state
    head_count = queries.shape[1] // head_size
    query_heads = queries.reshape(queries.shape[0], head_count, head_size)
    key_heads = key_rows.reshape(key_rows.shape[0], head_count, head_size)
    value_heads = value_rows.reshape(value_rows.shape[0], head_count, head_size)
    scores = jnp.einsum(
        "qhd,khd->hqk", query_heads, key_heads, preferred_element_type=jnp.float32
    ) * (1.0 / math.sqrt(head_size))
    if allowed is not None:
        scores = jnp.where(allowed[None, None, :], scores, -1e30)
    new_peak = jnp.maximum(maxima, jnp.max(scores, axis=2))
    weights = jnp.exp(scores - new_peak[:, :, None])
    if allowed is not None:
        weights = jnp.where(allowed[None, None, :], weights, 0.0)
    rescale = jnp.exp(maxima - new_peak)
    totals = totals * rescale + jnp.sum(weights, axis=2)
    running = running * rescale[:, :, None] + jnp.einsum(
        "hqk,khd->hqd",
        weights.astype(jnp.bfloat16),
        value_heads,
        preferred_element_type=jnp.float32,
    )
    return (new_peak, totals, running)


def finish(state, head_size):
    maxima, totals, running = state
    result = running / totals[:, :, None]
    return (
        result.transpose(1, 0, 2)
        .reshape(result.shape[1], result.shape[0] * head_size)
        .astype(jnp.bfloat16)
    )


def permitted(key_blocks, position, table_row, wide_count):
    offsets = key_blocks - position + REACH
    matches = (offsets[:, None] == jnp.arange(2 * REACH + 1, dtype=jnp.int32)[None, :]) & (
        table_row[None, :] > 0
    )
    inside = (key_blocks >= 0) & (key_blocks < wide_count)
    return jnp.any(matches, axis=1) & inside


def general_shards(
    video_hidden,
    audio_hidden,
    video_query,
    video_key,
    video_value,
    audio_query,
    audio_key,
    audio_value,
    cross_video_query,
    cross_audio_key,
    cross_audio_value,
    cross_audio_query,
    cross_video_key,
    cross_video_value,
    video_self_out,
    video_cross_out,
    audio_self_out,
    audio_cross_out,
    intersection,
):
    position = lax.axis_index("wide")
    wide_count = lax.axis_size("wide")
    video_count = video_query.shape[0]
    audio_count = audio_query.shape[0]
    head_count = video_query.shape[1] // HDV
    video_start = empty_state(video_count, head_count, HDV)
    audio_start = empty_state(audio_count, head_count, HDA)
    carried = (video_start, audio_start)
    portion = (
        lax.all_gather(video_key, "wide", axis=0, tiled=True),
        lax.all_gather(video_value, "wide", axis=0, tiled=True),
        lax.all_gather(audio_key, "wide", axis=0, tiled=True),
        lax.all_gather(audio_value, "wide", axis=0, tiled=True),
    )
    video_state = absorb(carried[0], video_query, portion[0], portion[1], HDV, None)
    audio_state = absorb(carried[1], audio_query, portion[2], portion[3], HDA, None)
    table_row = lax.dynamic_slice_in_dim(intersection, position, 1, 0)[0]
    padded_table = jnp.pad(intersection, ((REACH, REACH), (0, 0)))
    flag_row = jnp.diagonal(
        jnp.fliplr(lax.dynamic_slice_in_dim(padded_table, position, 2 * REACH + 1, 0))
    )
    stacked = jnp.concatenate(
        [cross_audio_key, cross_audio_value, cross_video_key, cross_video_value], 0
    )

    def take_cross(carried, portion, block):
        audio_keys = portion[:audio_count]
        audio_values = portion[audio_count : 2 * audio_count]
        video_keys = portion[2 * audio_count : 2 * audio_count + video_count]
        video_values = portion[2 * audio_count + video_count :]
        audio_blocks = jnp.full((audio_count,), block, jnp.int32)
        video_blocks = jnp.full((video_count,), block, jnp.int32)
        return (
            absorb(
                carried[0],
                cross_video_query,
                audio_keys,
                audio_values,
                HDA,
                permitted(audio_blocks, position, table_row, wide_count),
            ),
            absorb(
                carried[1],
                cross_audio_query,
                video_keys,
                video_values,
                HDA,
                permitted(video_blocks, position, flag_row, wide_count),
            ),
        )

    cross_start = (
        empty_state(video_count, head_count, HDA),
        empty_state(audio_count, head_count, HDA),
    )
    carried = take_cross(cross_start, stacked, position)
    for offset in range(-REACH, REACH + 1):
        if offset != 0:
            nearby = passed_along(stacked, "wide", -offset)
            carried = take_cross(carried, nearby, position + offset)
    to_video, to_audio = carried
    video_joined = jnp.concatenate([finish(video_state, HDV), finish(to_video, HDA)], 1)
    audio_joined = jnp.concatenate([finish(audio_state, HDA), finish(to_audio, HDA)], 1)
    video_weights = jnp.concatenate([video_self_out, video_cross_out], 0)
    audio_weights = jnp.concatenate([audio_self_out, audio_cross_out], 0)
    video_terms = jnp.dot(
        video_joined,
        lax.all_gather(video_weights, "wide", axis=1, tiled=True),
        preferred_element_type=jnp.float32,
    )
    audio_terms = jnp.dot(
        audio_joined,
        lax.all_gather(audio_weights, "wide", axis=1, tiled=True),
        preferred_element_type=jnp.float32,
    )
    video_sum, audio_sum = (
        lax.psum_scatter(
            video_terms.astype(jnp.bfloat16), "heads", scatter_dimension=1, tiled=True
        ).astype(jnp.float32),
        lax.psum_scatter(
            audio_terms.astype(jnp.bfloat16), "heads", scatter_dimension=1, tiled=True
        ).astype(jnp.float32),
    )
    video_out = (video_hidden.astype(jnp.float32) + video_sum).astype(jnp.bfloat16)
    audio_out = (audio_hidden.astype(jnp.float32) + audio_sum).astype(jnp.bfloat16)
    return (video_out, audio_out)


NT = (((1,), (1,)), ((), ()))
MESH = pl.DeviceIdType.MESH


def scope(name):
    return contextlib.nullcontext()


def softmax(scores, head_size):
    factor = math.log2(math.e) / math.sqrt(head_size)
    weights = jnp.exp2((scores - jnp.max(scores, axis=1, keepdims=True)) * factor)
    return weights.astype(jnp.bfloat16), jnp.sum(weights, axis=1, keepdims=True)


def scored(queries, keys):
    return lax.dot_general(queries, keys, NT, preferred_element_type=jnp.float32)


def mixed(weights, values):
    return jnp.dot(weights, values, preferred_element_type=jnp.float32)


def joint_kernel(
    n,
    vq, vk, vv, cvq, cvk, cvv, aq, ak, av, caq, cak, cav, ws, wc, aso, aco, table,
    out_v, out_a,
    q_all, k_all, v_all, self_stage, wide_stage, few_stage, pack, p_all, ws_all, wc_all, wa_all,
    tall_bias, wide_bias, o_self, o_rest, r_self, r_rest, totals, sum_v, sum_a,
    a_send, a_recv, w_send, w_recv, x_recv, z_send, z_recv, m_recv, r_send,
    e_send, e_recv, local,
):
    g = lax.axis_index("groups")
    w = lax.axis_index("wide")
    h = lax.axis_index("heads")
    rows, few = vq.shape[0], aq.shape[0]
    half = rows // 2
    part_rows, part_few = rows // n, few // n
    depth = p_all.shape[1]
    bf16 = jnp.bfloat16

    mine = h * n + w
    side = w // (n // 2)
    mate = w + 1 - 2 * lax.rem(w, 2)
    across_side = n // 2 - side
    far_start = (1 - side) * (n // 2)
    inner = (w > 0) & (w < n - 1)

    def place(dw, dh):
        return {"wide": lax.rem(w + dw, n), "heads": lax.rem(h + dh, n)}

    def remote(source, target, send, recv, device):
        return pltpu.make_async_remote_copy(
            src_ref=source, dst_ref=target, send_sem=send, recv_sem=recv,
            device_id=device, device_id_type=MESH,
        )

    others = [(d, 0) for d in range(1, n)] + [(0, d) for d in range(1, n)]
    barrier = pltpu.get_barrier_semaphore()
    for dw, dh in others:
        pl.semaphore_signal(barrier, inc=1, device_id=place(dw, dh), device_id_type=MESH)
    twin = {"groups": 1 - g}
    pl.semaphore_signal(barrier, inc=1, device_id=twin, device_id_type=MESH)

    def settle(piece, sem):
        pltpu.make_async_copy(piece, piece, sem).wait()

    def head_cols(ref, who):
        return ref.at[:, pl.ds(pl.multiple_of(who * HDV, HDV), HDV)]

    def start(copies):
        for copy in copies:
            copy.start()
        return copies

    streams = ((vq, q_all), (vk, k_all), (vv, v_all))
    self_staged = start(
        [
            pltpu.make_async_copy(source, self_stage.at[i], local.at[2])
            for i, (source, _) in enumerate(streams)
        ]
    )
    staged = start(
        [
            pltpu.make_async_copy(source, wide_stage.at[i], local.at[0])
            for i, source in enumerate((cvq, cvk, cvv))
        ]
        + [
            pltpu.make_async_copy(source, few_stage.at[i], local.at[1])
            for i, source in enumerate((cak, cav, caq, aq, av, ak))
        ]
    )
    own = start(
        [
            pltpu.make_async_copy(head_cols(source, w), target.at[w], local.at[3])
            for i, (source, target) in enumerate(streams)
        ]
        + [
            pltpu.make_async_copy(source, target.at[h], local.at[4 + i])
            for i, (source, target) in enumerate(((ws, ws_all), (wc, wc_all)))
        ]
    )
    for j in range(n):
        for k, source in enumerate((aso, aco)):
            at = (2 * j + k) * HDA
            pltpu.make_async_copy(
                source.at[j * HDA : (j + 1) * HDA], wa_all.at[h, at : at + HDA], local.at[6]
            ).start()
    own.append(pltpu.make_async_copy(wa_all.at[h], wa_all.at[h], local.at[6]))
    settle(self_stage, local.at[2])
    with scope("T0barrier"):
        pl.semaphore_wait(barrier, len(others) + 1)

    far_end = (1 - side) * (n - 1)

    def exchange(target):
        for i, (_, landing) in enumerate(streams):
            remote(
                head_cols(self_stage.at[i], target), landing.at[w], a_send.at[i], a_recv.at[i],
                {"wide": target, "heads": h},
            ).start()

    near = jnp.where(inner, across_side, mate)
    last = jnp.where(inner, mate, across_side)
    for target in (far_end, near, last):
        exchange(target)

    targets = (ws_all, wc_all, wa_all)
    sources = (ws, wc, wa_all.at[h])
    partner = {"wide": w, "heads": h + 1 - 2 * lax.rem(h, 2)}
    opposite = lax.rem(h + n // 2, n)

    def part_of(ref, which):
        size = ref.shape[0] // 2
        return ref.at[pl.ds(pl.multiple_of(which * size, size), size)]

    def send_weights(i):
        remote(
            part_of(sources[i], g), part_of(targets[i].at[h], g),
            w_send.at[i], w_recv.at[i, 0], {"wide": w, "heads": opposite},
        ).start()

    def share_weights(i):
        remote(sources[i], targets[i].at[h], w_send.at[i], w_recv.at[i, 1], partner).start()

    def swap_weights(i):
        piece = part_of(targets[i].at[opposite], g)
        settle(piece, w_recv.at[i, 0])
        remote(piece, piece, w_send.at[i], w_recv.at[i, 2], twin).start()

    def pass_weights(i):
        slot = targets[i].at[opposite]
        settle(part_of(slot, 1 - g), w_recv.at[i, 2])
        remote(slot, slot, w_send.at[i], w_recv.at[i, 3], partner).start()

    def settle_weights(i):
        settle(targets[i].at[h], w_recv.at[i, 1])
        settle(targets[i].at[h], w_recv.at[i, 3])

    for i in range(2):
        send_weights(i)
        share_weights(i)

    settle(wide_stage, local.at[0])
    settle(few_stage, local.at[1])
    later = half + few
    for j in range(n):
        cols = slice(j * HDA, (j + 1) * HDA)
        for begin, k in ((0, 0), (later, 1), (later + half, 2)):
            pack[j, begin : begin + half, :] = jnp.concatenate(
                [wide_stage[k, :half, cols], wide_stage[k, half:, cols]], 1
            )
        for begin, k in ((half, 0), (later + 2 * half, 2), (later + 2 * half + few, 4)):
            pack[j, begin : begin + few, :] = jnp.concatenate(
                [few_stage[k, :, cols], few_stage[k + 1, :, cols]], 1
            )

    portions = (slice(0, later), slice(later, depth))

    def exchange_rest(target, k):
        remote(
            pack.at[target, portions[k]], p_all.at[w, portions[k]], a_send.at[3 + k],
            a_recv.at[3 + k], {"wide": target, "heads": h},
        ).start()

    outer = jnp.logical_not(inner)
    exchange_rest(mate, 0)
    exchange_rest(mate, 1)

    @pl.when(outer)
    def _():
        exchange_rest(far_end, 0)
        exchange_rest(far_end, 1)
        exchange_rest(across_side, 0)

    own_pack = pltpu.make_async_copy(pack.at[w], p_all.at[w], local.at[7])
    own_pack.start()
    own.pop().wait()
    send_weights(2)
    share_weights(2)

    for i in range(n):
        for j in range(n):
            column = j - i + REACH
            drop = jnp.float32(-1e30)
            if 0 <= column < table.shape[1]:
                drop = jnp.where(table[i, column] > 0, jnp.float32(0.0), drop)
            tall_bias[i * part_rows : (i + 1) * part_rows, j * few : (j + 1) * few] = jnp.full(
                (part_rows, few), drop
            )
            for k in range(2):
                begin = (k * n + i) * half
                wide_bias[j * few : (j + 1) * few, begin : begin + half] = jnp.full(
                    (few, half), drop
                )

    splits = (half // 2, half // 2, n * part_few)
    starts = (n * part_few, n * part_few + half // 2, 0)

    def chunk(ref, kind):
        if kind == 0:
            return ref
        return ref.at[pl.ds(starts[kind - 1], splits[kind - 1])]

    def buffers(kind):
        return (o_self, r_self) if kind == 0 else (o_rest, r_rest)

    orders = ((1, 0, 2, 3), (2, 3, 1, 0))

    def moved(e):
        return lax.rem(h // 2 + e // 2, 2) * 2 + lax.rem(h + e, 2)

    def turn_of(i):
        return orders[0][i] + lax.rem(w, 2) * (orders[1][i] - orders[0][i])

    def outgoing(kind, i):
        source, landing = buffers(kind)
        d = turn_of(i)
        part = moved(d)
        return d, part, chunk(source.at[part], kind), chunk(landing.at[mine], kind)

    def to_plane(kind, i):
        _, part, piece, where = outgoing(kind, i)

        @pl.when(part != h)
        def _():
            remote(
                piece, where, z_send.at[kind], x_recv.at[kind], {"wide": w, "heads": part}
            ).start()

    def to_across(kind, i):
        d, part, piece, where = outgoing(kind, i)
        remote(
            piece, where, z_send.at[kind], z_recv.at[kind, d, lax.rem(w, 2)],
            {"wide": across_side, "heads": part},
        ).start()

    def to_mate(kind, i):
        _, part, piece, where = outgoing(kind, i)
        remote(
            piece, where, z_send.at[kind], m_recv.at[kind], {"wide": mate, "heads": part}
        ).start()

    def far_piece(kind, d, k):
        return chunk(buffers(kind)[1].at[moved(d) * n + far_start + k], kind)

    def forward(kind, i, ks):
        for k in ks:
            d = orders[0][i] + k * (orders[1][i] - orders[0][i])
            piece = far_piece(kind, d, k)
            settle(piece, z_recv.at[kind, d, k])
            remote(
                piece, piece, r_send.at[kind], z_recv.at[kind, d, k],
                {"wide": mate, "heads": h},
            ).start()

    def many(kind, count):
        landing = buffers(kind)[1]
        if kind == 0:
            return landing.at[:count]
        return landing.at[:count, pl.ds(starts[kind - 1], splits[kind - 1])]

    def gathered(kind):
        settle(many(kind, n - 1), x_recv.at[kind])
        settle(many(kind, n), m_recv.at[kind])

        @pl.when(outer)
        def _():
            for d in range(n):
                for k in range(2):
                    settle(far_piece(kind, d, k), z_recv.at[kind, d, k])

    with scope("T1self"):
        settle(q_all.at[: len(streams)], local.at[3])
        for i, target in enumerate((q_all, k_all, v_all)):
            settle(target.at[: n - 1], a_recv.at[i])

    @pl.when(inner)
    def _():
        exchange_rest(far_end, 0)
        exchange_rest(far_end, 1)
        exchange_rest(across_side, 0)

    keys = k_all[...].reshape(n * rows, HDV)
    values = v_all[...].reshape(n * rows, HDV)

    def self_scores(i):
        at = pl.multiple_of(moved(turn_of(i)) * part_rows, part_rows)
        return scored(q_all[:, pl.ds(at, part_rows), :].reshape(rows, HDV), keys)

    scores = self_scores(0)
    for i in range(n):
        following = self_scores(i + 1) if i + 1 < n else None
        weights, sums = softmax(scores, HDV)
        result = (mixed(weights, values) / sums).astype(bf16)
        scores = following
        o_self[pl.ds(moved(turn_of(i)), 1)] = result[None]
        to_plane(0, i)
        to_across(0, i)
        to_mate(0, i)
    r_self[pl.ds(mine, 1)] = o_self[pl.ds(h, 1)]
    ends, peers = [lax.rem(w, 2)], [lax.rem(w + 1, 2)]

    with scope("T2weights"):
        swap_weights(0)
        swap_weights(1)
    with scope("T2ends"):
        @pl.when(inner)
        def _():
            for i in range(n):
                forward(0, i, ends)

    with scope("T2video"):
        own_pack.wait()
        settle(p_all.at[: n - 1, portions[0]], a_recv.at[3])
    lane = lax.broadcasted_iota(jnp.int32, (n * few, 2 * HDA), 1)
    left = lane < HDA

    def swapped(block):
        return jnp.concatenate([block[:, HDA:], block[:, :HDA]], 1)

    def only(block, keep_left):
        zero = jnp.zeros_like(block)
        return jnp.where(left, block, zero) if keep_left else jnp.where(left, zero, block)

    keyed = p_all[:, half:later, :].reshape(n * few, 2 * HDA)
    key_left, key_right = only(keyed, True), only(swapped(keyed), False)
    twice = jnp.concatenate([keyed[:, HDA:], keyed[:, HDA:]], 1)

    def cross_scores(i):
        part = moved(turn_of(i))
        begin = pl.multiple_of(lax.rem(part, n // 2) * part_rows, part_rows)
        queries = p_all[:, pl.ds(begin, part_rows), :].reshape(rows, 2 * HDA)
        chosen = jnp.where(part < n // 2, key_left, key_right)
        return scored(queries, chosen) + tall_bias[...]

    low = lax.broadcasted_iota(jnp.int32, (half, 2 * HDA), 1) < HDA
    tail = n * part_few
    scores = cross_scores(0)
    for i in range(n):
        following = cross_scores(i + 1) if i + 1 < n else None
        weights, sums = softmax(scores, HDA)
        result = mixed(weights, twice) / sums
        scores = following
        block = moved(turn_of(i))
        upper = [result[j * part_rows : (j + 1) * part_rows] for j in reversed(range(n // 2))]
        packed = jnp.where(low, jnp.concatenate(upper, 0), result[half:]).astype(bf16)
        o_rest[pl.ds(block, 1), tail:, :] = packed[None]
        for kind in (1, 2):
            to_plane(kind, i)

        @pl.when(inner)
        def _():
            for kind in (1, 2):
                to_across(kind, i)
                to_mate(kind, i)

    r_rest[pl.ds(mine, 1), tail:, :] = o_rest[pl.ds(h, 1), tail:, :]

    @pl.when(outer)
    def _():
        for kind in (1, 2):
            for i in range(n):
                to_mate(kind, i)

    exchange_rest(across_side, 1)
    with scope("T2peers"):
        @pl.when(inner)
        def _():
            for i in range(n):
                forward(0, i, peers)
            for i in range(2):
                pass_weights(i)

    swap_weights(2)
    with scope("T3peers"):
        @pl.when(inner)
        def _():
            for kind in (1, 2):
                for i in range(n):
                    forward(kind, i, peers)

    with scope("T3rest"):
        settle(p_all.at[: n - 1, portions[1]], a_recv.at[4])
    begin = later
    both = p_all[:, begin : begin + half, :].reshape(n * half, 2 * HDA)
    vals = p_all[:, begin + half : begin + 2 * half, :].reshape(n * half, 2 * HDA)
    begin += 2 * half
    asked = p_all[:, begin : begin + few, :].reshape(n * few, 2 * HDA)
    third = p_all[:, begin + few : depth, :].reshape(n * few, 2 * HDA)
    scores_a = scored(asked, only(third, False))
    scores_c = jnp.concatenate(
        [scored(only(asked, True), both), scored(only(swapped(asked), False), both)], 1
    ) + wide_bias[...]
    weights, sums = softmax(scores_a, HDA)
    audio_own = mixed(weights, third) / sums
    weights, sums = softmax(scores_c, HDA)
    upper, lower = weights[:, : n * half], weights[:, n * half :]
    audio_other = (pltpu.roll(mixed(upper, vals), HDA, 1) + mixed(lower, vals)) / sums
    audio = jnp.where(left, audio_own, audio_other).astype(bf16)
    for t in range(n):
        o_rest[t, :tail, :] = jnp.concatenate(
            [audio[j * few + t * part_few : j * few + (t + 1) * part_few, :] for j in range(n)], 0
        )
    r_rest[pl.ds(mine, 1), :tail, :] = o_rest[pl.ds(h, 1), :tail, :]
    for i in range(n):
        to_plane(3, i)
        to_mate(3, i)

    @pl.when(inner)
    def _():
        for i in range(n):
            to_across(3, i)

    with scope("T4pass"):
        @pl.when(outer)
        def _():
            for i in range(3):
                pass_weights(i)

    with scope("T5w"):
        own[3].wait()
        own[4].wait()
        settle_weights(0)
    with scope("T6self"):
        gathered(0)

    @pl.when(outer)
    def _():
        for kind in (1, 2, 3):
            for i in range(n):
                to_across(kind, i)

    heads = n * n
    joined = jnp.concatenate([r_self[s] for s in range(heads)], 1)
    totals[...] = jnp.dot(
        joined, ws_all[...].reshape(-1, ws.shape[1]), preferred_element_type=jnp.float32
    )

    with scope("T7forward"):
        @pl.when(inner)
        def _():
            for kind in (1, 2):
                for i in range(n):
                    forward(kind, i, ends)
            pass_weights(2)

    with scope("T7w"):
        settle_weights(1)

    def rows_of(ref, block, size):
        return ref.at[pl.ds(pl.multiple_of(block * size, size), size)]

    def deliver(c, b):
        source, out, size = ((sum_v, out_v, part_rows), (sum_a, out_a, part_few))[c]
        piece, target = rows_of(source, b, size), rows_of(out, h, size)
        away = (w != b) | (w != h)

        @pl.when(away)
        def _():
            remote(
                piece, target, e_send.at[c], e_recv.at[c], {"wide": b, "heads": w}
            ).start()

        @pl.when(jnp.logical_not(away))
        def _():
            pltpu.make_async_copy(piece, target, e_recv.at[c]).start()

    flat_c = wc_all[...].reshape(-1, wc.shape[1])
    for u in range(2):
        with scope("T8gather%d" % u):
            gathered(1 + u)
        begin = tail + u * (half // 2)
        piece = slice(begin, begin + half // 2)
        crossed = jnp.concatenate(
            [
                jnp.concatenate([r_rest[s, piece, :HDA] for s in range(heads)], 1),
                jnp.concatenate([r_rest[s, piece, HDA:] for s in range(heads)], 1),
            ],
            0,
        )
        products = jnp.dot(crossed, flat_c, preferred_element_type=jnp.float32)
        size = half // 2
        for k in range(2):
            b = (n // 2 - 1 - u, n // 2 + u)[k]
            where = slice(b * size, (b + 1) * size)
            sum_v[where, :] = (
                totals[where, :] + products[k * size : (k + 1) * size, :]
            ).astype(bf16)
        if u == 0:
            for b in (n // 2 - 1, n // 2):
                deliver(0, b)
    with scope("T7audio"):
        @pl.when(inner)
        def _():
            for ks in (ends, peers):
                for i in range(n):
                    forward(3, i, ks)

    @pl.when(inner)
    def _():
        deliver(0, mate)
        deliver(0, far_end)

    @pl.when(outer)
    def _():
        deliver(0, w)

    with scope("T8audio"):
        settle_weights(2)
        gathered(3)
    audio_joined = jnp.concatenate([r_rest[s, :tail, :] for s in range(heads)], 1)
    sum_a[...] = jnp.dot(
        audio_joined, wa_all[...].reshape(-1, aso.shape[1]), preferred_element_type=jnp.float32
    ).astype(bf16)
    for b in range(n):
        deliver(1, b)

    @pl.when(outer)
    def _():
        deliver(0, far_end)


    with scope("T9results"):
        settle(out_v, e_recv.at[0])
        settle(out_a, e_recv.at[1])

    with scope("TBsends"):
        for i, target in enumerate((q_all, k_all, v_all)):
            settle(target.at[: n - 1], a_send.at[i])
        for k, portion in enumerate(portions):
            settle(p_all.at[: n - 1, portion], a_send.at[3 + k])
        for i in range(3):
            settle(targets[i].at[:3], w_send.at[i])
        for kind in range(4):
            settle(many(kind, 3 * n - 1), z_send.at[kind])
        @pl.when(inner)
        def _():
            for kind in range(4):
                settle(many(kind, 2 * n), r_send.at[kind])

        for c, (ref, size) in enumerate(((sum_v, part_rows), (sum_a, part_few))):
            settle(ref.at[: (n - 1) * size], e_send.at[c])

            @pl.when(w != h)
            def _():
                settle(ref.at[:size], e_send.at[c])


def shards(*args):
    n = lax.axis_size("wide")
    count = lax.axis_size("heads")
    head_count = args[2].shape[1] // HDV
    paired = lax.axis_size("groups") == 2
    if not (paired and n == count == head_count == 2 * REACH and args[5].shape[0] % (16 * n) == 0):
        return general_shards(*args)
    (video_hidden, audio_hidden, vq, vk, vv, aq, ak, av, cvq, cak, cav, caq, cvk, cvv,
     vso, vco, aso, aco, table) = args
    rows, few = vq.shape[0], aq.shape[0]
    depth = rows + rows // 2 + 3 * few
    anywhere = pl.BlockSpec(memory_space=pl.ANY)
    bf16, f32 = jnp.bfloat16, jnp.float32
    rest = rows // 2 + few
    dma = pltpu.SemaphoreType.DMA
    video_sum, audio_sum = pl.pallas_call(
        functools.partial(joint_kernel, n),
        out_shape=(
            jax.ShapeDtypeStruct(video_hidden.shape, bf16),
            jax.ShapeDtypeStruct(audio_hidden.shape, bf16),
        ),
        in_specs=[pl.BlockSpec(memory_space=pltpu.HBM)] * 16 + [pl.BlockSpec(memory_space=pltpu.SMEM)],
        out_specs=(anywhere, anywhere),
        scratch_shapes=[
            pltpu.VMEM((n, rows, HDV), bf16),
            pltpu.VMEM((n, rows, HDV), bf16),
            pltpu.VMEM((n, rows, HDV), bf16),
            pltpu.VMEM((3,) + vq.shape, bf16),
            pltpu.VMEM((3,) + cvq.shape, bf16),
            pltpu.VMEM((6,) + aq.shape, bf16),
            pltpu.VMEM((n, depth, 2 * HDA), bf16),
            pltpu.VMEM((n, depth, 2 * HDA), bf16),
            pltpu.VMEM((n,) + vso.shape, bf16),
            pltpu.VMEM((n,) + vco.shape, bf16),
            pltpu.VMEM((n, 2 * aso.shape[0], aso.shape[1]), bf16),
            pltpu.VMEM((rows, n * few), f32),
            pltpu.VMEM((n * few, n * rows), f32),
            pltpu.VMEM((n, rows, HDV), bf16),
            pltpu.VMEM((n, rest, 2 * HDA), bf16),
            pltpu.VMEM((n * n, rows, HDV), bf16),
            pltpu.VMEM((n * n, rest, 2 * HDA), bf16),
            pltpu.VMEM(video_hidden.shape, f32),
            pltpu.VMEM(video_hidden.shape, bf16),
            pltpu.VMEM(audio_hidden.shape, bf16),
            dma((5,)), dma((5,)),
            dma((3,)), dma((3, 4)),
            dma((4,)),
            dma((4,)), dma((4, n, 2)), dma((4,)), dma((4,)),
            dma((2,)), dma((2,)),
            dma((8,)),
        ],
        compiler_params=pltpu.CompilerParams(
            collective_id=0, has_side_effects=True, vmem_limit_bytes=48 * 1024 * 1024
        ),
        name="joint",
    )(
        *(
            pltpu.with_memory_space_constraint(operand, pltpu.HBM)
            for operand in (
                vq, vk, vv, cvq, cvk, cvv, aq, ak, av, caq, cak, cav, vso, vco, aso, aco, table
            )
        )
    )
    video_out = video_hidden.astype(f32) + video_sum.astype(f32)
    audio_out = audio_hidden.astype(f32) + audio_sum.astype(f32)
    return (video_out.astype(bf16), audio_out.astype(bf16))


def solution(mesh):
    placed = (
        P(("groups", "wide"), "heads"),
        P(("groups", "wide"), "heads"),
        P(("groups", "wide"), "heads"),
        P(("groups", "wide"), "heads"),
        P(("groups", "wide"), "heads"),
        P(("groups", "wide"), "heads"),
        P(("groups", "wide"), "heads"),
        P(("groups", "wide"), "heads"),
        P(("groups", "wide"), "heads"),
        P(("groups", "wide"), "heads"),
        P(("groups", "wide"), "heads"),
        P(("groups", "wide"), "heads"),
        P(("groups", "wide"), "heads"),
        P(("groups", "wide"), "heads"),
        P("heads", "wide"),
        P("heads", "wide"),
        P("heads", "wide"),
        P("heads", "wide"),
        P("groups", None),
    )
    return jax.shard_map(
        shards,
        mesh=mesh,
        in_specs=placed,
        out_specs=(P(("groups", "wide"), "heads"), P(("groups", "wide"), "heads")),
        check_vma=False,
    )
```

```python
import contextlib
import functools
import math

import jax
import jax.numpy as jnp
from jax import lax
from jax.experimental import pallas as pl
from jax.experimental.pallas import tpu as pltpu
from jax.sharding import PartitionSpec as P

HDV = 128
HDA = 64
REACH = 2


def passed_along(value, axis, by):
    length = lax.axis_size(axis)
    pairs = [(i, i + by) for i in range(length) if 0 <= i + by < length]
    return lax.ppermute(value, axis, pairs)


def empty_state(row_count, head_count, head_size):
    return (
        jnp.full((head_count, row_count), -1e30, jnp.float32),
        jnp.zeros((head_count, row_count), jnp.float32),
        jnp.zeros((head_count, row_count, head_size), jnp.float32),
    )


def absorb(state, queries, key_rows, value_rows, head_size, allowed):
    maxima, totals, running = state
    head_count = queries.shape[1] // head_size
    query_heads = queries.reshape(queries.shape[0], head_count, head_size)
    key_heads = key_rows.reshape(key_rows.shape[0], head_count, head_size)
    value_heads = value_rows.reshape(value_rows.shape[0], head_count, head_size)
    scores = jnp.einsum(
        "qhd,khd->hqk", query_heads, key_heads, preferred_element_type=jnp.float32
    ) * (1.0 / math.sqrt(head_size))
    if allowed is not None:
        scores = jnp.where(allowed[None, None, :], scores, -1e30)
    new_peak = jnp.maximum(maxima, jnp.max(scores, axis=2))
    weights = jnp.exp(scores - new_peak[:, :, None])
    if allowed is not None:
        weights = jnp.where(allowed[None, None, :], weights, 0.0)
    rescale = jnp.exp(maxima - new_peak)
    totals = totals * rescale + jnp.sum(weights, axis=2)
    running = running * rescale[:, :, None] + jnp.einsum(
        "hqk,khd->hqd",
        weights.astype(jnp.bfloat16),
        value_heads,
        preferred_element_type=jnp.float32,
    )
    return (new_peak, totals, running)


def finish(state, head_size):
    maxima, totals, running = state
    result = running / totals[:, :, None]
    return (
        result.transpose(1, 0, 2)
        .reshape(result.shape[1], result.shape[0] * head_size)
        .astype(jnp.bfloat16)
    )


def permitted(key_blocks, position, table_row, wide_count):
    offsets = key_blocks - position + REACH
    matches = (offsets[:, None] == jnp.arange(2 * REACH + 1, dtype=jnp.int32)[None, :]) & (
        table_row[None, :] > 0
    )
    inside = (key_blocks >= 0) & (key_blocks < wide_count)
    return jnp.any(matches, axis=1) & inside


def general_shards(
    video_hidden,
    audio_hidden,
    video_query,
    video_key,
    video_value,
    audio_query,
    audio_key,
    audio_value,
    cross_video_query,
    cross_audio_key,
    cross_audio_value,
    cross_audio_query,
    cross_video_key,
    cross_video_value,
    video_self_out,
    video_cross_out,
    audio_self_out,
    audio_cross_out,
    intersection,
):
    position = lax.axis_index("wide")
    wide_count = lax.axis_size("wide")
    video_count = video_query.shape[0]
    audio_count = audio_query.shape[0]
    head_count = video_query.shape[1] // HDV
    video_start = empty_state(video_count, head_count, HDV)
    audio_start = empty_state(audio_count, head_count, HDA)
    carried = (video_start, audio_start)
    portion = (
        lax.all_gather(video_key, "wide", axis=0, tiled=True),
        lax.all_gather(video_value, "wide", axis=0, tiled=True),
        lax.all_gather(audio_key, "wide", axis=0, tiled=True),
        lax.all_gather(audio_value, "wide", axis=0, tiled=True),
    )
    video_state = absorb(carried[0], video_query, portion[0], portion[1], HDV, None)
    audio_state = absorb(carried[1], audio_query, portion[2], portion[3], HDA, None)
    table_row = lax.dynamic_slice_in_dim(intersection, position, 1, 0)[0]
    padded_table = jnp.pad(intersection, ((REACH, REACH), (0, 0)))
    flag_row = jnp.diagonal(
        jnp.fliplr(lax.dynamic_slice_in_dim(padded_table, position, 2 * REACH + 1, 0))
    )
    stacked = jnp.concatenate(
        [cross_audio_key, cross_audio_value, cross_video_key, cross_video_value], 0
    )

    def take_cross(carried, portion, block):
        audio_keys = portion[:audio_count]
        audio_values = portion[audio_count : 2 * audio_count]
        video_keys = portion[2 * audio_count : 2 * audio_count + video_count]
        video_values = portion[2 * audio_count + video_count :]
        audio_blocks = jnp.full((audio_count,), block, jnp.int32)
        video_blocks = jnp.full((video_count,), block, jnp.int32)
        return (
            absorb(
                carried[0],
                cross_video_query,
                audio_keys,
                audio_values,
                HDA,
                permitted(audio_blocks, position, table_row, wide_count),
            ),
            absorb(
                carried[1],
                cross_audio_query,
                video_keys,
                video_values,
                HDA,
                permitted(video_blocks, position, flag_row, wide_count),
            ),
        )

    cross_start = (
        empty_state(video_count, head_count, HDA),
        empty_state(audio_count, head_count, HDA),
    )
    carried = take_cross(cross_start, stacked, position)
    for offset in range(-REACH, REACH + 1):
        if offset != 0:
            nearby = passed_along(stacked, "wide", -offset)
            carried = take_cross(carried, nearby, position + offset)
    to_video, to_audio = carried
    video_joined = jnp.concatenate([finish(video_state, HDV), finish(to_video, HDA)], 1)
    audio_joined = jnp.concatenate([finish(audio_state, HDA), finish(to_audio, HDA)], 1)
    video_weights = jnp.concatenate([video_self_out, video_cross_out], 0)
    audio_weights = jnp.concatenate([audio_self_out, audio_cross_out], 0)
    video_terms = jnp.dot(
        video_joined,
        lax.all_gather(video_weights, "wide", axis=1, tiled=True),
        preferred_element_type=jnp.float32,
    )
    audio_terms = jnp.dot(
        audio_joined,
        lax.all_gather(audio_weights, "wide", axis=1, tiled=True),
        preferred_element_type=jnp.float32,
    )
    video_sum, audio_sum = (
        lax.psum_scatter(
            video_terms.astype(jnp.bfloat16), "heads", scatter_dimension=1, tiled=True
        ).astype(jnp.float32),
        lax.psum_scatter(
            audio_terms.astype(jnp.bfloat16), "heads", scatter_dimension=1, tiled=True
        ).astype(jnp.float32),
    )
    video_out = (video_hidden.astype(jnp.float32) + video_sum).astype(jnp.bfloat16)
    audio_out = (audio_hidden.astype(jnp.float32) + audio_sum).astype(jnp.bfloat16)
    return (video_out, audio_out)


NT = (((1,), (1,)), ((), ()))
MESH = pl.DeviceIdType.MESH


def scope(name):
    return contextlib.nullcontext()


def softmax(scores, head_size):
    factor = math.log2(math.e) / math.sqrt(head_size)
    weights = jnp.exp2((scores - jnp.max(scores, axis=1, keepdims=True)) * factor)
    return weights.astype(jnp.bfloat16), jnp.sum(weights, axis=1, keepdims=True)


def scored(queries, keys):
    return lax.dot_general(queries, keys, NT, preferred_element_type=jnp.float32)


def mixed(weights, values):
    return jnp.dot(weights, values, preferred_element_type=jnp.float32)


def joint_kernel(
    n,
    vq, vk, vv, cvq, cvk, cvv, aq, ak, av, caq, cak, cav, ws, wc, aso, aco, table_in,
    out_v, out_a,
    q_all, k_all, v_all, self_stage, wide_stage, few_stage, pack, p_all, ws_all, wc_all, wa_all,
    tall_bias, wide_bias, o_self, o_rest, r_self, r_rest, totals, sum_v, sum_a,
    a_send, a_recv, w_send, w_recv, x_recv, z_send, z_recv, m_recv, r_send,
    e_send, e_recv, table, local,
):
    g = lax.axis_index("groups")
    w = lax.axis_index("wide")
    h = lax.axis_index("heads")
    rows, few = vq.shape[0], aq.shape[0]
    half = rows // 2
    part_rows, part_few = rows // n, few // n
    depth = p_all.shape[1]
    bf16 = jnp.bfloat16

    mine = h * n + w
    side = w // (n // 2)
    mate = w + 1 - 2 * lax.rem(w, 2)
    across_side = n // 2 - side
    far_start = (1 - side) * (n // 2)
    inner = (w > 0) & (w < n - 1)

    def place(dw, dh):
        return {"wide": lax.rem(w + dw, n), "heads": lax.rem(h + dh, n)}

    def remote(source, target, send, recv, device):
        return pltpu.make_async_remote_copy(
            src_ref=source, dst_ref=target, send_sem=send, recv_sem=recv,
            device_id=device, device_id_type=MESH,
        )

    others = [(d, 0) for d in range(1, n)] + [(0, d) for d in range(1, n)]
    barrier = pltpu.get_barrier_semaphore()
    for dw, dh in others:
        pl.semaphore_signal(barrier, inc=1, device_id=place(dw, dh), device_id_type=MESH)
    twin = {"groups": 1 - g}
    pl.semaphore_signal(barrier, inc=1, device_id=twin, device_id_type=MESH)

    def settle(piece, sem):
        pltpu.make_async_copy(piece, piece, sem).wait()

    def head_cols(ref, who):
        return ref.at[:, pl.ds(pl.multiple_of(who * HDV, HDV), HDV)]

    def start(copies):
        for copy in copies:
            copy.start()
        return copies

    streams = ((vq, q_all), (vk, k_all), (vv, v_all))
    table_copy = pltpu.make_async_copy(table_in, table, local.at[8])
    table_copy.start()
    self_staged = start(
        [
            pltpu.make_async_copy(source, self_stage.at[i], local.at[2])
            for i, (source, _) in enumerate(streams)
        ]
    )
    staged = start(
        [
            pltpu.make_async_copy(source, wide_stage.at[i], local.at[0])
            for i, source in enumerate((cvq, cvk, cvv))
        ]
        + [
            pltpu.make_async_copy(source, few_stage.at[i], local.at[1])
            for i, source in enumerate((cak, cav, caq, aq, av, ak))
        ]
    )
    own = start(
        [
            pltpu.make_async_copy(head_cols(source, w), target.at[w], local.at[3])
            for i, (source, target) in enumerate(streams)
        ]
        + [
            pltpu.make_async_copy(source, target.at[h], local.at[4 + i])
            for i, (source, target) in enumerate(((ws, ws_all), (wc, wc_all)))
        ]
    )
    for j in range(n):
        for k, source in enumerate((aso, aco)):
            at = (2 * j + k) * HDA
            pltpu.make_async_copy(
                source.at[j * HDA : (j + 1) * HDA], wa_all.at[h, at : at + HDA], local.at[6]
            ).start()
    own.append(pltpu.make_async_copy(wa_all.at[h], wa_all.at[h], local.at[6]))
    settle(self_stage, local.at[2])
    with scope("T0barrier"):
        pl.semaphore_wait(barrier, len(others) + 1)

    far_end = (1 - side) * (n - 1)

    def exchange(target):
        for i, (_, landing) in enumerate(streams):
            remote(
                head_cols(self_stage.at[i], target), landing.at[w], a_send.at[i], a_recv.at[i],
                {"wide": target, "heads": h},
            ).start()

    near = jnp.where(inner, across_side, mate)
    last = jnp.where(inner, mate, across_side)
    for target in (far_end, near, last):
        exchange(target)

    targets = (ws_all, wc_all, wa_all)
    sources = (ws, wc, wa_all.at[h])
    partner = {"wide": w, "heads": h + 1 - 2 * lax.rem(h, 2)}
    opposite = lax.rem(h + n // 2, n)

    def part_of(ref, which):
        size = ref.shape[0] // 2
        return ref.at[pl.ds(pl.multiple_of(which * size, size), size)]

    def send_weights(i):
        remote(
            part_of(sources[i], g), part_of(targets[i].at[h], g),
            w_send.at[i], w_recv.at[i, 0], {"wide": w, "heads": opposite},
        ).start()

    def share_weights(i):
        remote(sources[i], targets[i].at[h], w_send.at[i], w_recv.at[i, 1], partner).start()

    def swap_weights(i):
        piece = part_of(targets[i].at[opposite], g)
        settle(piece, w_recv.at[i, 0])
        remote(piece, piece, w_send.at[i], w_recv.at[i, 2], twin).start()

    def pass_weights(i):
        slot = targets[i].at[opposite]
        settle(part_of(slot, 1 - g), w_recv.at[i, 2])
        remote(slot, slot, w_send.at[i], w_recv.at[i, 3], partner).start()

    def settle_weights(i):
        settle(targets[i].at[h], w_recv.at[i, 1])
        settle(targets[i].at[h], w_recv.at[i, 3])

    for i in range(2):
        send_weights(i)
        share_weights(i)

    settle(wide_stage, local.at[0])
    settle(few_stage, local.at[1])
    later = half + few
    for j in range(n):
        cols = slice(j * HDA, (j + 1) * HDA)
        for begin, k in ((0, 0), (later, 1), (later + half, 2)):
            pack[j, begin : begin + half, :] = jnp.concatenate(
                [wide_stage[k, :half, cols], wide_stage[k, half:, cols]], 1
            )
        for begin, k in ((half, 0), (later + 2 * half, 2), (later + 2 * half + few, 4)):
            pack[j, begin : begin + few, :] = jnp.concatenate(
                [few_stage[k, :, cols], few_stage[k + 1, :, cols]], 1
            )

    portions = (slice(0, later), slice(later, depth))

    def exchange_rest(target, k):
        remote(
            pack.at[target, portions[k]], p_all.at[w, portions[k]], a_send.at[3 + k],
            a_recv.at[3 + k], {"wide": target, "heads": h},
        ).start()

    outer = jnp.logical_not(inner)
    exchange_rest(mate, 0)
    exchange_rest(mate, 1)

    @pl.when(outer)
    def _():
        exchange_rest(far_end, 0)
        exchange_rest(far_end, 1)
        exchange_rest(across_side, 0)

    own_pack = pltpu.make_async_copy(pack.at[w], p_all.at[w], local.at[7])
    own_pack.start()
    own.pop().wait()
    send_weights(2)
    share_weights(2)

    table_copy.wait()
    for i in range(n):
        for j in range(n):
            column = j - i + REACH
            drop = jnp.float32(-1e30)
            if 0 <= column < table.shape[1]:
                drop = jnp.where(table[i, column] > 0, jnp.float32(0.0), drop)
            tall_bias[i * part_rows : (i + 1) * part_rows, j * few : (j + 1) * few] = jnp.full(
                (part_rows, few), drop
            )
            for k in range(2):
                begin = (k * n + i) * half
                wide_bias[j * few : (j + 1) * few, begin : begin + half] = jnp.full(
                    (few, half), drop
                )

    splits = (half // 2, half // 2, n * part_few)
    starts = (n * part_few, n * part_few + half // 2, 0)

    def chunk(ref, kind):
        if kind == 0:
            return ref
        return ref.at[pl.ds(starts[kind - 1], splits[kind - 1])]

    def buffers(kind):
        return (o_self, r_self) if kind == 0 else (o_rest, r_rest)

    orders = ((1, 0, 2, 3), (2, 3, 1, 0))

    def moved(e):
        return lax.rem(h // 2 + e // 2, 2) * 2 + lax.rem(h + e, 2)

    def turn_of(i):
        return orders[0][i] + lax.rem(w, 2) * (orders[1][i] - orders[0][i])

    def outgoing(kind, i):
        source, landing = buffers(kind)
        d = turn_of(i)
        part = moved(d)
        return d, part, chunk(source.at[part], kind), chunk(landing.at[mine], kind)

    def to_plane(kind, i):
        _, part, piece, where = outgoing(kind, i)

        @pl.when(part != h)
        def _():
            remote(
                piece, where, z_send.at[kind], x_recv.at[kind], {"wide": w, "heads": part}
            ).start()

    def to_across(kind, i):
        d, part, piece, where = outgoing(kind, i)
        remote(
            piece, where, z_send.at[kind], z_recv.at[kind, d, lax.rem(w, 2)],
            {"wide": across_side, "heads": part},
        ).start()

    def to_mate(kind, i):
        _, part, piece, where = outgoing(kind, i)
        remote(
            piece, where, z_send.at[kind], m_recv.at[kind], {"wide": mate, "heads": part}
        ).start()

    def far_piece(kind, d, k):
        return chunk(buffers(kind)[1].at[moved(d) * n + far_start + k], kind)

    def forward(kind, i, ks):
        for k in ks:
            d = orders[0][i] + k * (orders[1][i] - orders[0][i])
            piece = far_piece(kind, d, k)
            settle(piece, z_recv.at[kind, d, k])
            remote(
                piece, piece, r_send.at[kind], z_recv.at[kind, d, k],
                {"wide": mate, "heads": h},
            ).start()

    def many(kind, count):
        landing = buffers(kind)[1]
        if kind == 0:
            return landing.at[:count]
        return landing.at[:count, pl.ds(starts[kind - 1], splits[kind - 1])]

    def gathered(kind):
        settle(many(kind, n - 1), x_recv.at[kind])
        settle(many(kind, n), m_recv.at[kind])

        @pl.when(outer)
        def _():
            for d in range(n):
                for k in range(2):
                    settle(far_piece(kind, d, k), z_recv.at[kind, d, k])

    with scope("T1self"):
        settle(q_all.at[: len(streams)], local.at[3])
        for i, target in enumerate((q_all, k_all, v_all)):
            settle(target.at[: n - 1], a_recv.at[i])

    @pl.when(inner)
    def _():
        exchange_rest(far_end, 0)
        exchange_rest(far_end, 1)
        exchange_rest(across_side, 0)

    keys = k_all[...].reshape(n * rows, HDV)
    values = v_all[...].reshape(n * rows, HDV)

    def self_scores(i):
        at = pl.multiple_of(moved(turn_of(i)) * part_rows, part_rows)
        return scored(q_all[:, pl.ds(at, part_rows), :].reshape(rows, HDV), keys)

    scores = self_scores(0)
    for i in range(n):
        following = self_scores(i + 1) if i + 1 < n else None
        weights, sums = softmax(scores, HDV)
        result = (mixed(weights, values) / sums).astype(bf16)
        scores = following
        o_self[pl.ds(moved(turn_of(i)), 1)] = result[None]
        to_plane(0, i)
        to_across(0, i)
        to_mate(0, i)
    r_self[pl.ds(mine, 1)] = o_self[pl.ds(h, 1)]
    ends, peers = [lax.rem(w, 2)], [lax.rem(w + 1, 2)]

    with scope("T2weights"):
        swap_weights(0)
        swap_weights(1)
    with scope("T2ends"):
        @pl.when(inner)
        def _():
            for i in range(n):
                forward(0, i, ends)

    with scope("T2video"):
        own_pack.wait()
        settle(p_all.at[: n - 1, portions[0]], a_recv.at[3])
    lane = lax.broadcasted_iota(jnp.int32, (n * few, 2 * HDA), 1)
    left = lane < HDA

    def swapped(block):
        return jnp.concatenate([block[:, HDA:], block[:, :HDA]], 1)

    def only(block, keep_left):
        zero = jnp.zeros_like(block)
        return jnp.where(left, block, zero) if keep_left else jnp.where(left, zero, block)

    keyed = p_all[:, half:later, :].reshape(n * few, 2 * HDA)
    key_left, key_right = only(keyed, True), only(swapped(keyed), False)
    twice = jnp.concatenate([keyed[:, HDA:], keyed[:, HDA:]], 1)

    def cross_scores(i):
        part = moved(turn_of(i))
        begin = pl.multiple_of(lax.rem(part, n // 2) * part_rows, part_rows)
        queries = p_all[:, pl.ds(begin, part_rows), :].reshape(rows, 2 * HDA)
        chosen = jnp.where(part < n // 2, key_left, key_right)
        return scored(queries, chosen) + tall_bias[...]

    low = lax.broadcasted_iota(jnp.int32, (half, 2 * HDA), 1) < HDA
    tail = n * part_few
    scores = cross_scores(0)
    for i in range(n):
        following = cross_scores(i + 1) if i + 1 < n else None
        weights, sums = softmax(scores, HDA)
        result = mixed(weights, twice) / sums
        scores = following
        block = moved(turn_of(i))
        upper = [result[j * part_rows : (j + 1) * part_rows] for j in reversed(range(n // 2))]
        packed = jnp.where(low, jnp.concatenate(upper, 0), result[half:]).astype(bf16)
        o_rest[pl.ds(block, 1), tail:, :] = packed[None]
        for kind in (1, 2):
            to_plane(kind, i)

        @pl.when(inner)
        def _():
            for kind in (1, 2):
                to_across(kind, i)
                to_mate(kind, i)

    r_rest[pl.ds(mine, 1), tail:, :] = o_rest[pl.ds(h, 1), tail:, :]

    @pl.when(outer)
    def _():
        for kind in (1, 2):
            for i in range(n):
                to_mate(kind, i)

    exchange_rest(across_side, 1)
    with scope("T2peers"):
        @pl.when(inner)
        def _():
            for i in range(n):
                forward(0, i, peers)
            for i in range(2):
                pass_weights(i)

    swap_weights(2)
    with scope("T3peers"):
        @pl.when(inner)
        def _():
            for kind in (1, 2):
                for i in range(n):
                    forward(kind, i, peers)

    with scope("T3rest"):
        settle(p_all.at[: n - 1, portions[1]], a_recv.at[4])
    begin = later
    both = p_all[:, begin : begin + half, :].reshape(n * half, 2 * HDA)
    vals = p_all[:, begin + half : begin + 2 * half, :].reshape(n * half, 2 * HDA)
    begin += 2 * half
    asked = p_all[:, begin : begin + few, :].reshape(n * few, 2 * HDA)
    third = p_all[:, begin + few : depth, :].reshape(n * few, 2 * HDA)
    scores_a = scored(asked, only(third, False))
    scores_c = jnp.concatenate(
        [scored(only(asked, True), both), scored(only(swapped(asked), False), both)], 1
    ) + wide_bias[...]
    weights, sums = softmax(scores_a, HDA)
    audio_own = mixed(weights, third) / sums
    weights, sums = softmax(scores_c, HDA)
    upper, lower = weights[:, : n * half], weights[:, n * half :]
    audio_other = (pltpu.roll(mixed(upper, vals), HDA, 1) + mixed(lower, vals)) / sums
    audio = jnp.where(left, audio_own, audio_other).astype(bf16)
    for t in range(n):
        o_rest[t, :tail, :] = jnp.concatenate(
            [audio[j * few + t * part_few : j * few + (t + 1) * part_few, :] for j in range(n)], 0
        )
    r_rest[pl.ds(mine, 1), :tail, :] = o_rest[pl.ds(h, 1), :tail, :]
    for i in range(n):
        to_plane(3, i)
        to_mate(3, i)

    @pl.when(inner)
    def _():
        for i in range(n):
            to_across(3, i)

    with scope("T4pass"):
        @pl.when(outer)
        def _():
            for i in range(3):
                pass_weights(i)

    with scope("T5w"):
        own[3].wait()
        own[4].wait()
        settle_weights(0)
    with scope("T6self"):
        gathered(0)

    @pl.when(outer)
    def _():
        for kind in (1, 2, 3):
            for i in range(n):
                to_across(kind, i)

    heads = n * n
    joined = jnp.concatenate([r_self[s] for s in range(heads)], 1)
    totals[...] = jnp.dot(
        joined, ws_all[...].reshape(-1, ws.shape[1]), preferred_element_type=jnp.float32
    )

    with scope("T7forward"):
        @pl.when(inner)
        def _():
            for kind in (1, 2):
                for i in range(n):
                    forward(kind, i, ends)
            pass_weights(2)

    with scope("T7w"):
        settle_weights(1)

    def rows_of(ref, block, size):
        return ref.at[pl.ds(pl.multiple_of(block * size, size), size)]

    def deliver(c, b):
        source, out, size = ((sum_v, out_v, part_rows), (sum_a, out_a, part_few))[c]
        piece, target = rows_of(source, b, size), rows_of(out, h, size)
        away = (w != b) | (w != h)

        @pl.when(away)
        def _():
            remote(
                piece, target, e_send.at[c], e_recv.at[c], {"wide": b, "heads": w}
            ).start()

        @pl.when(jnp.logical_not(away))
        def _():
            pltpu.make_async_copy(piece, target, e_recv.at[c]).start()

    flat_c = wc_all[...].reshape(-1, wc.shape[1])
    for u in range(2):
        with scope("T8gather%d" % u):
            gathered(1 + u)
        begin = tail + u * (half // 2)
        piece = slice(begin, begin + half // 2)
        crossed = jnp.concatenate(
            [
                jnp.concatenate([r_rest[s, piece, :HDA] for s in range(heads)], 1),
                jnp.concatenate([r_rest[s, piece, HDA:] for s in range(heads)], 1),
            ],
            0,
        )
        products = jnp.dot(crossed, flat_c, preferred_element_type=jnp.float32)
        size = half // 2
        for k in range(2):
            b = (n // 2 - 1 - u, n // 2 + u)[k]
            where = slice(b * size, (b + 1) * size)
            sum_v[where, :] = (
                totals[where, :] + products[k * size : (k + 1) * size, :]
            ).astype(bf16)
        if u == 0:
            for b in (n // 2 - 1, n // 2):
                deliver(0, b)
    with scope("T7audio"):
        @pl.when(inner)
        def _():
            for ks in (ends, peers):
                for i in range(n):
                    forward(3, i, ks)

    @pl.when(inner)
    def _():
        deliver(0, mate)
        deliver(0, far_end)

    @pl.when(outer)
    def _():
        deliver(0, w)

    with scope("T8audio"):
        settle_weights(2)
        gathered(3)
    audio_joined = jnp.concatenate([r_rest[s, :tail, :] for s in range(heads)], 1)
    sum_a[...] = jnp.dot(
        audio_joined, wa_all[...].reshape(-1, aso.shape[1]), preferred_element_type=jnp.float32
    ).astype(bf16)
    for b in range(n):
        deliver(1, b)

    @pl.when(outer)
    def _():
        deliver(0, far_end)


    with scope("T9results"):
        settle(out_v, e_recv.at[0])
        settle(out_a, e_recv.at[1])

    with scope("TBsends"):
        for i, target in enumerate((q_all, k_all, v_all)):
            settle(target.at[: n - 1], a_send.at[i])
        for k, portion in enumerate(portions):
            settle(p_all.at[: n - 1, portion], a_send.at[3 + k])
        for i in range(3):
            settle(targets[i].at[:3], w_send.at[i])
        for kind in range(4):
            settle(many(kind, 3 * n - 1), z_send.at[kind])
        @pl.when(inner)
        def _():
            for kind in range(4):
                settle(many(kind, 2 * n), r_send.at[kind])

        for c, (ref, size) in enumerate(((sum_v, part_rows), (sum_a, part_few))):
            settle(ref.at[: (n - 1) * size], e_send.at[c])

            @pl.when(w != h)
            def _():
                settle(ref.at[:size], e_send.at[c])


def shards(*args):
    n = lax.axis_size("wide")
    count = lax.axis_size("heads")
    head_count = args[2].shape[1] // HDV
    paired = lax.axis_size("groups") == 2
    if not (paired and n == count == head_count == 2 * REACH and args[5].shape[0] % (16 * n) == 0):
        return general_shards(*args)
    (video_hidden, audio_hidden, vq, vk, vv, aq, ak, av, cvq, cak, cav, caq, cvk, cvv,
     vso, vco, aso, aco, table) = args
    rows, few = vq.shape[0], aq.shape[0]
    depth = rows + rows // 2 + 3 * few
    anywhere = pl.BlockSpec(memory_space=pl.ANY)
    bf16, f32 = jnp.bfloat16, jnp.float32
    rest = rows // 2 + few
    dma = pltpu.SemaphoreType.DMA
    video_sum, audio_sum = pl.pallas_call(
        functools.partial(joint_kernel, n),
        out_shape=(
            jax.ShapeDtypeStruct(video_hidden.shape, bf16),
            jax.ShapeDtypeStruct(audio_hidden.shape, bf16),
        ),
        in_specs=[pl.BlockSpec(memory_space=pltpu.HBM)] * 17,
        out_specs=(anywhere, anywhere),
        scratch_shapes=[
            pltpu.VMEM((n, rows, HDV), bf16),
            pltpu.VMEM((n, rows, HDV), bf16),
            pltpu.VMEM((n, rows, HDV), bf16),
            pltpu.VMEM((3,) + vq.shape, bf16),
            pltpu.VMEM((3,) + cvq.shape, bf16),
            pltpu.VMEM((6,) + aq.shape, bf16),
            pltpu.VMEM((n, depth, 2 * HDA), bf16),
            pltpu.VMEM((n, depth, 2 * HDA), bf16),
            pltpu.VMEM((n,) + vso.shape, bf16),
            pltpu.VMEM((n,) + vco.shape, bf16),
            pltpu.VMEM((n, 2 * aso.shape[0], aso.shape[1]), bf16),
            pltpu.VMEM((rows, n * few), f32),
            pltpu.VMEM((n * few, n * rows), f32),
            pltpu.VMEM((n, rows, HDV), bf16),
            pltpu.VMEM((n, rest, 2 * HDA), bf16),
            pltpu.VMEM((n * n, rows, HDV), bf16),
            pltpu.VMEM((n * n, rest, 2 * HDA), bf16),
            pltpu.VMEM(video_hidden.shape, f32),
            pltpu.VMEM(video_hidden.shape, bf16),
            pltpu.VMEM(audio_hidden.shape, bf16),
            dma((5,)), dma((5,)),
            dma((3,)), dma((3, 4)),
            dma((4,)),
            dma((4,)), dma((4, n, 2)), dma((4,)), dma((4,)),
            dma((2,)), dma((2,)),
            pltpu.SMEM(table.shape, jnp.int32),
            dma((9,)),
        ],
        compiler_params=pltpu.CompilerParams(
            collective_id=0, has_side_effects=True, vmem_limit_bytes=48 * 1024 * 1024
        ),
        name="joint",
    )(
        *(
            pltpu.with_memory_space_constraint(operand, pltpu.HBM)
            for operand in (
                vq, vk, vv, cvq, cvk, cvv, aq, ak, av, caq, cak, cav, vso, vco, aso, aco, table
            )
        )
    )
    video_out = video_hidden.astype(f32) + video_sum.astype(f32)
    audio_out = audio_hidden.astype(f32) + audio_sum.astype(f32)
    return (video_out.astype(bf16), audio_out.astype(bf16))


def solution(mesh):
    placed = (
        P(("groups", "wide"), "heads"),
        P(("groups", "wide"), "heads"),
        P(("groups", "wide"), "heads"),
        P(("groups", "wide"), "heads"),
        P(("groups", "wide"), "heads"),
        P(("groups", "wide"), "heads"),
        P(("groups", "wide"), "heads"),
        P(("groups", "wide"), "heads"),
        P(("groups", "wide"), "heads"),
        P(("groups", "wide"), "heads"),
        P(("groups", "wide"), "heads"),
        P(("groups", "wide"), "heads"),
        P(("groups", "wide"), "heads"),
        P(("groups", "wide"), "heads"),
        P("heads", "wide"),
        P("heads", "wide"),
        P("heads", "wide"),
        P("heads", "wide"),
        P("groups", None),
    )
    return jax.shard_map(
        shards,
        mesh=mesh,
        in_specs=placed,
        out_specs=(P(("groups", "wide"), "heads"), P(("groups", "wide"), "heads")),
        check_vma=False,
    )
```

```python
import contextlib
import functools
import math

import jax
import jax.numpy as jnp
from jax import lax
from jax.experimental import pallas as pl
from jax.experimental.pallas import tpu as pltpu
from jax.sharding import PartitionSpec as P

HDV = 128
HDA = 64
REACH = 2


def passed_along(value, axis, by):
    length = lax.axis_size(axis)
    pairs = [(i, i + by) for i in range(length) if 0 <= i + by < length]
    return lax.ppermute(value, axis, pairs)


def empty_state(row_count, head_count, head_size):
    return (
        jnp.full((head_count, row_count), -1e30, jnp.float32),
        jnp.zeros((head_count, row_count), jnp.float32),
        jnp.zeros((head_count, row_count, head_size), jnp.float32),
    )


def absorb(state, queries, key_rows, value_rows, head_size, allowed):
    maxima, totals, running = state
    head_count = queries.shape[1] // head_size
    query_heads = queries.reshape(queries.shape[0], head_count, head_size)
    key_heads = key_rows.reshape(key_rows.shape[0], head_count, head_size)
    value_heads = value_rows.reshape(value_rows.shape[0], head_count, head_size)
    scores = jnp.einsum(
        "qhd,khd->hqk", query_heads, key_heads, preferred_element_type=jnp.float32
    ) * (1.0 / math.sqrt(head_size))
    if allowed is not None:
        scores = jnp.where(allowed[None, None, :], scores, -1e30)
    new_peak = jnp.maximum(maxima, jnp.max(scores, axis=2))
    weights = jnp.exp(scores - new_peak[:, :, None])
    if allowed is not None:
        weights = jnp.where(allowed[None, None, :], weights, 0.0)
    rescale = jnp.exp(maxima - new_peak)
    totals = totals * rescale + jnp.sum(weights, axis=2)
    running = running * rescale[:, :, None] + jnp.einsum(
        "hqk,khd->hqd",
        weights.astype(jnp.bfloat16),
        value_heads,
        preferred_element_type=jnp.float32,
    )
    return (new_peak, totals, running)


def finish(state, head_size):
    maxima, totals, running = state
    result = running / totals[:, :, None]
    return (
        result.transpose(1, 0, 2)
        .reshape(result.shape[1], result.shape[0] * head_size)
        .astype(jnp.bfloat16)
    )


def permitted(key_blocks, position, table_row, wide_count):
    offsets = key_blocks - position + REACH
    matches = (offsets[:, None] == jnp.arange(2 * REACH + 1, dtype=jnp.int32)[None, :]) & (
        table_row[None, :] > 0
    )
    inside = (key_blocks >= 0) & (key_blocks < wide_count)
    return jnp.any(matches, axis=1) & inside


def general_shards(
    video_hidden,
    audio_hidden,
    video_query,
    video_key,
    video_value,
    audio_query,
    audio_key,
    audio_value,
    cross_video_query,
    cross_audio_key,
    cross_audio_value,
    cross_audio_query,
    cross_video_key,
    cross_video_value,
    video_self_out,
    video_cross_out,
    audio_self_out,
    audio_cross_out,
    intersection,
):
    position = lax.axis_index("wide")
    wide_count = lax.axis_size("wide")
    video_count = video_query.shape[0]
    audio_count = audio_query.shape[0]
    head_count = video_query.shape[1] // HDV
    video_start = empty_state(video_count, head_count, HDV)
    audio_start = empty_state(audio_count, head_count, HDA)
    carried = (video_start, audio_start)
    portion = (
        lax.all_gather(video_key, "wide", axis=0, tiled=True),
        lax.all_gather(video_value, "wide", axis=0, tiled=True),
        lax.all_gather(audio_key, "wide", axis=0, tiled=True),
        lax.all_gather(audio_value, "wide", axis=0, tiled=True),
    )
    video_state = absorb(carried[0], video_query, portion[0], portion[1], HDV, None)
    audio_state = absorb(carried[1], audio_query, portion[2], portion[3], HDA, None)
    table_row = lax.dynamic_slice_in_dim(intersection, position, 1, 0)[0]
    padded_table = jnp.pad(intersection, ((REACH, REACH), (0, 0)))
    flag_row = jnp.diagonal(
        jnp.fliplr(lax.dynamic_slice_in_dim(padded_table, position, 2 * REACH + 1, 0))
    )
    stacked = jnp.concatenate(
        [cross_audio_key, cross_audio_value, cross_video_key, cross_video_value], 0
    )

    def take_cross(carried, portion, block):
        audio_keys = portion[:audio_count]
        audio_values = portion[audio_count : 2 * audio_count]
        video_keys = portion[2 * audio_count : 2 * audio_count + video_count]
        video_values = portion[2 * audio_count + video_count :]
        audio_blocks = jnp.full((audio_count,), block, jnp.int32)
        video_blocks = jnp.full((video_count,), block, jnp.int32)
        return (
            absorb(
                carried[0],
                cross_video_query,
                audio_keys,
                audio_values,
                HDA,
                permitted(audio_blocks, position, table_row, wide_count),
            ),
            absorb(
                carried[1],
                cross_audio_query,
                video_keys,
                video_values,
                HDA,
                permitted(video_blocks, position, flag_row, wide_count),
            ),
        )

    cross_start = (
        empty_state(video_count, head_count, HDA),
        empty_state(audio_count, head_count, HDA),
    )
    carried = take_cross(cross_start, stacked, position)
    for offset in range(-REACH, REACH + 1):
        if offset != 0:
            nearby = passed_along(stacked, "wide", -offset)
            carried = take_cross(carried, nearby, position + offset)
    to_video, to_audio = carried
    video_joined = jnp.concatenate([finish(video_state, HDV), finish(to_video, HDA)], 1)
    audio_joined = jnp.concatenate([finish(audio_state, HDA), finish(to_audio, HDA)], 1)
    video_weights = jnp.concatenate([video_self_out, video_cross_out], 0)
    audio_weights = jnp.concatenate([audio_self_out, audio_cross_out], 0)
    video_terms = jnp.dot(
        video_joined,
        lax.all_gather(video_weights, "wide", axis=1, tiled=True),
        preferred_element_type=jnp.float32,
    )
    audio_terms = jnp.dot(
        audio_joined,
        lax.all_gather(audio_weights, "wide", axis=1, tiled=True),
        preferred_element_type=jnp.float32,
    )
    video_sum, audio_sum = (
        lax.psum_scatter(
            video_terms.astype(jnp.bfloat16), "heads", scatter_dimension=1, tiled=True
        ).astype(jnp.float32),
        lax.psum_scatter(
            audio_terms.astype(jnp.bfloat16), "heads", scatter_dimension=1, tiled=True
        ).astype(jnp.float32),
    )
    video_out = (video_hidden.astype(jnp.float32) + video_sum).astype(jnp.bfloat16)
    audio_out = (audio_hidden.astype(jnp.float32) + audio_sum).astype(jnp.bfloat16)
    return (video_out, audio_out)


NT = (((1,), (1,)), ((), ()))
MESH = pl.DeviceIdType.MESH


def scope(name):
    return contextlib.nullcontext()


def softmax(scores, head_size):
    factor = math.log2(math.e) / math.sqrt(head_size)
    weights = jnp.exp2((scores - jnp.max(scores, axis=1, keepdims=True)) * factor)
    return weights.astype(jnp.bfloat16), jnp.sum(weights, axis=1, keepdims=True)


def scored(queries, keys):
    return lax.dot_general(queries, keys, NT, preferred_element_type=jnp.float32)


def mixed(weights, values):
    return jnp.dot(weights, values, preferred_element_type=jnp.float32)


def joint_kernel(
    n,
    vq, vk, vv, cvq, cvk, cvv, aq, ak, av, caq, cak, cav, ws, wc, aso, aco, table_in,
    out_v, out_a,
    q_all, k_all, v_all, self_stage, wide_stage, few_stage, pack, p_all, ws_all, wc_all, wa_all,
    tall_bias, wide_bias, o_self, o_rest, r_self, r_rest, totals, sum_v, sum_a,
    a_send, a_recv, w_send, w_recv, x_recv, z_send, z_recv, m_recv, r_send,
    e_send, e_recv, table, local,
):
    g = lax.axis_index("groups")
    w = lax.axis_index("wide")
    h = lax.axis_index("heads")
    rows, few = vq.shape[0], aq.shape[0]
    half = rows // 2
    part_rows, part_few = rows // n, few // n
    depth = p_all.shape[1]
    bf16 = jnp.bfloat16

    mine = h * n + w
    side = w // (n // 2)
    mate = w + 1 - 2 * lax.rem(w, 2)
    across_side = n // 2 - side
    far_start = (1 - side) * (n // 2)
    inner = (w > 0) & (w < n - 1)

    def place(dw, dh):
        return {"wide": lax.rem(w + dw, n), "heads": lax.rem(h + dh, n)}

    def remote(source, target, send, recv, device):
        return pltpu.make_async_remote_copy(
            src_ref=source, dst_ref=target, send_sem=send, recv_sem=recv,
            device_id=device, device_id_type=MESH,
        )

    others = [(d, 0) for d in range(1, n)] + [(0, d) for d in range(1, n)]
    barrier = pltpu.get_barrier_semaphore()
    for dw, dh in others:
        pl.semaphore_signal(barrier, inc=1, device_id=place(dw, dh), device_id_type=MESH)
    twin = {"groups": 1 - g}
    pl.semaphore_signal(barrier, inc=1, device_id=twin, device_id_type=MESH)

    def settle(piece, sem):
        pltpu.make_async_copy(piece, piece, sem).wait()

    def head_cols(ref, who):
        return ref.at[:, pl.ds(pl.multiple_of(who * HDV, HDV), HDV)]

    def start(copies):
        for copy in copies:
            copy.start()
        return copies

    streams = ((vq, q_all), (vk, k_all), (vv, v_all))
    table_copy = pltpu.make_async_copy(table_in, table, local.at[8])
    table_copy.start()
    self_staged = start(
        [
            pltpu.make_async_copy(source, self_stage.at[i], local.at[2])
            for i, (source, _) in enumerate(streams)
        ]
    )
    settle(self_stage, local.at[2])
    with scope("T0barrier"):
        pl.semaphore_wait(barrier, len(others) + 1)

    far_end = (1 - side) * (n - 1)

    def exchange(target):
        for i, (_, landing) in enumerate(streams):
            remote(
                head_cols(self_stage.at[i], target), landing.at[w], a_send.at[i], a_recv.at[i],
                {"wide": target, "heads": h},
            ).start()

    near = jnp.where(inner, across_side, mate)
    last = jnp.where(inner, mate, across_side)
    for target in (far_end, near, last):
        exchange(target)

    staged = start(
        [
            pltpu.make_async_copy(source, wide_stage.at[i], local.at[0])
            for i, source in enumerate((cvq, cvk, cvv))
        ]
        + [
            pltpu.make_async_copy(source, few_stage.at[i], local.at[1])
            for i, source in enumerate((cak, cav, caq, aq, av, ak))
        ]
    )
    own = start(
        [
            pltpu.make_async_copy(head_cols(source, w), target.at[w], local.at[3])
            for i, (source, target) in enumerate(streams)
        ]
        + [
            pltpu.make_async_copy(source, target.at[h], local.at[4 + i])
            for i, (source, target) in enumerate(((ws, ws_all), (wc, wc_all)))
        ]
    )
    for j in range(n):
        for k, source in enumerate((aso, aco)):
            at = (2 * j + k) * HDA
            pltpu.make_async_copy(
                source.at[j * HDA : (j + 1) * HDA], wa_all.at[h, at : at + HDA], local.at[6]
            ).start()
    own.append(pltpu.make_async_copy(wa_all.at[h], wa_all.at[h], local.at[6]))

    targets = (ws_all, wc_all, wa_all)
    sources = (ws, wc, wa_all.at[h])
    partner = {"wide": w, "heads": h + 1 - 2 * lax.rem(h, 2)}
    opposite = lax.rem(h + n // 2, n)

    def part_of(ref, which):
        size = ref.shape[0] // 2
        return ref.at[pl.ds(pl.multiple_of(which * size, size), size)]

    def send_weights(i):
        remote(
            part_of(sources[i], g), part_of(targets[i].at[h], g),
            w_send.at[i], w_recv.at[i, 0], {"wide": w, "heads": opposite},
        ).start()

    def share_weights(i):
        remote(sources[i], targets[i].at[h], w_send.at[i], w_recv.at[i, 1], partner).start()

    def swap_weights(i):
        piece = part_of(targets[i].at[opposite], g)
        settle(piece, w_recv.at[i, 0])
        remote(piece, piece, w_send.at[i], w_recv.at[i, 2], twin).start()

    def pass_weights(i):
        slot = targets[i].at[opposite]
        settle(part_of(slot, 1 - g), w_recv.at[i, 2])
        remote(slot, slot, w_send.at[i], w_recv.at[i, 3], partner).start()

    def settle_weights(i):
        settle(targets[i].at[h], w_recv.at[i, 1])
        settle(targets[i].at[h], w_recv.at[i, 3])

    for i in range(2):
        send_weights(i)
        share_weights(i)

    settle(wide_stage, local.at[0])
    settle(few_stage, local.at[1])
    later = half + few
    for j in range(n):
        cols = slice(j * HDA, (j + 1) * HDA)
        for begin, k in ((0, 0), (later, 1), (later + half, 2)):
            pack[j, begin : begin + half, :] = jnp.concatenate(
                [wide_stage[k, :half, cols], wide_stage[k, half:, cols]], 1
            )
        for begin, k in ((half, 0), (later + 2 * half, 2), (later + 2 * half + few, 4)):
            pack[j, begin : begin + few, :] = jnp.concatenate(
                [few_stage[k, :, cols], few_stage[k + 1, :, cols]], 1
            )

    portions = (slice(0, later), slice(later, depth))

    def exchange_rest(target, k):
        remote(
            pack.at[target, portions[k]], p_all.at[w, portions[k]], a_send.at[3 + k],
            a_recv.at[3 + k], {"wide": target, "heads": h},
        ).start()

    outer = jnp.logical_not(inner)
    exchange_rest(mate, 0)
    exchange_rest(mate, 1)

    @pl.when(outer)
    def _():
        exchange_rest(far_end, 0)
        exchange_rest(far_end, 1)
        exchange_rest(across_side, 0)

    own_pack = pltpu.make_async_copy(pack.at[w], p_all.at[w], local.at[7])
    own_pack.start()
    own.pop().wait()
    send_weights(2)
    share_weights(2)

    table_copy.wait()
    for i in range(n):
        for j in range(n):
            column = j - i + REACH
            drop = jnp.float32(-1e30)
            if 0 <= column < table.shape[1]:
                drop = jnp.where(table[i, column] > 0, jnp.float32(0.0), drop)
            tall_bias[i * part_rows : (i + 1) * part_rows, j * few : (j + 1) * few] = jnp.full(
                (part_rows, few), drop
            )
            for k in range(2):
                begin = (k * n + i) * half
                wide_bias[j * few : (j + 1) * few, begin : begin + half] = jnp.full(
                    (few, half), drop
                )

    splits = (half // 2, half // 2, n * part_few)
    starts = (n * part_few, n * part_few + half // 2, 0)

    def chunk(ref, kind):
        if kind == 0:
            return ref
        return ref.at[pl.ds(starts[kind - 1], splits[kind - 1])]

    def buffers(kind):
        return (o_self, r_self) if kind == 0 else (o_rest, r_rest)

    orders = ((1, 0, 2, 3), (2, 3, 1, 0))

    def moved(e):
        return lax.rem(h // 2 + e // 2, 2) * 2 + lax.rem(h + e, 2)

    def turn_of(i):
        return orders[0][i] + lax.rem(w, 2) * (orders[1][i] - orders[0][i])

    def outgoing(kind, i):
        source, landing = buffers(kind)
        d = turn_of(i)
        part = moved(d)
        return d, part, chunk(source.at[part], kind), chunk(landing.at[mine], kind)

    def to_plane(kind, i):
        _, part, piece, where = outgoing(kind, i)

        @pl.when(part != h)
        def _():
            remote(
                piece, where, z_send.at[kind], x_recv.at[kind], {"wide": w, "heads": part}
            ).start()

    def to_across(kind, i):
        d, part, piece, where = outgoing(kind, i)
        remote(
            piece, where, z_send.at[kind], z_recv.at[kind, d, lax.rem(w, 2)],
            {"wide": across_side, "heads": part},
        ).start()

    def to_mate(kind, i):
        _, part, piece, where = outgoing(kind, i)
        remote(
            piece, where, z_send.at[kind], m_recv.at[kind], {"wide": mate, "heads": part}
        ).start()

    def far_piece(kind, d, k):
        return chunk(buffers(kind)[1].at[moved(d) * n + far_start + k], kind)

    def forward(kind, i, ks):
        for k in ks:
            d = orders[0][i] + k * (orders[1][i] - orders[0][i])
            piece = far_piece(kind, d, k)
            settle(piece, z_recv.at[kind, d, k])
            remote(
                piece, piece, r_send.at[kind], z_recv.at[kind, d, k],
                {"wide": mate, "heads": h},
            ).start()

    def many(kind, count):
        landing = buffers(kind)[1]
        if kind == 0:
            return landing.at[:count]
        return landing.at[:count, pl.ds(starts[kind - 1], splits[kind - 1])]

    def gathered(kind):
        settle(many(kind, n - 1), x_recv.at[kind])
        settle(many(kind, n), m_recv.at[kind])

        @pl.when(outer)
        def _():
            for d in range(n):
                for k in range(2):
                    settle(far_piece(kind, d, k), z_recv.at[kind, d, k])

    with scope("T1self"):
        settle(q_all.at[: len(streams)], local.at[3])
        for i, target in enumerate((q_all, k_all, v_all)):
            settle(target.at[: n - 1], a_recv.at[i])

    @pl.when(inner)
    def _():
        exchange_rest(far_end, 0)
        exchange_rest(far_end, 1)
        exchange_rest(across_side, 0)

    keys = k_all[...].reshape(n * rows, HDV)
    values = v_all[...].reshape(n * rows, HDV)

    def self_scores(i):
        at = pl.multiple_of(moved(turn_of(i)) * part_rows, part_rows)
        return scored(q_all[:, pl.ds(at, part_rows), :].reshape(rows, HDV), keys)

    scores = self_scores(0)
    for i in range(n):
        following = self_scores(i + 1) if i + 1 < n else None
        weights, sums = softmax(scores, HDV)
        result = (mixed(weights, values) / sums).astype(bf16)
        scores = following
        o_self[pl.ds(moved(turn_of(i)), 1)] = result[None]
        to_plane(0, i)
        to_across(0, i)
        to_mate(0, i)
    r_self[pl.ds(mine, 1)] = o_self[pl.ds(h, 1)]
    ends, peers = [lax.rem(w, 2)], [lax.rem(w + 1, 2)]

    with scope("T2weights"):
        swap_weights(0)
        swap_weights(1)
    with scope("T2ends"):
        @pl.when(inner)
        def _():
            for i in range(n):
                forward(0, i, ends)

    with scope("T2video"):
        own_pack.wait()
        settle(p_all.at[: n - 1, portions[0]], a_recv.at[3])
    lane = lax.broadcasted_iota(jnp.int32, (n * few, 2 * HDA), 1)
    left = lane < HDA

    def swapped(block):
        return jnp.concatenate([block[:, HDA:], block[:, :HDA]], 1)

    def only(block, keep_left):
        zero = jnp.zeros_like(block)
        return jnp.where(left, block, zero) if keep_left else jnp.where(left, zero, block)

    keyed = p_all[:, half:later, :].reshape(n * few, 2 * HDA)
    key_left, key_right = only(keyed, True), only(swapped(keyed), False)
    twice = jnp.concatenate([keyed[:, HDA:], keyed[:, HDA:]], 1)

    def cross_scores(i):
        part = moved(turn_of(i))
        begin = pl.multiple_of(lax.rem(part, n // 2) * part_rows, part_rows)
        queries = p_all[:, pl.ds(begin, part_rows), :].reshape(rows, 2 * HDA)
        chosen = jnp.where(part < n // 2, key_left, key_right)
        return scored(queries, chosen) + tall_bias[...]

    low = lax.broadcasted_iota(jnp.int32, (half, 2 * HDA), 1) < HDA
    tail = n * part_few
    scores = cross_scores(0)
    for i in range(n):
        following = cross_scores(i + 1) if i + 1 < n else None
        weights, sums = softmax(scores, HDA)
        result = mixed(weights, twice) / sums
        scores = following
        block = moved(turn_of(i))
        upper = [result[j * part_rows : (j + 1) * part_rows] for j in reversed(range(n // 2))]
        packed = jnp.where(low, jnp.concatenate(upper, 0), result[half:]).astype(bf16)
        o_rest[pl.ds(block, 1), tail:, :] = packed[None]
        for kind in (1, 2):
            to_plane(kind, i)

        @pl.when(inner)
        def _():
            for kind in (1, 2):
                to_across(kind, i)
                to_mate(kind, i)

    r_rest[pl.ds(mine, 1), tail:, :] = o_rest[pl.ds(h, 1), tail:, :]

    @pl.when(outer)
    def _():
        for kind in (1, 2):
            for i in range(n):
                to_mate(kind, i)

    exchange_rest(across_side, 1)
    with scope("T2peers"):
        @pl.when(inner)
        def _():
            for i in range(n):
                forward(0, i, peers)
            for i in range(2):
                pass_weights(i)

    swap_weights(2)
    with scope("T3peers"):
        @pl.when(inner)
        def _():
            for kind in (1, 2):
                for i in range(n):
                    forward(kind, i, peers)

    with scope("T3rest"):
        settle(p_all.at[: n - 1, portions[1]], a_recv.at[4])
    begin = later
    both = p_all[:, begin : begin + half, :].reshape(n * half, 2 * HDA)
    vals = p_all[:, begin + half : begin + 2 * half, :].reshape(n * half, 2 * HDA)
    begin += 2 * half
    asked = p_all[:, begin : begin + few, :].reshape(n * few, 2 * HDA)
    third = p_all[:, begin + few : depth, :].reshape(n * few, 2 * HDA)
    scores_a = scored(asked, only(third, False))
    scores_c = jnp.concatenate(
        [scored(only(asked, True), both), scored(only(swapped(asked), False), both)], 1
    ) + wide_bias[...]
    weights, sums = softmax(scores_a, HDA)
    audio_own = mixed(weights, third) / sums
    weights, sums = softmax(scores_c, HDA)
    upper, lower = weights[:, : n * half], weights[:, n * half :]
    audio_other = (pltpu.roll(mixed(upper, vals), HDA, 1) + mixed(lower, vals)) / sums
    audio = jnp.where(left, audio_own, audio_other).astype(bf16)
    for t in range(n):
        o_rest[t, :tail, :] = jnp.concatenate(
            [audio[j * few + t * part_few : j * few + (t + 1) * part_few, :] for j in range(n)], 0
        )
    r_rest[pl.ds(mine, 1), :tail, :] = o_rest[pl.ds(h, 1), :tail, :]
    for i in range(n):
        to_plane(3, i)
        to_mate(3, i)

    @pl.when(inner)
    def _():
        for i in range(n):
            to_across(3, i)

    with scope("T4pass"):
        @pl.when(outer)
        def _():
            for i in range(3):
                pass_weights(i)

    with scope("T5w"):
        own[3].wait()
        own[4].wait()
        settle_weights(0)
    with scope("T6self"):
        gathered(0)

    @pl.when(outer)
    def _():
        for kind in (1, 2, 3):
            for i in range(n):
                to_across(kind, i)

    heads = n * n
    joined = jnp.concatenate([r_self[s] for s in range(heads)], 1)
    totals[...] = jnp.dot(
        joined, ws_all[...].reshape(-1, ws.shape[1]), preferred_element_type=jnp.float32
    )

    with scope("T7forward"):
        @pl.when(inner)
        def _():
            for kind in (1, 2):
                for i in range(n):
                    forward(kind, i, ends)
            pass_weights(2)

    with scope("T7w"):
        settle_weights(1)

    def rows_of(ref, block, size):
        return ref.at[pl.ds(pl.multiple_of(block * size, size), size)]

    def deliver(c, b):
        source, out, size = ((sum_v, out_v, part_rows), (sum_a, out_a, part_few))[c]
        piece, target = rows_of(source, b, size), rows_of(out, h, size)
        away = (w != b) | (w != h)

        @pl.when(away)
        def _():
            remote(
                piece, target, e_send.at[c], e_recv.at[c], {"wide": b, "heads": w}
            ).start()

        @pl.when(jnp.logical_not(away))
        def _():
            pltpu.make_async_copy(piece, target, e_recv.at[c]).start()

    flat_c = wc_all[...].reshape(-1, wc.shape[1])
    for u in range(2):
        with scope("T8gather%d" % u):
            gathered(1 + u)
        begin = tail + u * (half // 2)
        piece = slice(begin, begin + half // 2)
        crossed = jnp.concatenate(
            [
                jnp.concatenate([r_rest[s, piece, :HDA] for s in range(heads)], 1),
                jnp.concatenate([r_rest[s, piece, HDA:] for s in range(heads)], 1),
            ],
            0,
        )
        products = jnp.dot(crossed, flat_c, preferred_element_type=jnp.float32)
        size = half // 2
        for k in range(2):
            b = (n // 2 - 1 - u, n // 2 + u)[k]
            where = slice(b * size, (b + 1) * size)
            sum_v[where, :] = (
                totals[where, :] + products[k * size : (k + 1) * size, :]
            ).astype(bf16)
        if u == 0:
            for b in (n // 2 - 1, n // 2):
                deliver(0, b)
    with scope("T7audio"):
        @pl.when(inner)
        def _():
            for ks in (ends, peers):
                for i in range(n):
                    forward(3, i, ks)

    @pl.when(inner)
    def _():
        deliver(0, mate)
        deliver(0, far_end)

    @pl.when(outer)
    def _():
        deliver(0, w)

    with scope("T8audio"):
        settle_weights(2)
        gathered(3)
    audio_joined = jnp.concatenate([r_rest[s, :tail, :] for s in range(heads)], 1)
    sum_a[...] = jnp.dot(
        audio_joined, wa_all[...].reshape(-1, aso.shape[1]), preferred_element_type=jnp.float32
    ).astype(bf16)
    for b in range(n):
        deliver(1, b)

    @pl.when(outer)
    def _():
        deliver(0, far_end)


    with scope("T9results"):
        settle(out_v, e_recv.at[0])
        settle(out_a, e_recv.at[1])

    with scope("TBsends"):
        for i, target in enumerate((q_all, k_all, v_all)):
            settle(target.at[: n - 1], a_send.at[i])
        for k, portion in enumerate(portions):
            settle(p_all.at[: n - 1, portion], a_send.at[3 + k])
        for i in range(3):
            settle(targets[i].at[:3], w_send.at[i])
        for kind in range(4):
            settle(many(kind, 3 * n - 1), z_send.at[kind])
        @pl.when(inner)
        def _():
            for kind in range(4):
                settle(many(kind, 2 * n), r_send.at[kind])

        for c, (ref, size) in enumerate(((sum_v, part_rows), (sum_a, part_few))):
            settle(ref.at[: (n - 1) * size], e_send.at[c])

            @pl.when(w != h)
            def _():
                settle(ref.at[:size], e_send.at[c])


def shards(*args):
    n = lax.axis_size("wide")
    count = lax.axis_size("heads")
    head_count = args[2].shape[1] // HDV
    paired = lax.axis_size("groups") == 2
    if not (paired and n == count == head_count == 2 * REACH and args[5].shape[0] % (16 * n) == 0):
        return general_shards(*args)
    (video_hidden, audio_hidden, vq, vk, vv, aq, ak, av, cvq, cak, cav, caq, cvk, cvv,
     vso, vco, aso, aco, table) = args
    rows, few = vq.shape[0], aq.shape[0]
    depth = rows + rows // 2 + 3 * few
    anywhere = pl.BlockSpec(memory_space=pl.ANY)
    bf16, f32 = jnp.bfloat16, jnp.float32
    rest = rows // 2 + few
    dma = pltpu.SemaphoreType.DMA
    video_sum, audio_sum = pl.pallas_call(
        functools.partial(joint_kernel, n),
        out_shape=(
            jax.ShapeDtypeStruct(video_hidden.shape, bf16),
            jax.ShapeDtypeStruct(audio_hidden.shape, bf16),
        ),
        in_specs=[pl.BlockSpec(memory_space=pltpu.HBM)] * 17,
        out_specs=(anywhere, anywhere),
        scratch_shapes=[
            pltpu.VMEM((n, rows, HDV), bf16),
            pltpu.VMEM((n, rows, HDV), bf16),
            pltpu.VMEM((n, rows, HDV), bf16),
            pltpu.VMEM((3,) + vq.shape, bf16),
            pltpu.VMEM((3,) + cvq.shape, bf16),
            pltpu.VMEM((6,) + aq.shape, bf16),
            pltpu.VMEM((n, depth, 2 * HDA), bf16),
            pltpu.VMEM((n, depth, 2 * HDA), bf16),
            pltpu.VMEM((n,) + vso.shape, bf16),
            pltpu.VMEM((n,) + vco.shape, bf16),
            pltpu.VMEM((n, 2 * aso.shape[0], aso.shape[1]), bf16),
            pltpu.VMEM((rows, n * few), f32),
            pltpu.VMEM((n * few, n * rows), f32),
            pltpu.VMEM((n, rows, HDV), bf16),
            pltpu.VMEM((n, rest, 2 * HDA), bf16),
            pltpu.VMEM((n * n, rows, HDV), bf16),
            pltpu.VMEM((n * n, rest, 2 * HDA), bf16),
            pltpu.VMEM(video_hidden.shape, f32),
            pltpu.VMEM(video_hidden.shape, bf16),
            pltpu.VMEM(audio_hidden.shape, bf16),
            dma((5,)), dma((5,)),
            dma((3,)), dma((3, 4)),
            dma((4,)),
            dma((4,)), dma((4, n, 2)), dma((4,)), dma((4,)),
            dma((2,)), dma((2,)),
            pltpu.SMEM(table.shape, jnp.int32),
            dma((9,)),
        ],
        compiler_params=pltpu.CompilerParams(
            collective_id=0, has_side_effects=True, vmem_limit_bytes=48 * 1024 * 1024
        ),
        name="joint",
    )(
        *(
            pltpu.with_memory_space_constraint(operand, pltpu.HBM)
            for operand in (
                vq, vk, vv, cvq, cvk, cvv, aq, ak, av, caq, cak, cav, vso, vco, aso, aco, table
            )
        )
    )
    video_out = video_hidden.astype(f32) + video_sum.astype(f32)
    audio_out = audio_hidden.astype(f32) + audio_sum.astype(f32)
    return (video_out.astype(bf16), audio_out.astype(bf16))


def solution(mesh):
    placed = (
        P(("groups", "wide"), "heads"),
        P(("groups", "wide"), "heads"),
        P(("groups", "wide"), "heads"),
        P(("groups", "wide"), "heads"),
        P(("groups", "wide"), "heads"),
        P(("groups", "wide"), "heads"),
        P(("groups", "wide"), "heads"),
        P(("groups", "wide"), "heads"),
        P(("groups", "wide"), "heads"),
        P(("groups", "wide"), "heads"),
        P(("groups", "wide"), "heads"),
        P(("groups", "wide"), "heads"),
        P(("groups", "wide"), "heads"),
        P(("groups", "wide"), "heads"),
        P("heads", "wide"),
        P("heads", "wide"),
        P("heads", "wide"),
        P("heads", "wide"),
        P("groups", None),
    )
    return jax.shard_map(
        shards,
        mesh=mesh,
        in_specs=placed,
        out_specs=(P(("groups", "wide"), "heads"), P(("groups", "wide"), "heads")),
        check_vma=False,
    )
```
